32 devices in a mesh: dp: 16 (over z, y, x), stream: 2 (over core).
Axes of the slice: x: 2, y: 2, z: 4, core: 2. Of those that a mesh axis runs over, the one named last changes fastest.
Arguments:
- residual: bfloat16 [32768, 1024], P(('dp', 'stream')), may hold values from -6 to 6
- cotangent: bfloat16 [32768, 1024], P(('dp', 'stream')), may hold values from -6 to 6
- ln_gain: bfloat16 [1024], replicated, may hold values from 0.5 to 1.5
- ln_bias: bfloat16 [1024], replicated, may hold values from -1.25 to 1.25
- w_qkv: bfloat16 [1024, 3072], replicated, may hold values from -0.1875 to 0.1875
- b_qkv: bfloat16 [3072], replicated, may hold values from -1.25 to 1.25
- w_proj: bfloat16 [1024, 1024], replicated, may hold values from -0.375 to 0.375
- b_proj: bfloat16 [1024], replicated, may hold values from -1.25 to 1.25
- feature_scale: bfloat16 [1024], replicated, may hold values from 0.5 to 2
- w_up: bfloat16 [1024, 4096], replicated, may hold values from -0.1875 to 0.1875
- b_up: bfloat16 [4096], replicated, may hold values from -1.25 to 1.25
- w_down: bfloat16 [4096, 1024], replicated, may hold values from -0.09375 to 0.09375
- b_down: bfloat16 [1024], replicated, may hold values from -1.25 to 1.25
- qmc_points: float32 [64, 64], replicated, may hold values from -5 to 5
- slot_lengths: int32 [16], P('dp'), may hold values from 128 to 2048, as said below
Outputs:
- block_out: bfloat16 [32768, 1024], P(('dp', 'stream'))
- residual_grad: float32 [32768, 1024], P(('dp', 'stream'))
- gain_grad: float32 [1024], P(('dp', 'stream'))
- shift_grad: float32 [1024], P(('dp', 'stream'))
- qkvw_grad: float32 [1024, 3072], P(('dp', 'stream'))
- qkvb_grad: float32 [3072], P(('dp', 'stream'))
- projw_grad: float32 [1024, 1024], P(('dp', 'stream'))
- projb_grad: float32 [1024], P(('dp', 'stream'))
- scale_grad: float32 [1024], P(('dp', 'stream'))
- upw_grad: float32 [1024, 4096], P(('dp', 'stream'))
- upb_grad: float32 [4096], P(('dp', 'stream'))
- downw_grad: float32 [4096, 1024], P(('dp', 'stream'))
- downb_grad: float32 [1024], P(('dp', 'stream'))
The draws below stay inside these ranges and needn't reach their ends.
Inputs may be any that keep to these rules, and one draw needn't show every extreme that they name: Slot j holds one sequence at its first slot_lengths[j] positions; the rest of its 2048 positions is padding. The least and the largest length occur in every draw.
All inputs are finite; a program needn't handle non-finite values.
Results may differ from the reference program's by a relative error of at most 0.0093.
Values may be sent and summed in bfloat16 or wider, within the bound.
No kernel may reach another device: no remote copies, remote signals or barrier semaphores. Data moves between devices by JAX's collectives and lax.ppermute only.
A program may use at most 384 MiB of HBM per device.

```python
import math
import jax
import jax.numpy as jnp
from jax import lax

D = 1024
HEADS = 16
HEAD = 64
ROT = 16
FF = 4096
FEAT = 64
SPAN = 64
LEN = 2048
MIN_LEN = 128
SLOTS = 16
ROWS = 32768


def draw_slot_lengths(key, part):
    key_base = jax.random.fold_in(key, 11)
    key_pick = jax.random.fold_in(key, 12)
    room = LEN - MIN_LEN
    base = jax.random.randint(key_base, (SLOTS,), 0, room + 1)
    lengths = MIN_LEN + (base * base // room + base) // 2
    chosen = jax.random.randint(key_pick, (), 0, SLOTS)
    places = jnp.arange(SLOTS)
    lengths = jnp.where(places == chosen, LEN, lengths)
    lengths = jnp.where(places == (chosen + 1) % SLOTS, MIN_LEN, lengths)
    return lengths.astype(jnp.int32)


def steps_of(own_key, shape, split, low, largest):
    level = 1.0
    for dim, parts in split:
        steps = jax.random.uniform(jax.random.fold_in(jax.random.fold_in(own_key, 6), dim), (parts,), jnp.float32, low / len(split), largest / len(split))
        level = level * jnp.repeat(jnp.exp(steps), shape[dim] // parts).reshape((-1,) + (1,) * (len(shape) - 1 - dim))
    return level


def bell_draw(own_key, shape, scale, reach, shards=(), kind=jnp.bfloat16):
    entries = jax.random.normal(own_key, shape, jnp.float32) * scale
    if len(shards) > 0:
        entries = steps_of(own_key, shape, shards, -0.22, 0.18) * entries
    return jnp.clip(entries, min=-reach, max=reach).astype(kind)


def setup_inputs(seed: int = 0) -> dict:
    keys = jax.random.split(jax.random.key(seed), 16)
    return {
        "residual": bell_draw(keys[0], (ROWS, D), 1.0, 6.0, ((0, 32),)),
        "cotangent": bell_draw(keys[1], (ROWS, D), 1.0, 6.0, ((0, 32),)),
        "ln_gain": jnp.clip(1.0 + 0.1 * jax.random.normal(keys[2], (D,), jnp.float32), 0.5, 1.5).astype(jnp.bfloat16),
        "ln_bias": bell_draw(keys[3], (D,), 0.2, 1.25),
        "w_qkv": bell_draw(keys[4], (D, 3 * D), D ** -0.5, 0.1875),
        "b_qkv": bell_draw(keys[5], (3 * D,), 0.2, 1.25),
        "w_proj": bell_draw(keys[6], (D, D), (D // 4) ** -0.5, 0.375),
        "b_proj": bell_draw(keys[7], (D,), 0.2, 1.25),
        "feature_scale": jnp.clip(jnp.exp(jax.random.uniform(keys[8], (HEADS * FEAT,), jnp.float32, math.log(0.5), math.log(2.0))), 0.5, 2.0).astype(jnp.bfloat16),
        "w_up": bell_draw(keys[9], (D, FF), D ** -0.5, 0.1875),
        "b_up": bell_draw(keys[10], (FF,), 0.2, 1.25),
        "w_down": bell_draw(keys[11], (FF, D), FF ** -0.5, 0.09375),
        "b_down": bell_draw(keys[12], (D,), 0.2, 1.25),
        "qmc_points": bell_draw(keys[13], (HEAD, FEAT), 1.0, 5.0, (), jnp.float32),
        "slot_lengths": draw_slot_lengths(jax.random.fold_in(keys[15], 71), 0),
    }


@jax.custom_vjp
def low(v):
    return lax.optimization_barrier(v.astype(jnp.bfloat16)).astype(jnp.float32)

@jax.custom_vjp
def low_back(v):
    return v

def low_keep(v):
    return (low(v), None)

def low_pass(kept, grad):
    return (grad,)

def back_keep(v):
    return (v, None)

def back_low(kept, grad):
    return (low(grad),)
low.defvjp(low_keep, low_pass)
low_back.defvjp(back_keep, back_low)
PRECISE = lax.Precision.HIGHEST
EPSILON = 1e-05

def dct_table(extent):
    places = jnp.arange(extent, dtype=jnp.float32)
    cosines = jnp.cos(math.pi * (places[:, None] + 0.5) * places[None, :] / extent)
    factor = jnp.where(places == 0, math.sqrt(1.0 / extent), math.sqrt(2.0 / extent))
    return cosines * factor[None, :]

def rotate(tensor, positions):
    half_rot = ROT // 2
    rot_freqs = 10000.0 ** (-jnp.arange(half_rot, dtype=jnp.float32) / half_rot)
    angles = positions[:, None] * rot_freqs[None, :]
    cosine = jnp.cos(angles)[:, None, :]
    sine_part = jnp.sin(angles)[:, None, :]
    leading = tensor[..., :half_rot]
    trailing = tensor[..., half_rot:ROT]
    return jnp.concatenate([leading * cosine - trailing * sine_part, trailing * cosine + leading * sine_part, tensor[..., ROT:]], axis=-1)

def features(tensor, cosines, qmc_points, weights):
    turned = jnp.einsum('...n,nk->...k', tensor, cosines, precision=PRECISE)
    spread = jnp.einsum('...k,km->...m', turned, qmc_points, precision=PRECISE) * HEAD ** (-0.25)
    square = lax.optimization_barrier(jnp.sum(turned * turned, axis=-1, keepdims=True)) * (0.5 * HEAD ** (-0.5))
    return weights * jnp.exp(spread - square)

def core(query_feat, key_feat, values, carry_state, carry_total):
    length, head_count, feat_count = query_feat.shape
    value_width = values.shape[-1]
    block_count = length // SPAN
    query_feat = query_feat.reshape(block_count, SPAN, head_count, feat_count)
    key_feat = key_feat.reshape(block_count, SPAN, head_count, feat_count)
    values = values.reshape(block_count, SPAN, head_count, value_width)
    places = jnp.arange(SPAN)
    causal = (places[:, None] >= places[None, :]).astype(query_feat.dtype)
    scores = jnp.einsum('cthf,cshf->chts', query_feat, key_feat, precision=PRECISE) * causal
    inner_num = jnp.einsum('chts,cshe->cthe', scores, values, precision=PRECISE)
    inner_den = jnp.transpose(lax.optimization_barrier(jnp.sum(scores, axis=-1)), (0, 2, 1))
    block_kv = jnp.einsum('cshf,cshe->chfe', key_feat, values, precision=PRECISE)
    block_keys = lax.optimization_barrier(jnp.sum(key_feat, axis=1))
    running = jnp.cumsum(block_kv, axis=0)
    running_keys = jnp.cumsum(block_keys, axis=0)
    before = carry_state[None] + jnp.concatenate([jnp.zeros_like(block_kv[:1]), running[:-1]], axis=0)
    before_keys = carry_total[None] + jnp.concatenate([jnp.zeros_like(block_keys[:1]), running_keys[:-1]], axis=0)
    cross_num = jnp.einsum('cthf,chfe->cthe', query_feat, before, precision=PRECISE)
    cross_den = jnp.einsum('cthf,chf->cth', query_feat, before_keys, precision=PRECISE)
    result = (inner_num + cross_num) / (inner_den + cross_den)[..., None]
    return (result.reshape(length, head_count, value_width), carry_state + running[-1], carry_total + running_keys[-1])

def attention_piece(qkv_rows, scale, carry_state, carry_total, positions, qmc_points):
    seg_count, length, triple = qkv_rows.shape
    model_width = triple // 3
    head_count = model_width // HEAD
    cosines = dct_table(HEAD)
    weights = scale.reshape(head_count, FEAT)
    query = rotate(qkv_rows[..., :model_width].reshape(seg_count, length, head_count, HEAD), positions)
    key_part = rotate(qkv_rows[..., model_width:2 * model_width].reshape(seg_count, length, head_count, HEAD), positions)
    values = qkv_rows[..., 2 * model_width:].reshape(seg_count, length, head_count, HEAD)
    query_feat = features(query, cosines, qmc_points, weights)
    key_feat = features(key_part, cosines, qmc_points, weights)
    result, new_state, new_total = jax.vmap(core)(query_feat, key_feat, values, carry_state, carry_total)
    return (result.reshape(seg_count, length, model_width), new_state, new_total)

def block(hidden, gain, shift, w_qkv, b_qkv, w_proj, b_proj, scale, w_up, b_up, w_down, b_down, qmc_points):
    row_count, model_width = hidden.shape
    mean_val = lax.optimization_barrier(jnp.mean(hidden, axis=-1, keepdims=True))
    centred = hidden - mean_val
    spread = lax.optimization_barrier(jnp.mean(centred * centred, axis=-1, keepdims=True))
    normed = low(centred * lax.rsqrt(spread + EPSILON) * gain + shift)
    qkv = low_back(jnp.dot(normed, w_qkv, precision=PRECISE) + b_qkv)
    seg_count = row_count // LEN
    zero_state = jnp.zeros((seg_count, model_width // HEAD, FEAT, HEAD), jnp.float32)
    zero_total = jnp.zeros((seg_count, model_width // HEAD, FEAT), jnp.float32)
    positions = jnp.arange(LEN, dtype=jnp.float32)
    mixed, unused_state, unused_total = attention_piece(qkv.reshape(seg_count, LEN, 3 * model_width), scale, zero_state, zero_total, positions, qmc_points)
    attended = low(mixed.reshape(row_count, model_width))
    attn_branch = jnp.dot(attended, w_proj, precision=PRECISE) + b_proj
    up_rows = low_back(jnp.dot(normed, w_up, precision=PRECISE) + b_up)
    act_rows = low(jax.nn.gelu(up_rows, approximate=False))
    return hidden + attn_branch + jnp.dot(act_rows, w_down, precision=PRECISE) + b_down

def reference(residual, cotangent, ln_gain, ln_bias, w_qkv, b_qkv, w_proj, b_proj, feature_scale, w_up, b_up, w_down, b_down, qmc_points, slot_lengths):
    params = tuple((item.astype(jnp.float32) for item in (ln_gain, ln_bias, w_qkv, b_qkv, w_proj, b_proj, feature_scale, w_up, b_up, w_down, b_down)))
    points = qmc_points.astype(jnp.float32)
    groups = SLOTS // 2
    model_width = residual.shape[1]
    hidden = residual.astype(jnp.float32).reshape(groups, 2 * LEN, model_width)
    slot_pos = jnp.arange(LEN, dtype=jnp.int32)
    live_mask = (slot_pos[None, :] < slot_lengths[:, None]).astype(jnp.float32).reshape(groups, 2 * LEN, 1)
    target = cotangent.astype(jnp.float32).reshape(groups, 2 * LEN, model_width) * live_mask

    def forward_rows(row_block, param_set):
        return block(row_block, *param_set, points)

    def advance(totals, item):
        row_block, grad_block = item
        result, pullback = jax.vjp(forward_rows, row_block, params)
        row_grad, param_grads = pullback(grad_block)
        totals = jax.tree.map(lambda lhs_val, rhs_val: lhs_val + rhs_val, totals, param_grads)
        return (totals, (result, row_grad))
    start = tuple((jnp.zeros_like(item) for item in params))
    totals, (results, row_grads) = lax.scan(advance, start, (hidden, target))
    return (results.reshape(-1, model_width).astype(jnp.bfloat16), row_grads.reshape(-1, model_width), totals[0], totals[1], totals[2], totals[3], totals[4], totals[5], totals[6], totals[7], totals[8], totals[9], totals[10])
```

```python
from functools import partial
import math

import jax
import jax.numpy as jnp
import numpy as np
from jax import lax
from jax.experimental import pallas as pl
from jax.experimental.pallas import tpu as pltpu
from jax.sharding import PartitionSpec as P

HEAD = 64
ROT = 16
LEN = 2048
EPSILON = 1e-05

BF = jnp.bfloat16
F32 = jnp.float32
TILE = 256
CHUNK = 128
GROUP = 256
PACK = GROUP // HEAD
LANES = 128
ERFC = tuple(
    item * math.sqrt(0.5 * math.pi)
    for item in (0.254829592, -0.284496736, 1.421413741, -1.453152027, 1.061405429)
)
VMEM_CAP = 60 * 1024 * 1024

NN = (((1,), (0,)), ((), ()))
NT = (((1,), (1,)), ((), ()))
TN = (((0,), (0,)), ((), ()))


def mm(left, right, dims=NN):
    return lax.dot_general(left, right, dims, preferred_element_type=F32)


def split(value):
    high = value.astype(BF)
    return high, (value - high.astype(F32)).astype(BF)


def whole(shape):
    rank = len(shape)
    return pl.BlockSpec(shape, lambda *_: (0,) * rank, pipeline_mode=pl.Buffered(1))


def anywhere():
    return pl.BlockSpec(memory_space=pl.ANY)


def params():
    return pltpu.CompilerParams(vmem_limit_bytes=VMEM_CAP)


def vector_spec(width, at, side=None):
    return pl.BlockSpec(
        (1, width),
        lambda i, info: (0, at // width + (0 if side is None else info[0])),
        pipeline_mode=pl.Buffered(1),
    )


def cost(flops, moved, trans=0):
    return pl.CostEstimate(flops=int(flops), bytes_accessed=int(moved), transcendentals=int(trans))


def norm_stats(rows):
    mean = jnp.mean(rows, axis=-1, keepdims=True)
    centred = rows - mean
    rstd = lax.rsqrt(jnp.mean(centred * centred, axis=-1, keepdims=True) + EPSILON)
    return centred * rstd, rstd


def strip_copy(side, source, buf, sems, kind, j):
    there = pl.ds(pl.multiple_of((2 * j + side) * LANES, LANES), LANES)
    here = pl.ds(pl.multiple_of(j * LANES, LANES), LANES)
    if kind == 0:
        return pltpu.make_async_copy(source.at[:, there], buf.at[:, here], sems.at[kind, j])
    return pltpu.make_async_copy(source.at[there, :], buf.at[here, :], sems.at[kind, j])


def mlp_kernel(half, tiles, info, res, cot, gain, bias, b_up, w_up, w_down, *rest):
    normed, target, act, up_grad, upb, sums, up_buf, down_buf, sems = rest[-9:]
    step = pl.program_id(0)
    side = info[0]

    @pl.when(step == 0)
    def _():
        @pl.loop(0, up_buf.shape[1] // LANES)
        def _(j):
            strip_copy(side, w_up, up_buf, sems, 0, j).start()
            strip_copy(side, w_down, down_buf, sems, 1, j).start()

        if half == 0:
            upb[...] = jnp.zeros_like(upb)
            sums[...] = jnp.zeros_like(sums)
        else:
            upb[...] = rest[4][...]

    rows = res.shape[0]
    xhat, _ = norm_stats(res[...].astype(F32))
    low = (xhat * gain[...] + bias[...]).astype(BF)
    normed[...] = low
    part = side if half == 0 else 1 - side
    place = (part * tiles + step) * rows + lax.broadcasted_iota(jnp.int32, (rows, 1), 0)
    tgt = jnp.where(place < info[2], cot[...], jnp.zeros_like(cot))
    target[...] = tgt
    ones = jnp.ones((8, rows), BF)
    if half == 0:
        sums[...] += mm(ones, tgt)[0:1]
    width = 1024
    strips = width // LANES

    @pl.loop(0, up_buf.shape[1] // width)
    def _(j):
        cols = pl.ds(pl.multiple_of(j * width, width), width)

        @pl.when(step == 0)
        def _():
            for b in range(strips):
                strip_copy(side, w_up, up_buf, sems, 0, j * strips + b).wait()
                strip_copy(side, w_down, down_buf, sems, 1, j * strips + b).wait()

        shift = jnp.concatenate(
            [
                b_up[:, pl.ds(pl.multiple_of((2 * (j * strips + b) + side) * LANES, LANES), LANES)]
                for b in range(strips)
            ],
            axis=1,
        )
        up = mm(low, up_buf[:, cols]) + shift
        back = mm(tgt, down_buf[cols, :], NT)
        bell = jnp.exp2(up * up * (-0.5 * math.log2(math.e)) - 0.5 * math.log2(2.0 * math.pi))
        t = 1.0 / (1.0 + (0.3275911 * math.sqrt(0.5)) * jnp.abs(up))
        poly = ERFC[4]
        for item in ERFC[3::-1]:
            poly = item + t * poly
        tail = (t * bell) * poly
        phi = jnp.where(up >= 0, 1.0 - tail, tail)
        act[:, cols] = (up * phi).astype(BF)
        grad = (back * (phi + up * bell)).astype(BF)
        up_grad[:, cols] = grad
        upb[:, cols] += mm(ones, grad)[0:1]

    if half == 1:

        @pl.when(step == tiles - 1)
        def _():
            high, least = split(jnp.broadcast_to(upb[...], (8, upb.shape[1])))
            sums[...] = (mm(high, up_buf[...], NT) + mm(least, up_buf[...], NT))[0:1]


def mlp_rows(half, info, res, cot, vectors, w_up, w_down, earlier=()):
    rows, dim = res.shape
    ff = w_up.shape[1] // 2
    tiles = rows // TILE
    total = 2 * rows
    shift = half * tiles
    row_map = lambda i, info: (i, 0)
    out_map = lambda i, info: (i + shift, 0)
    outs = (
        jax.ShapeDtypeStruct((total, dim), BF),
        jax.ShapeDtypeStruct((total, dim), BF),
        jax.ShapeDtypeStruct((total, ff), BF),
        jax.ShapeDtypeStruct((total, ff), BF),
        jax.ShapeDtypeStruct((1, ff), F32),
        jax.ShapeDtypeStruct((1, dim), F32),
    )
    return pl.pallas_call(
        partial(mlp_kernel, half, tiles),
        out_shape=outs,
        grid_spec=pltpu.PrefetchScalarGridSpec(
            num_scalar_prefetch=1,
            grid=(tiles,),
            in_specs=[
                pl.BlockSpec((TILE, dim), row_map),
                pl.BlockSpec((TILE, dim), row_map),
                vector_spec(dim, 0),
                vector_spec(dim, dim),
                vector_spec(2 * ff, 8 * dim),
                anywhere(),
                anywhere(),
            ]
            + [anywhere()] * (len(earlier) - 1)
            + [whole((1, ff))] * min(len(earlier), 1),
            out_specs=[
                pl.BlockSpec((TILE, dim), out_map),
                pl.BlockSpec((TILE, dim), out_map),
                pl.BlockSpec((TILE, ff), out_map),
                pl.BlockSpec((TILE, ff), out_map),
                whole((1, ff)),
                whole((1, dim)),
            ],
            scratch_shapes=[
                pltpu.VMEM((dim, ff), BF),
                pltpu.VMEM((ff, dim), BF),
                pltpu.SemaphoreType.DMA((2, ff // LANES)),
            ],
        ),
        input_output_aliases={8 + j: j for j in range(len(earlier) - 1)},
        compiler_params=params(),
        cost_estimate=cost(4 * rows * dim * ff, 12 * rows * dim + 16 * rows * ff, 2 * rows * ff),
        name="mlp_rows",
    )(info, res, cot, vectors, vectors, vectors, w_up, w_down, *earlier)


def ship(table, which, buf, send, keep, sems, first, count):
    half = send.shape[0]
    for b in range(count):
        spot = table[which, first + b]

        @pl.when(spot >= half)
        def _():
            pltpu.make_async_copy(buf.at[first + b], send.at[spot - half], sems.at[first + b]).start()

        @pl.when(spot < half)
        def _():
            pltpu.make_async_copy(buf.at[first + b], keep.at[spot], sems.at[first + b]).start()


def shipped(buf, keep, sems):
    for b in range(buf.shape[0]):
        pltpu.make_async_copy(buf.at[b], keep.at[0], sems.at[b]).wait()


def mlp_grad_kernel(which, pieces, table, left, right, send, keep, buf, sems):
    value = mm(left[...], right[...], TN).astype(BF)
    size = buf.shape[1] // pieces
    width = buf.shape[2]
    count = value.shape[0] // size
    first = pl.program_id(0) * count
    for b in range(count):
        for p in range(pieces):
            buf[first + b, p * size : (p + 1) * size, :] = value[
                b * size : (b + 1) * size, p * width : (p + 1) * width
            ]
    ship(table, which, buf, send, keep, sems, first, count)

    @pl.when(pl.program_id(0) == pl.num_programs(0) - 1)
    def _():
        shipped(buf, keep, sems)


def mlp_weight_grad(which, pieces, ndp, table, left, right):
    total, deep = left.shape
    wide = right.shape[1]
    rows, width = deep // ndp * pieces, wide // pieces
    shape = jax.ShapeDtypeStruct((ndp // 2, rows, width), BF)
    step = 512 if pieces == 1 else 256
    return pl.pallas_call(
        partial(mlp_grad_kernel, which, pieces),
        out_shape=(shape, shape),
        grid_spec=pltpu.PrefetchScalarGridSpec(
            num_scalar_prefetch=1,
            grid=(deep // step,),
            in_specs=[pl.BlockSpec((total, step), lambda i, t: (0, i)), whole((total, wide))],
            out_specs=[anywhere(), anywhere()],
            scratch_shapes=[pltpu.VMEM((ndp, rows, width), BF), pltpu.SemaphoreType.DMA((ndp,))],
        ),
        compiler_params=params(),
        cost_estimate=cost(2 * total * deep * wide, 2 * total * (deep + wide) + 2 * deep * wide),
        name="mlp_weight_grad",
    )(table, left, right)


def attn_grad_kernel(
    table, normed, attended, target, dq, dk, dv, extra, send_a, keep_a, send_b, keep_b, buf_a, buf_b, sems_a, sems_b
):
    step = pl.program_id(0)
    ndp = buf_a.shape[0]
    size = buf_a.shape[1] // 2
    small = size // 2
    half = dq.shape[1]

    @pl.when(step == 0)
    def _():
        value = mm(attended[...], target[...], TN).astype(BF)
        for b in range(ndp):
            for p in range(2):
                at = size + p * small
                buf_b[b, at : at + small, :] = value[b * small : (b + 1) * small, p * half : (p + 1) * half]
            buf_b[b, 2 * size :, :] = extra[b]

    count = normed.shape[1] // size
    first = step * count
    for item, buf, at in ((dq, buf_a, 0), (dk, buf_a, size), (dv, buf_b, 0)):
        value = mm(normed[...], item[...], TN).astype(BF)
        for b in range(count):
            buf[first + b, at : at + size, :] = value[b * size : (b + 1) * size, :]
    ship(table, 0, buf_a, send_a, keep_a, sems_a, first, count)
    ship(table, 1, buf_b, send_b, keep_b, sems_b, first, count)

    @pl.when(step == pl.num_programs(0) - 1)
    def _():
        shipped(buf_a, keep_a, sems_a)
        shipped(buf_b, keep_b, sems_b)


def attn_weight_grads(ndp, table, normed, target, attended, dq, dk, dv, extra):
    total, dim = normed.shape
    half = dq.shape[1]
    rows = 2 * dim // ndp
    more = extra.shape[1]
    shapes = [jax.ShapeDtypeStruct((ndp // 2, rows + j * more, half), BF) for j in range(2)]
    step = 256
    return pl.pallas_call(
        attn_grad_kernel,
        out_shape=(shapes[0], shapes[0], shapes[1], shapes[1]),
        grid_spec=pltpu.PrefetchScalarGridSpec(
            num_scalar_prefetch=1,
            grid=(dim // step,),
            in_specs=[
                pl.BlockSpec((total, step), lambda i, t: (0, i)),
                whole((total, half)),
                whole((total, dim)),
            ]
            + [whole((total, half))] * 3
            + [whole(extra.shape)],
            out_specs=[anywhere()] * 4,
            scratch_shapes=[pltpu.VMEM((ndp, rows + j * more, half), BF) for j in range(2)]
            + [pltpu.SemaphoreType.DMA((ndp,))] * 2,
        ),
        compiler_params=params(),
        cost_estimate=cost(8 * total * dim * half, 2 * total * (2 * dim + 4 * half) + 8 * dim * half),
        name="attn_weight_grads",
    )(table, normed, attended, target, dq, dk, dv, extra)


def turn(value, cosine, sine_low, sine_high):
    pieces = []
    for j in range(value.shape[1] // LANES):
        item = value[:, j * LANES : (j + 1) * LANES]
        pieces.append(
            item * cosine
            + pltpu.roll(item, LANES - ROT // 2, 1) * sine_low
            + pltpu.roll(item, ROT // 2, 1) * sine_high
        )
    return jnp.concatenate(pieces, axis=1)


def patterns():
    row_head = lax.broadcasted_iota(jnp.int32, (PACK * CHUNK, GROUP), 0) // CHUNK
    lane_head = lax.broadcasted_iota(jnp.int32, (PACK * CHUNK, GROUP), 1) // HEAD
    block_row = lax.broadcasted_iota(jnp.int32, (GROUP, GROUP), 0) // HEAD
    block_col = lax.broadcasted_iota(jnp.int32, (GROUP, GROUP), 1) // HEAD
    return row_head == lane_head, block_row == block_col


def interleave(items, lag):
    waiting = [(j * lag, item) for j, item in enumerate(items)]
    at = 0
    while waiting:
        alive = []
        for begin, item in waiting:
            if at < begin or next(item, waiting) is not waiting:
                alive.append((begin, item))
        waiting = alive
        at += 1


def stack(mask, item):
    return jnp.where(mask, jnp.concatenate([item] * PACK, axis=0), jnp.zeros((), BF))


def sum_heads(item, ones):
    high, low = split(item)
    return mm(high, ones) + mm(low, ones)


def tables(base, inner, first, span):
    cosines, lows, highs = [], [], []
    for c in range(span):
        outer = base[first + c]
        co, so = outer[0:1, :], outer[1:2, :]
        ci, si = inner[0], inner[1]
        cosines.append(co * ci - so * si)
        sine = so * ci + co * si
        lows.append(sine * inner[2])
        highs.append(sine * inner[3])
    join = lambda items: jnp.concatenate(items, axis=0)
    return join(cosines), join(lows), join(highs)


def attn_front_kernel(
    info, normed, target, w_q, w_k, w_v, b_q, b_k, b_v, w_proj, scale, mix_high, mix_low, base, inner,
    attended, dq, fq_s, fk_s, v_s, tk_s, gn_s, gx_s, bias_q, scale_grad, state, total,
):
    step = pl.program_id(0)
    groups = w_q.shape[1] // GROUP
    span = TILE // CHUNK
    stack_mask, block_mask = patterns()
    ones = jnp.where(block_mask, 1.0, 0.0).astype(BF)
    causal = lax.broadcasted_iota(jnp.int32, (CHUNK, PACK * CHUNK), 0) >= (
        lax.broadcasted_iota(jnp.int32, (CHUNK, PACK * CHUNK), 1) % CHUNK
    )
    lower = jnp.where(
        lax.broadcasted_iota(jnp.int32, (CHUNK, CHUNK), 0) >= lax.broadcasted_iota(jnp.int32, (CHUNK, CHUNK), 1),
        1.0,
        0.0,
    ).astype(BF)

    @pl.when(step == 0)
    def _():
        for item in (state, total, bias_q, scale_grad):
            item[...] = jnp.zeros_like(item)

    x = normed[...]
    cosine, low, high = tables(base, inner, step * span, span)
    grad_all = mm(target[...], w_proj[...], NT)
    feats, turned, values, held, before = {}, {}, {}, {}, {}

    def feature(g, which):
        cols = slice(g * GROUP, (g + 1) * GROUP)
        w, b, out = ((w_q, b_q, fq_s), (w_k, b_k, fk_s))[which]
        t = mm(x, w[:, cols]) + b[:, cols]
        yield
        t = turn(t, cosine, low, high)
        turned[which, g] = t
        t_high, t_low = split(t)
        spread = mm(t_high, mix_high[...]) + mm(t_low, mix_high[...]) + mm(t_high, mix_low[...])
        yield
        square = sum_heads(t * t, ones)
        yield
        feats[which, g] = (scale[:, cols] * jnp.exp(spread - square * (0.5 * HEAD ** (-0.5)))).astype(BF)
        out[:, cols] = feats[which, g]
        if which == 1:
            tk_s[:, cols] = t.astype(BF)
            values[g] = (mm(x, w_v[:, cols]) + b_v[:, cols]).astype(BF)
            v_s[:, cols] = values[g]
        yield

    def unit(g, c):
        cols = slice(g * GROUP, (g + 1) * GROUP)
        rows = slice(c * CHUNK, (c + 1) * CHUNK)
        fq, fk, vc = feats[0, g][rows], feats[1, g][rows], values[g][rows]
        stack_k, stack_v = stack(stack_mask, fk), stack(stack_mask, vc)
        kept = state[g]
        held = kept.astype(BF)
        state[g] = kept + jnp.where(block_mask, mm(fk, vc, TN), 0.0)
        keys = mm(lower, fk) + total[g]
        total[g] = keys[CHUNK - 1 : CHUNK, :]
        yield
        weight = jnp.where(causal, mm(fq, stack_k, NT), 0.0).astype(BF)
        wide = fq.astype(F32)
        den = sum_heads(wide * keys, ones)
        yield
        num = mm(weight, stack_v) + mm(fq, held)
        inverse = 1.0 / den
        yield
        mixed = num * inverse
        attended[rows, cols] = mixed.astype(BF)
        gn = (grad_all[rows, cols] * inverse).astype(BF)
        gn_s[rows, cols] = gn
        edge = jnp.where(causal, mm(gn, stack_v, NT), 0.0).astype(BF)
        yield
        grad_den = -sum_heads(gn.astype(F32) * mixed, ones)
        gx_s[rows, cols] = (grad_den * wide).astype(BF)
        yield
        dfq = mm(edge, stack_k) + mm(gn, held, NT) + grad_den * keys
        back = dfq * wide
        back_low = back.astype(BF)
        scale_grad[:, cols] += jnp.sum(back, axis=0, keepdims=True)
        yield
        dt = mm(back_low, mix_high[...], NT) + mm(back_low, mix_low[...], NT)
        dt = dt - mm(back_low, ones) * turned[0, g][rows] * (HEAD ** (-0.5))
        yield
        out = turn(dt, cosine[rows], -low[rows], -high[rows]).astype(BF)
        dq[rows, cols] = out
        bias_q[:, cols] += jnp.sum(out.astype(F32), axis=0, keepdims=True)
        yield

    interleave([feature(g, which) for g in range(groups) for which in range(2)], 0)
    interleave([unit(g, c) for c in range(span) for g in range(groups)], 0)


def attn_rear_kernel(
    tiles, info, fq_s, fk_s, v_s, tk_s, gn_s, gx_s, mix_high, mix_low, base, inner, bias_in, scale_in, scale,
    w_q, w_k, w_v, shift_in, dk, dv, sums_out, shift_out, bias_k, bias_v, scale_grad, state, total,
):
    step = pl.program_id(0)
    tile = tiles - 1 - step
    groups = dk.shape[1] // GROUP
    span = TILE // CHUNK
    stack_mask, block_mask = patterns()
    ones = jnp.where(block_mask, 1.0, 0.0).astype(BF)
    causal = lax.broadcasted_iota(jnp.int32, (CHUNK, PACK * CHUNK), 1) % CHUNK >= (
        lax.broadcasted_iota(jnp.int32, (CHUNK, PACK * CHUNK), 0)
    )
    upper = jnp.where(
        lax.broadcasted_iota(jnp.int32, (CHUNK, CHUNK), 1) >= lax.broadcasted_iota(jnp.int32, (CHUNK, CHUNK), 0),
        1.0,
        0.0,
    ).astype(BF)

    @pl.when(step == 0)
    def _():
        for item in (state, total, bias_k, bias_v):
            item[...] = jnp.zeros_like(item)
        scale_grad[...] = scale_in[...]

    cosine, low, high = tables(base, inner, tile * span, span)

    def unit(g, c):
        cols = slice(g * GROUP, (g + 1) * GROUP)
        rows = slice(c * CHUNK, (c + 1) * CHUNK)
        fq, fk, vc, gn = fq_s[rows, cols], fk_s[rows, cols], v_s[rows, cols], gn_s[rows, cols]
        stack_q, stack_g = stack(stack_mask, fq), stack(stack_mask, gn)
        kept = state[g]
        held = kept.astype(BF)
        state[g] = kept + jnp.where(block_mask, mm(fq, gn, TN), 0.0)
        sums = mm(upper, gx_s[rows, cols]) + total[g]
        total[g] = sums[0:1, :]
        yield
        edge = jnp.where(causal, mm(vc, stack_g, NT), 0.0).astype(BF)
        yield
        weight = jnp.where(causal, mm(fk, stack_q, NT), 0.0).astype(BF)
        yield
        dfk = mm(edge, stack_q) + mm(vc, held, NT) + sums
        back = dfk * fk.astype(F32)
        back_low = back.astype(BF)
        scale_grad[:, cols] += jnp.sum(back, axis=0, keepdims=True)
        yield
        dvc = (mm(weight, stack_g) + mm(fk, held)).astype(BF)
        dv[rows, cols] = dvc
        bias_v[:, cols] += jnp.sum(dvc.astype(F32), axis=0, keepdims=True)
        yield
        dt = mm(back_low, mix_high[...], NT) + mm(back_low, mix_low[...], NT)
        dt = dt - mm(back_low, ones) * tk_s[rows, cols].astype(F32) * (HEAD ** (-0.5))
        yield
        out = turn(dt, cosine[rows], -low[rows], -high[rows]).astype(BF)
        dk[rows, cols] = out
        bias_k[:, cols] += jnp.sum(out.astype(F32), axis=0, keepdims=True)
        yield

    interleave([unit(g, c) for c in reversed(range(span)) for g in range(groups)], 1)

    @pl.when(step == tiles - 1)
    def _():
        sums_out[0:1, :] = bias_in[...]
        sums_out[1:2, :] = bias_k[...]
        sums_out[2:3, :] = bias_v[...]
        sums_out[3:4, :] = scale_grad[...] / scale[...]
        shift = jnp.broadcast_to(shift_in[...], (8, shift_in.shape[1]))
        for item, w in ((bias_in, w_q), (bias_k, w_k), (bias_v, w_v)):
            high, low_part = split(jnp.broadcast_to(item[...], (8, item.shape[1])))
            shift = shift + mm(high, w[...], NT) + mm(low_part, w[...], NT)
        shift_out[...] = shift[0:1]


def turn_tables():
    lane = np.arange(LANES) % HEAD
    freqs = np.where(lane < ROT, 10000.0 ** (-(lane % (ROT // 2)) / (ROT // 2)), 0.0)
    outer = (np.arange(LEN // CHUNK) * CHUNK)[:, None] * freqs[None, :]
    inner = np.arange(CHUNK)[:, None] * freqs[None, :]
    low = np.broadcast_to(np.where(lane < ROT // 2, -1.0, 0.0), inner.shape)
    high = np.broadcast_to(np.where((lane >= ROT // 2) & (lane < ROT), 1.0, 0.0), inner.shape)
    base = np.stack([np.cos(outer), np.sin(outer)], axis=1).astype(np.float32)
    return base, np.stack([np.cos(inner), np.sin(inner), low, high]).astype(np.float32)


def mixing(qmc_points):
    places = np.arange(HEAD)
    cosines = np.cos(np.pi * (places[:, None] + 0.5) * places[None, :] / HEAD)
    cosines = cosines * np.where(places == 0, math.sqrt(1.0 / HEAD), math.sqrt(2.0 / HEAD))[None, :]
    table = jnp.dot(
        jnp.asarray(cosines * HEAD ** (-0.25), F32), qmc_points, precision=lax.Precision.HIGHEST
    )
    tiled = jnp.tile(table, (PACK, PACK))
    heads = np.arange(GROUP) // HEAD
    tiled = jnp.where(jnp.asarray(heads[:, None] == heads[None, :]), tiled, 0.0)
    high = lax.reduce_precision(tiled, 8, 7)
    return high.astype(BF), (tiled - high).astype(BF)


def stored(tile, info, own):
    return ((tile // own) ^ info[0]) * own + tile % own


def attention_front(info, normed, target, w_qkv, w_proj, vectors, mix, turns):
    total, dim = normed.shape
    half = dim // 2
    tiles = total // TILE
    front = lambda i, info: (stored(i, info, tiles // 2), 0)
    plain = lambda i, info: (i, 0)
    block = lambda k: pl.BlockSpec((dim, half), lambda i, info: (0, 2 * k + info[0]), pipeline_mode=pl.Buffered(1))
    groups = half // GROUP
    return pl.pallas_call(
        attn_front_kernel,
        out_shape=(
            *(jax.ShapeDtypeStruct((total, half), BF) for _ in range(8)),
            *(jax.ShapeDtypeStruct((1, half), F32) for _ in range(2)),
        ),
        grid_spec=pltpu.PrefetchScalarGridSpec(
            num_scalar_prefetch=1,
            grid=(tiles,),
            in_specs=[
                pl.BlockSpec((TILE, dim), front),
                pl.BlockSpec((TILE, dim), front),
                block(0),
                block(1),
                block(2),
                vector_spec(half, 5 * dim, 0),
                vector_spec(half, 6 * dim, 0),
                vector_spec(half, 7 * dim, 0),
                pl.BlockSpec((half, dim), lambda i, info: (info[0], 0), pipeline_mode=pl.Buffered(1)),
                vector_spec(half, 2 * dim, 0),
            ]
            + [whole(item.shape) for item in (*mix, *turns)],
            out_specs=[pl.BlockSpec((TILE, half), front)] * 2
            + [pl.BlockSpec((TILE, half), plain)] * 6
            + [whole((1, half))] * 2,
            scratch_shapes=[pltpu.VMEM((groups, GROUP, GROUP), F32), pltpu.VMEM((groups, 1, GROUP), F32)],
        ),
        compiler_params=params(),
        cost_estimate=cost(8 * total * dim * half + 64 * total * half * GROUP, 12 * total * dim, 2 * total * half),
        name="attention_front",
    )(info, normed, target, w_qkv, w_qkv, w_qkv, vectors, vectors, vectors, w_proj, vectors, *mix, *turns)


def attention_rear(info, saved, bias_q, scale_sum, w_qkv, vectors, shift, mix, turns):
    total, half = saved[0].shape
    dim = w_qkv.shape[0]
    tiles = total // TILE
    rear = lambda i, info: (stored(tiles - 1 - i, info, tiles // 2), 0)
    plain = lambda i, info: (tiles - 1 - i, 0)
    block = lambda k: pl.BlockSpec((dim, half), lambda i, info: (0, 2 * k + info[0]), pipeline_mode=pl.Buffered(1))
    groups = half // GROUP
    return pl.pallas_call(
        partial(attn_rear_kernel, tiles),
        out_shape=(
            *(jax.ShapeDtypeStruct((total, half), BF) for _ in range(2)),
            jax.ShapeDtypeStruct((4, half), F32),
            jax.ShapeDtypeStruct((1, dim), F32),
        ),
        grid_spec=pltpu.PrefetchScalarGridSpec(
            num_scalar_prefetch=1,
            grid=(tiles,),
            in_specs=[pl.BlockSpec((TILE, half), plain)] * 6
            + [whole(item.shape) for item in (*mix, *turns, bias_q, scale_sum)]
            + [vector_spec(half, 2 * dim, 0), block(0), block(1), block(2), whole(shift.shape)],
            out_specs=[pl.BlockSpec((TILE, half), rear)] * 2 + [whole((4, half)), whole((1, dim))],
            scratch_shapes=[pltpu.VMEM((1, half), F32) for _ in range(3)]
            + [pltpu.VMEM((groups, GROUP, GROUP), F32), pltpu.VMEM((groups, 1, GROUP), F32)],
        ),
        compiler_params=params(),
        cost_estimate=cost(48 * total * half * GROUP, 16 * total * half, 0),
        name="attention_rear",
    )(info, *saved, *mix, *turns, bias_q, scale_sum, vectors, w_qkv, w_qkv, w_qkv, shift)


def out_kernel(own, info, act, attended, w_proj, w_down, *rest):
    step = pl.program_id(0)
    if own:
        res, received, first, second, out, down_buf, sems = rest
    else:
        out, down_buf, sems = rest

    @pl.when(step == 0)
    def _():
        @pl.loop(0, down_buf.shape[0] // LANES)
        def _(j):
            strip_copy(info[0], w_down, down_buf, sems, 1, j).start()

        @pl.loop(0, down_buf.shape[0] // LANES)
        def _(j):
            strip_copy(info[0], w_down, down_buf, sems, 1, j).wait()

    value = mm(act[...], down_buf[...]) + mm(attended[...], w_proj[...])
    if own:
        value = value + received[...].astype(F32) + (first[...] + second[...]) + res[...].astype(F32)
    out[...] = value.astype(BF)


def out_rows(own, info, act, attended, w_proj, w_down, res=None, received=None, vectors=None):
    total, ff = act.shape
    dim = w_proj.shape[1]
    half = attended.shape[1]
    rows = total // 2
    tiles = rows // TILE
    shift = 0 if own else tiles
    shifted = lambda i, info: (i + shift, 0)
    plain = lambda i, info: (i, 0)
    extra, extra_specs = (), []
    if own:
        extra = (res, received, vectors, vectors)
        extra_specs = [pl.BlockSpec((TILE, dim), plain), pl.BlockSpec((TILE, dim), plain)]
        extra_specs += [vector_spec(dim, 3 * dim), vector_spec(dim, 4 * dim)]
    return pl.pallas_call(
        partial(out_kernel, own),
        out_shape=jax.ShapeDtypeStruct((rows, dim), BF),
        grid_spec=pltpu.PrefetchScalarGridSpec(
            num_scalar_prefetch=1,
            grid=(tiles,),
            in_specs=[
                pl.BlockSpec((TILE, ff), shifted),
                pl.BlockSpec((TILE, half), shifted),
                pl.BlockSpec((half, dim), lambda i, info: (info[0], 0), pipeline_mode=pl.Buffered(1)),
                anywhere(),
            ]
            + extra_specs,
            out_specs=pl.BlockSpec((TILE, dim), plain),
            scratch_shapes=[pltpu.VMEM((ff, dim), BF), pltpu.SemaphoreType.DMA((2, ff // LANES))],
        ),
        compiler_params=params(),
        cost_estimate=cost(2 * rows * dim * (ff + half), 2 * rows * (ff + half + dim) + 2 * dim * (ff + half)),
        name="out_rows",
    )(info, act, attended, w_proj, w_down, *extra)


def back_kernel(own, info, dq, dk, dv, up_grad, w_q, w_k, w_v, w_up, *rest):
    step = pl.program_id(0)
    if own:
        res, gain, target, received, out, up_buf, sems = rest
    else:
        out, up_buf, sems = rest

    @pl.when(step == 0)
    def _():
        @pl.loop(0, up_buf.shape[1] // LANES)
        def _(j):
            strip_copy(info[0], w_up, up_buf, sems, 0, j).start()

        @pl.loop(0, up_buf.shape[1] // LANES)
        def _(j):
            strip_copy(info[0], w_up, up_buf, sems, 0, j).wait()

    value = mm(up_grad[...], up_buf[...], NT)
    for grad, w in ((dq, w_q), (dk, w_k), (dv, w_v)):
        value = value + mm(grad[...], w[...], NT)
    if own:
        xhat, rstd = norm_stats(res[...].astype(F32))
        scaled = (value + received[...].astype(F32)) * gain[...]
        middle = jnp.mean(scaled, axis=-1, keepdims=True)
        slope = jnp.mean(scaled * xhat, axis=-1, keepdims=True)
        out[...] = target[...].astype(F32) + rstd * (scaled - middle - xhat * slope)
    else:
        out[...] = value.astype(BF)


def back_rows(own, info, dq, dk, dv, up_grad, w_qkv, w_up, res=None, vectors=None, target=None, received=None):
    total, ff = up_grad.shape
    rows, dim = total // 2, w_qkv.shape[0]
    half = dq.shape[1]
    tiles = rows // TILE
    shift = 0 if own else tiles
    shifted = lambda i, info: (i + shift, 0)
    plain = lambda i, info: (i, 0)
    block = lambda k: pl.BlockSpec((dim, half), lambda i, info: (0, 2 * k + info[0]), pipeline_mode=pl.Buffered(1))
    extra, extra_specs = (), []
    if own:
        extra = (res, vectors, target, received)
        extra_specs = [
            pl.BlockSpec((TILE, dim), plain),
            vector_spec(dim, 0),
            pl.BlockSpec((TILE, dim), plain),
            pl.BlockSpec((TILE, dim), plain),
        ]
    return pl.pallas_call(
        partial(back_kernel, own),
        out_shape=jax.ShapeDtypeStruct((rows, dim), F32 if own else BF),
        grid_spec=pltpu.PrefetchScalarGridSpec(
            num_scalar_prefetch=1,
            grid=(tiles,),
            in_specs=[pl.BlockSpec((TILE, half), shifted)] * 3
            + [pl.BlockSpec((TILE, ff), shifted), block(0), block(1), block(2), anywhere()]
            + extra_specs,
            out_specs=pl.BlockSpec((TILE, dim), plain),
            scratch_shapes=[pltpu.VMEM((dim, ff), BF), pltpu.SemaphoreType.DMA((2, ff // LANES))],
        ),
        compiler_params=params(),
        cost_estimate=cost(2 * rows * dim * (ff + 3 * half), 2 * rows * (ff + 3 * half + 3 * dim) + 2 * dim * (ff + 3 * half)),
        name="back_rows",
    )(info, dq, dk, dv, up_grad, w_qkv, w_qkv, w_qkv, w_up, *extra)


def bit_orders(ndp):
    bits = [1 << j for j in range(ndp.bit_length() - 1)]
    return tuple(bits), tuple(bits[1::-1] + bits[2:])


def spots(me, ndp):
    apart = jnp.asarray(np.arange(ndp, dtype=np.int32)) ^ me
    rows = []
    for order in bit_orders(ndp):
        spot = jnp.zeros((ndp,), jnp.int32)
        for j, bit in enumerate(order):
            spot = spot + (((apart // bit) % 2) << (len(order) - 1 - j))
        rows.append(spot)
    return jnp.stack(rows)


def add(left, right, kind=BF):
    return (left.astype(F32) + right.astype(F32)).astype(kind)


def cross(value, bit, ndp):
    return lax.ppermute(value, "dp", [(i, i ^ bit) for i in range(ndp)])


class Reduction:
    def __init__(self, first, second, ndp):
        self.ndp = ndp
        self.orders = bit_orders(ndp)
        self.at = 0
        self.pairs = [first, second]
        self.fly()

    def fly(self):
        self.received = [
            cross(send, order[self.at], self.ndp) for (send, keep), order in zip(self.pairs, self.orders)
        ]

    def land(self, token=None):
        if token is not None:
            token, *self.received = lax.optimization_barrier((token, *self.received))
        self.step()
        return token

    def step(self):
        keeps = [keep for send, keep in self.pairs]
        self.at += 1
        steps = len(self.orders[0])
        if self.at == steps:
            parts = [add(k, r, F32)[0] for k, r in zip(keeps, self.received)]
            self.result = jnp.concatenate(parts, axis=0) if len(parts) > 1 else parts[0]
            return
        cut = keeps[0].shape[0] // 2
        pairs = [
            (add(k[cut:], r[cut:]), add(k[:cut], r[:cut])) for k, r in zip(keeps, self.received)
        ]
        if self.at == 2 and len(pairs) == 2:
            pairs = [tuple(jnp.concatenate(items, axis=1) for items in zip(*pairs))]
        self.pairs = pairs

    def finish(self):
        while self.at < len(self.orders[0]):
            self.land()
            if self.at < len(self.orders[0]):
                self.fly()
        return self.result

    def values(self):
        return [item for pair in self.pairs for item in pair]

    def after(self, token):
        if self.at < len(self.orders[0]):
            token, *items = lax.optimization_barrier((token, *self.values()))
            self.pairs = [(items[2 * j], items[2 * j + 1]) for j in range(len(items) // 2)]
            self.fly()
        else:
            token, self.result = lax.optimization_barrier((token, self.result))
        return token


def swap(value):
    return lax.ppermute(value, "stream", [(0, 1), (1, 0)])


def per_device(
    ndp, residual, cotangent, ln_gain, ln_bias, w_qkv, b_qkv, w_proj, b_proj, feature_scale,
    w_up, b_up, w_down, b_down, qmc_points, slot_lengths,
):
    own_rows, dim = residual.shape
    half = dim // 2
    ff = w_up.shape[1]
    side = lax.axis_index("stream")
    me = lax.axis_index("dp")
    info = jnp.stack([side, me, slot_lengths[0]]).astype(jnp.int32)
    table = spots(me, ndp)
    vectors = jnp.concatenate([ln_gain, ln_bias, feature_scale, b_proj, b_down, b_qkv, b_up])
    vectors = vectors.astype(F32).reshape(1, -1)

    other_res = swap(residual)
    other_cot = swap(cotangent)
    *mine, target_sum = mlp_rows(0, info, residual, cotangent, vectors, w_up, w_down)
    normed, target, act, up_grad, upb, shift = mlp_rows(
        1, info, other_res, other_cot, vectors, w_up, w_down, mine
    )

    mix = mixing(qmc_points)
    turns = tuple(jnp.asarray(item) for item in turn_tables())
    down_parts = mlp_weight_grad(0, 1, ndp, table, act, target)
    up_parts = mlp_weight_grad(1, 2, ndp, table, normed, up_grad)
    mlp_sums = Reduction(down_parts, up_parts, ndp)

    attended, dq, *saved, bias_q, scale_sum = attention_front(
        info, normed, target, w_qkv, w_proj, vectors, mix, turns
    )
    attended = mlp_sums.land(attended)
    info = mlp_sums.after(info)
    dk, dv, sums, shift = attention_rear(info, saved, bias_q, scale_sum, w_qkv, vectors, shift, mix, turns)
    dk = mlp_sums.land(dk)
    table = mlp_sums.after(table)

    mine = lax.broadcasted_iota(jnp.int32, (1, 2, 1), 1) == side
    spread = lambda item: jnp.where(mine, item[:, None, :], 0.0)
    four = spread(sums)
    small = jnp.concatenate(
        [
            shift.reshape(ndp, -1),
            four[:3].reshape(ndp, -1),
            target_sum.reshape(ndp, -1),
            four[3].reshape(ndp, -1),
            spread(upb.reshape(-1, LANES)).reshape(ndp, -1),
        ],
        axis=1,
    )
    count = small.shape[1]
    extra = jnp.pad(small.astype(BF), ((0, 0), (0, 8 * half - count))).reshape(ndp, 8, half)
    parts = attn_weight_grads(ndp, table, normed, target, attended, dq, dk, dv, extra)
    attn_sums = Reduction(parts[:2], parts[2:], ndp)
    mlp_sums.land()
    info = mlp_sums.after(info)

    back_send = back_rows(False, info, dq, dk, dv, up_grad, w_qkv, w_up)
    back_send = attn_sums.land(back_send)
    info = attn_sums.after(info)
    back_received = swap(back_send)
    out_send = out_rows(False, info, act, attended, w_proj, w_down)
    out_send = attn_sums.land(mlp_sums.land(out_send))
    info = attn_sums.after(mlp_sums.after(info))
    out_received = swap(out_send)
    residual_grad = back_rows(
        True, info, dq, dk, dv, up_grad, w_qkv, w_up, residual, vectors, target, back_received
    )
    residual_grad = attn_sums.land(residual_grad)
    info = attn_sums.after(info)
    block_out = out_rows(True, info, act, attended, w_proj, w_down, residual, out_received, vectors)
    mlp_total, attn_total = mlp_sums.finish(), attn_sums.finish()

    blk = ff // (2 * ndp)
    size = dim // ndp
    small_size = size // 2
    down_rows = mlp_total[:blk]
    per = max(LANES // blk, 1)
    owners = [
        (v * 2 + s, (2 * (v // per) + s) * per + v % per) for v in range(ndp) for s in range(2)
    ]
    if any(a != b for a, b in owners):
        down_rows = lax.ppermute(down_rows, ("dp", "stream"), owners)

    def halves(blocks):
        blocks = blocks.reshape(blocks.shape[0], 2, small_size, blocks.shape[2])
        pick = lambda at: lax.dynamic_index_in_dim(blocks, at, 1, keepdims=False)
        return pick(side), pick(1 - side)

    def order(own, other):
        return jnp.where(side == 0, own, other), jnp.where(side == 0, other, own)

    keep, give = halves(mlp_total[blk:].reshape(2, size, -1))
    first, second = order(keep, swap(give))
    apart = lambda item: jnp.transpose(item, (1, 0, 2)).reshape(small_size, -1, 1, LANES)
    upw_grad = jnp.concatenate([apart(first), apart(second)], axis=2).reshape(small_size, ff)

    keep, give = halves(attn_total[: 3 * size].reshape(3, size, half))
    rest = attn_total[4 * size :]
    received = swap(jnp.concatenate([give.reshape(3 * small_size, half), rest], axis=0))
    first, second = order(keep, received[: 3 * small_size].reshape(3, small_size, half))
    qkvw_grad = jnp.concatenate([item[p] for p in range(3) for item in (first, second)], axis=1)
    proj_rows = jnp.concatenate(
        [attn_total[3 * size + p * small_size : 3 * size + (p + 1) * small_size] for p in range(2)], axis=1
    )
    proj_owners = [(v * 2 + s, ndp * s + v) for v in range(ndp) for s in range(2)]
    projw_grad = lax.ppermute(proj_rows, ("dp", "stream"), proj_owners)

    flat = (rest + received[3 * small_size :]).reshape(-1)
    ends = np.cumsum([0, size, 3 * size, size, size, 2 * blk])
    pieces = [
        lax.dynamic_index_in_dim(flat[a:b].reshape(2, -1), side, 0, keepdims=False)
        for a, b in zip(ends[:-1], ends[1:])
    ]
    shift_grad, qkvb_grad, projb_grad, scale_grad, upb_grad = pieces
    mine_at = (2 * me + side) * small_size
    near = lambda item: lax.dynamic_slice_in_dim(item, mine_at, small_size).astype(F32)
    along = jnp.sum(near(w_qkv) * qkvw_grad, axis=1) + jnp.sum(near(w_up) * upw_grad, axis=1)
    gain_grad = (along - near(ln_bias) * shift_grad) / near(ln_gain)

    return (
        block_out, residual_grad, gain_grad, shift_grad, qkvw_grad, qkvb_grad, projw_grad,
        projb_grad, scale_grad, upw_grad, upb_grad, down_rows, projb_grad,
    )


def solution(mesh):
    rows = P(("dp", "stream"), None)
    items = P(("dp", "stream"))
    return jax.shard_map(
        partial(per_device, mesh.shape["dp"]),
        mesh=mesh,
        in_specs=(rows, rows) + (P(),) * 12 + (P("dp"),),
        out_specs=(rows, rows, items, items, rows, items, rows, items, items, rows, items, rows, items),
        check_vma=False,
    )
```

```python
from functools import partial
import math

import jax
import jax.numpy as jnp
import numpy as np
from jax import lax
from jax.experimental import pallas as pl
from jax.experimental.pallas import tpu as pltpu
from jax.sharding import PartitionSpec as P

HEAD = 64
ROT = 16
LEN = 2048
EPSILON = 1e-05

BF = jnp.bfloat16
F32 = jnp.float32
TILE = 256
CHUNK = 128
GROUP = 256
PACK = GROUP // HEAD
LANES = 128
ERFC = tuple(
    item * math.sqrt(0.5 * math.pi)
    for item in (0.254829592, -0.284496736, 1.421413741, -1.453152027, 1.061405429)
)
VMEM_CAP = 55 * 1024 * 1024

NN = (((1,), (0,)), ((), ()))
NT = (((1,), (1,)), ((), ()))
TN = (((0,), (0,)), ((), ()))


def mm(left, right, dims=NN):
    return lax.dot_general(left, right, dims, preferred_element_type=F32)


def split(value):
    high = value.astype(BF)
    return high, (value - high.astype(F32)).astype(BF)


def whole(shape):
    rank = len(shape)
    return pl.BlockSpec(shape, lambda *_: (0,) * rank, pipeline_mode=pl.Buffered(1))


def anywhere():
    return pl.BlockSpec(memory_space=pl.ANY)


def params(limit=VMEM_CAP):
    return pltpu.CompilerParams(vmem_limit_bytes=limit)


def vector_spec(width, at, side=None):
    return pl.BlockSpec(
        (1, width),
        lambda i, info: (0, at // width + (0 if side is None else info[0])),
        pipeline_mode=pl.Buffered(1),
    )


def cost(flops, moved, trans=0):
    return pl.CostEstimate(flops=int(0.4 * flops), bytes_accessed=int(0.4 * moved), transcendentals=int(0.4 * trans))


def exact_row(row, weights):
    high, low = split(jnp.broadcast_to(row, (8, row.shape[1])))
    both = mm(jnp.concatenate([high, low], axis=0), weights, NT)
    return both[0:1] + both[8:9]


def norm_stats(rows):
    mean = jnp.mean(rows, axis=-1, keepdims=True)
    centred = rows - mean
    rstd = lax.rsqrt(jnp.mean(centred * centred, axis=-1, keepdims=True) + EPSILON)
    return centred * rstd, rstd


def strip_copy(side, source, buf, sems, kind, j):
    there = pl.ds(pl.multiple_of((2 * j + side) * LANES, LANES), LANES)
    here = pl.ds(pl.multiple_of(j * LANES, LANES), LANES)
    if kind == 0:
        return pltpu.make_async_copy(source.at[:, there], buf.at[:, here], sems.at[kind, j])
    return pltpu.make_async_copy(source.at[there, :], buf.at[here, :], sems.at[kind, j])


def part_copy(side, source, buf, sems, p):
    width = buf.shape[1] // 3
    there = pl.ds(pl.multiple_of((2 * p + side) * width, LANES), width)
    return pltpu.make_async_copy(source.at[:, there], buf.at[:, p * width : (p + 1) * width], sems.at[p])


def mlp_kernel(half, tiles, info, res, cot, gain, bias, b_up, w_up, w_down, *rest):
    normed, target, act, up_grad, upb, sums, up_buf, down_buf, sems = rest[-9:]
    step = pl.program_id(0)
    side = info[0]

    @pl.when(step == 0)
    def _():
        @pl.loop(0, up_buf.shape[1] // LANES)
        def _(j):
            strip_copy(side, w_up, up_buf, sems, 0, j).start()
            strip_copy(side, w_down, down_buf, sems, 1, j).start()

        if half == 0:
            upb[...] = jnp.zeros_like(upb)
            sums[...] = jnp.zeros_like(sums)
        else:
            upb[...] = rest[4][...]

    rows = res.shape[0]
    xhat, _ = norm_stats(res[...].astype(F32))
    low = (xhat * gain[...] + bias[...]).astype(BF)
    normed[...] = low
    part = side if half == 0 else 1 - side
    place = (part * tiles + step) * rows + lax.broadcasted_iota(jnp.int32, (rows, 1), 0)
    tgt = jnp.where(place < info[2], cot[...], jnp.zeros_like(cot))
    target[...] = tgt
    ones = jnp.ones((8, rows), BF)
    if half == 0:
        sums[...] += mm(ones, tgt)[0:1]
    width = 1024
    strips = width // LANES

    @pl.loop(0, up_buf.shape[1] // width)
    def _(j):
        cols = pl.ds(pl.multiple_of(j * width, width), width)

        @pl.when(step == 0)
        def _():
            for b in range(strips):
                strip_copy(side, w_up, up_buf, sems, 0, j * strips + b).wait()
                strip_copy(side, w_down, down_buf, sems, 1, j * strips + b).wait()

        shift = jnp.concatenate(
            [
                b_up[:, pl.ds(pl.multiple_of((2 * (j * strips + b) + side) * LANES, LANES), LANES)]
                for b in range(strips)
            ],
            axis=1,
        )
        up = mm(low, up_buf[:, cols]) + shift
        back = mm(tgt, down_buf[cols, :], NT)
        bell = jnp.exp2(up * up * (-0.5 * math.log2(math.e)) - 0.5 * math.log2(2.0 * math.pi))
        t = 1.0 / (1.0 + (0.3275911 * math.sqrt(0.5)) * jnp.abs(up))
        poly = ERFC[4]
        for item in ERFC[3::-1]:
            poly = item + t * poly
        tail = (t * bell) * poly
        phi = jnp.where(up >= 0, 1.0 - tail, tail)
        act[:, cols] = (up * phi).astype(BF)
        grad = (back * (phi + up * bell)).astype(BF)
        up_grad[:, cols] = grad
        upb[:, cols] += mm(ones, grad)[0:1]

    if half == 1:

        @pl.when(step == tiles - 1)
        def _():
            sums[...] = jnp.zeros_like(sums)

            @pl.loop(0, upb.shape[1] // GROUP)
            def _(j):
                cols = pl.ds(pl.multiple_of(j * GROUP, GROUP), GROUP)
                sums[...] += exact_row(upb[:, cols], up_buf[:, cols])


def mlp_rows(half, info, res, cot, vectors, w_up, w_down, earlier=()):
    rows, dim = res.shape
    ff = w_up.shape[1] // 2
    tiles = rows // TILE
    total = 2 * rows
    shift = half * tiles
    row_map = lambda i, info: (i, 0)
    out_map = lambda i, info: (i + shift, 0)
    outs = (
        jax.ShapeDtypeStruct((total, dim), BF),
        jax.ShapeDtypeStruct((total, dim), BF),
        jax.ShapeDtypeStruct((total, ff), BF),
        jax.ShapeDtypeStruct((total, ff), BF),
        jax.ShapeDtypeStruct((1, ff), F32),
        jax.ShapeDtypeStruct((1, dim), F32),
    )
    return pl.pallas_call(
        partial(mlp_kernel, half, tiles),
        out_shape=outs,
        grid_spec=pltpu.PrefetchScalarGridSpec(
            num_scalar_prefetch=1,
            grid=(tiles,),
            in_specs=[
                pl.BlockSpec((TILE, dim), row_map),
                pl.BlockSpec((TILE, dim), row_map),
                vector_spec(dim, 0),
                vector_spec(dim, dim),
                vector_spec(2 * ff, 8 * dim),
                anywhere(),
                anywhere(),
            ]
            + [anywhere()] * (len(earlier) - 1)
            + [whole((1, ff))] * min(len(earlier), 1),
            out_specs=[
                pl.BlockSpec((TILE, dim), out_map),
                pl.BlockSpec((TILE, dim), out_map),
                pl.BlockSpec((TILE, ff), out_map),
                pl.BlockSpec((TILE, ff), out_map),
                whole((1, ff)),
                whole((1, dim)),
            ],
            scratch_shapes=[
                pltpu.VMEM((dim, ff), BF),
                pltpu.VMEM((ff, dim), BF),
                pltpu.SemaphoreType.DMA((2, ff // LANES)),
            ],
        ),
        input_output_aliases={8 + j: j for j in range(len(earlier) - 1)},
        compiler_params=params(63 * 1024 * 1024),
        cost_estimate=cost(4 * rows * dim * ff, 12 * rows * dim + 16 * rows * ff, 2 * rows * ff),
        name="mlp_rows",
    )(info, res, cot, vectors, vectors, vectors, w_up, w_down, *earlier)


def ship(table, which, buf, send, keep, sems, first, count):
    half = send.shape[0]
    for b in range(count):
        spot = table[which, first + b]

        @pl.when(spot >= half)
        def _():
            pltpu.make_async_copy(buf.at[first + b], send.at[spot - half], sems.at[first + b]).start()

        @pl.when(spot < half)
        def _():
            pltpu.make_async_copy(buf.at[first + b], keep.at[spot], sems.at[first + b]).start()


def shipped(buf, keep, sems):
    for b in range(buf.shape[0]):
        pltpu.make_async_copy(buf.at[b], keep.at[0], sems.at[b]).wait()


def mlp_grad_kernel(
    tiles, table, act, target, normed, up_grad, send_a, keep_a, send_b, keep_b,
    grads, buf_a, buf_b, sems_a, sems_b, sem,
):
    step = pl.program_id(0)

    @pl.when(step == 0)
    def _():
        pltpu.make_async_copy(up_grad, grads, sem).start()

    @pl.when(step < tiles)
    def _():
        value = mm(act[...], target[...], TN).astype(BF)
        size = buf_a.shape[1]
        count = value.shape[0] // size
        first = step * count
        for b in range(count):
            buf_a[first + b] = value[b * size : (b + 1) * size, :]
        ship(table, 0, buf_a, send_a, keep_a, sems_a, first, count)

    @pl.when(step == tiles)
    def _():
        pltpu.make_async_copy(up_grad, grads, sem).wait()

    @pl.when(step >= tiles)
    def _():
        value = mm(normed[...], grads[...], TN).astype(BF)
        size = buf_b.shape[1] // 2
        width = buf_b.shape[2]
        count = value.shape[0] // size
        first = (step - tiles) * count
        for b in range(count):
            for p in range(2):
                buf_b[first + b, p * size : (p + 1) * size, :] = value[
                    b * size : (b + 1) * size, p * width : (p + 1) * width
                ]
        ship(table, 1, buf_b, send_b, keep_b, sems_b, first, count)

    @pl.when(step == pl.num_programs(0) - 1)
    def _():
        shipped(buf_a, keep_a, sems_a)
        shipped(buf_b, keep_b, sems_b)


def mlp_weight_grads(ndp, table, act, target, normed, up_grad):
    total, dim = normed.shape
    ff = act.shape[1]
    rows = ff // ndp
    shape = jax.ShapeDtypeStruct((ndp // 2, rows, dim), BF)
    wide, narrow = 512, 256
    tiles = ff // wide
    return pl.pallas_call(
        partial(mlp_grad_kernel, tiles),
        out_shape=(shape,) * 4,
        grid_spec=pltpu.PrefetchScalarGridSpec(
            num_scalar_prefetch=1,
            grid=(tiles + dim // narrow,),
            in_specs=[
                pl.BlockSpec((total, wide), lambda i, t: (0, jnp.minimum(i, tiles - 1))),
                whole((total, dim)),
                pl.BlockSpec((total, narrow), lambda i, t: (0, jnp.maximum(i - tiles, 0))),
                anywhere(),
            ],
            out_specs=[anywhere()] * 4,
            scratch_shapes=[pltpu.VMEM((total, ff), BF)]
            + [pltpu.VMEM((ndp, rows, dim), BF)] * 2
            + [pltpu.SemaphoreType.DMA((ndp,))] * 2
            + [pltpu.SemaphoreType.DMA],
        ),
        compiler_params=params(),
        cost_estimate=cost(4 * total * dim * ff, 4 * total * (dim + ff) + 4 * dim * ff),
        name="mlp_weight_grads",
    )(table, act, target, normed, up_grad)


def attn_grad_kernel(
    table, normed, attended, target, dq, dk, dv, extra, send_a, keep_a, send_b, keep_b, buf_a, buf_b, sems_a, sems_b
):
    step = pl.program_id(0)
    ndp = buf_a.shape[0]
    size = buf_a.shape[1] // 2
    small = size // 2
    half = dq.shape[1]

    @pl.when(step == 0)
    def _():
        value = mm(attended[...], target[...], TN).astype(BF)
        for b in range(ndp):
            for p in range(2):
                at = size + p * small
                buf_b[b, at : at + small, :] = value[b * small : (b + 1) * small, p * half : (p + 1) * half]
            buf_b[b, 2 * size :, :] = extra[b]

    count = normed.shape[1] // size
    first = step * count
    for item, buf, at in ((dq, buf_a, 0), (dk, buf_a, size), (dv, buf_b, 0)):
        value = mm(normed[...], item[...], TN).astype(BF)
        for b in range(count):
            buf[first + b, at : at + size, :] = value[b * size : (b + 1) * size, :]
    ship(table, 0, buf_a, send_a, keep_a, sems_a, first, count)
    ship(table, 1, buf_b, send_b, keep_b, sems_b, first, count)

    @pl.when(step == pl.num_programs(0) - 1)
    def _():
        shipped(buf_a, keep_a, sems_a)
        shipped(buf_b, keep_b, sems_b)


def attn_weight_grads(ndp, table, normed, target, attended, dq, dk, dv, extra):
    total, dim = normed.shape
    half = dq.shape[1]
    rows = 2 * dim // ndp
    more = extra.shape[1]
    shapes = [jax.ShapeDtypeStruct((ndp // 2, rows + j * more, half), BF) for j in range(2)]
    step = 256
    return pl.pallas_call(
        attn_grad_kernel,
        out_shape=(shapes[0], shapes[0], shapes[1], shapes[1]),
        grid_spec=pltpu.PrefetchScalarGridSpec(
            num_scalar_prefetch=1,
            grid=(dim // step,),
            in_specs=[
                pl.BlockSpec((total, step), lambda i, t: (0, i)),
                whole((total, half)),
                whole((total, dim)),
            ]
            + [whole((total, half))] * 3
            + [whole(extra.shape)],
            out_specs=[anywhere()] * 4,
            scratch_shapes=[pltpu.VMEM((ndp, rows + j * more, half), BF) for j in range(2)]
            + [pltpu.SemaphoreType.DMA((ndp,))] * 2,
        ),
        compiler_params=params(),
        cost_estimate=cost(8 * total * dim * half, 2 * total * (2 * dim + 4 * half) + 8 * dim * half),
        name="attn_weight_grads",
    )(table, normed, attended, target, dq, dk, dv, extra)


def turn(value, cosine, sine_low, sine_high):
    pieces = []
    for j in range(value.shape[1] // LANES):
        item = value[:, j * LANES : (j + 1) * LANES]
        pieces.append(
            item * cosine
            + pltpu.roll(item, LANES - ROT // 2, 1) * sine_low
            + pltpu.roll(item, ROT // 2, 1) * sine_high
        )
    return jnp.concatenate(pieces, axis=1)


def patterns():
    row_head = lax.broadcasted_iota(jnp.int32, (PACK * CHUNK, GROUP), 0) // CHUNK
    lane_head = lax.broadcasted_iota(jnp.int32, (PACK * CHUNK, GROUP), 1) // HEAD
    block_row = lax.broadcasted_iota(jnp.int32, (GROUP, GROUP), 0) // HEAD
    block_col = lax.broadcasted_iota(jnp.int32, (GROUP, GROUP), 1) // HEAD
    return row_head == lane_head, block_row == block_col


def interleave(items, lag):
    waiting = [(j * lag, item) for j, item in enumerate(items)]
    at = 0
    while waiting:
        alive = []
        for begin, item in waiting:
            if at < begin or next(item, waiting) is not waiting:
                alive.append((begin, item))
        waiting = alive
        at += 1


def stack(mask, item):
    return jnp.where(mask, jnp.concatenate([item] * PACK, axis=0), jnp.zeros((), BF))


def sum_heads(item, ones):
    high, low = split(item)
    return mm(high, ones) + mm(low, ones)


def tables(coarse, fine, tile):
    rows = TILE // 8
    co, so = [], []
    outer = coarse[pl.ds(tile * rows, rows)]
    ci, si = fine[0:8, :][None], fine[8:16, :][None]
    co, so = outer[:, 0:1, :], outer[:, 1:2, :]
    flat = lambda item: item.reshape(TILE, LANES)
    cosine = flat(co * ci - so * si)
    sine = so * ci + co * si
    return cosine, flat(sine * fine[16:24, :][None]), flat(sine * fine[24:32, :][None])


def attn_front_kernel(
    info, normed, target, w_q, w_k, w_v, b_q, b_k, b_v, w_proj, scale, mix_high, mix_low, base, inner,
    attended, dq, fq_s, fk_s, v_s, tk_s, gn_s, gx_s, bias_q, scale_grad, state, total,
):
    step = pl.program_id(0)
    groups = w_q.shape[1] // GROUP
    span = TILE // CHUNK
    stack_mask, block_mask = patterns()
    ones = jnp.where(block_mask, 1.0, 0.0).astype(BF)
    causal = lax.broadcasted_iota(jnp.int32, (CHUNK, PACK * CHUNK), 0) >= (
        lax.broadcasted_iota(jnp.int32, (CHUNK, PACK * CHUNK), 1) % CHUNK
    )
    lower = jnp.where(
        lax.broadcasted_iota(jnp.int32, (CHUNK, CHUNK), 0) >= lax.broadcasted_iota(jnp.int32, (CHUNK, CHUNK), 1),
        1.0,
        0.0,
    ).astype(BF)

    @pl.when(step == 0)
    def _():
        for item in (state, total, bias_q, scale_grad):
            item[...] = jnp.zeros_like(item)

    x = normed[...]
    cosine, low, high = tables(base, inner, step)
    grad_all = mm(target[...], w_proj[...], NT)
    feats, turned, values, held, before = {}, {}, {}, {}, {}

    def feature(g, which):
        cols = slice(g * GROUP, (g + 1) * GROUP)
        w, b, out = ((w_q, b_q, fq_s), (w_k, b_k, fk_s))[which]
        t = mm(x, w[:, cols]) + b[:, cols]
        yield
        t = turn(t, cosine, low, high)
        turned[which, g] = t
        t_high, t_low = split(t)
        spread = mm(t_high, mix_high[...]) + mm(t_low, mix_high[...]) + mm(t_high, mix_low[...])
        yield
        square = sum_heads(t * t, ones)
        yield
        feats[which, g] = (scale[:, cols] * jnp.exp(spread - square * (0.5 * HEAD ** (-0.5)))).astype(BF)
        out[:, cols] = feats[which, g]
        if which == 1:
            tk_s[:, cols] = t.astype(BF)
            values[g] = (mm(x, w_v[:, cols]) + b_v[:, cols]).astype(BF)
            v_s[:, cols] = values[g]
        yield

    def unit(g, c):
        cols = slice(g * GROUP, (g + 1) * GROUP)
        rows = slice(c * CHUNK, (c + 1) * CHUNK)
        fq, fk, vc = feats[0, g][rows], feats[1, g][rows], values[g][rows]
        stack_k, stack_v = stack(stack_mask, fk), stack(stack_mask, vc)
        kept = state[g]
        held = kept.astype(BF)
        state[g] = kept + jnp.where(block_mask, mm(fk, vc, TN), 0.0)
        keys = mm(lower, fk) + total[g]
        total[g] = keys[CHUNK - 1 : CHUNK, :]
        yield
        weight = jnp.where(causal, mm(fq, stack_k, NT), 0.0).astype(BF)
        wide = fq.astype(F32)
        den = sum_heads(wide * keys, ones)
        yield
        num = mm(weight, stack_v) + mm(fq, held)
        inverse = 1.0 / den
        yield
        mixed = num * inverse
        attended[rows, cols] = mixed.astype(BF)
        gn = (grad_all[rows, cols] * inverse).astype(BF)
        gn_s[rows, cols] = gn
        edge = jnp.where(causal, mm(gn, stack_v, NT), 0.0).astype(BF)
        yield
        grad_den = -sum_heads(gn.astype(F32) * mixed, ones)
        gx_s[rows, cols] = (grad_den * wide).astype(BF)
        yield
        dfq = mm(edge, stack_k) + mm(gn, held, NT) + grad_den * keys
        back = dfq * wide
        back_low = back.astype(BF)
        scale_grad[:, cols] += jnp.sum(back, axis=0, keepdims=True)
        yield
        dt = mm(back_low, mix_high[...], NT) + mm(back_low, mix_low[...], NT)
        dt = dt - mm(back_low, ones) * turned[0, g][rows] * (HEAD ** (-0.5))
        yield
        out = turn(dt, cosine[rows], -low[rows], -high[rows]).astype(BF)
        dq[rows, cols] = out
        bias_q[:, cols] += jnp.sum(out.astype(F32), axis=0, keepdims=True)
        yield

    interleave([feature(g, which) for g in range(groups) for which in range(2)], 0)
    interleave([unit(g, c) for c in range(span) for g in range(groups)], 0)


def attn_rear_kernel(
    tiles, info, fq_s, fk_s, v_s, tk_s, gn_s, gx_s, mix_high, mix_low, base, inner, bias_in, scale_in, scale,
    w_qkv, shift_in, dk, dv, sums_out, shift_out, bias_k, bias_v, scale_grad, w_buf, sems, state, total,
):
    step = pl.program_id(0)
    tile = tiles - 1 - step
    groups = dk.shape[1] // GROUP
    span = TILE // CHUNK
    stack_mask, block_mask = patterns()
    ones = jnp.where(block_mask, 1.0, 0.0).astype(BF)
    causal = lax.broadcasted_iota(jnp.int32, (CHUNK, PACK * CHUNK), 1) % CHUNK >= (
        lax.broadcasted_iota(jnp.int32, (CHUNK, PACK * CHUNK), 0)
    )
    upper = jnp.where(
        lax.broadcasted_iota(jnp.int32, (CHUNK, CHUNK), 1) >= lax.broadcasted_iota(jnp.int32, (CHUNK, CHUNK), 0),
        1.0,
        0.0,
    ).astype(BF)

    @pl.when(step == 0)
    def _():
        for item in (state, total, bias_k, bias_v):
            item[...] = jnp.zeros_like(item)
        for p in range(3):
            part_copy(info[0], w_qkv, w_buf, sems, p).start()
        scale_grad[...] = scale_in[...]

    cosine, low, high = tables(base, inner, tile)

    def unit(g, c):
        cols = slice(g * GROUP, (g + 1) * GROUP)
        rows = slice(c * CHUNK, (c + 1) * CHUNK)
        fq, fk, vc, gn = fq_s[rows, cols], fk_s[rows, cols], v_s[rows, cols], gn_s[rows, cols]
        stack_q, stack_g = stack(stack_mask, fq), stack(stack_mask, gn)
        kept = state[g]
        held = kept.astype(BF)
        state[g] = kept + jnp.where(block_mask, mm(fq, gn, TN), 0.0)
        sums = mm(upper, gx_s[rows, cols]) + total[g]
        total[g] = sums[0:1, :]
        yield
        edge = jnp.where(causal, mm(vc, stack_g, NT), 0.0).astype(BF)
        yield
        weight = jnp.where(causal, mm(fk, stack_q, NT), 0.0).astype(BF)
        yield
        dfk = mm(edge, stack_q) + mm(vc, held, NT) + sums
        back = dfk * fk.astype(F32)
        back_low = back.astype(BF)
        scale_grad[:, cols] += jnp.sum(back, axis=0, keepdims=True)
        yield
        dvc = (mm(weight, stack_g) + mm(fk, held)).astype(BF)
        dv[rows, cols] = dvc
        bias_v[:, cols] += jnp.sum(dvc.astype(F32), axis=0, keepdims=True)
        yield
        dt = mm(back_low, mix_high[...], NT) + mm(back_low, mix_low[...], NT)
        dt = dt - mm(back_low, ones) * tk_s[rows, cols].astype(F32) * (HEAD ** (-0.5))
        yield
        out = turn(dt, cosine[rows], -low[rows], -high[rows]).astype(BF)
        dk[rows, cols] = out
        bias_k[:, cols] += jnp.sum(out.astype(F32), axis=0, keepdims=True)
        yield

    interleave([unit(g, c) for c in reversed(range(span)) for g in range(groups)], 1)

    @pl.when(step == tiles - 1)
    def _():
        sums_out[0:1, :] = bias_in[...]
        sums_out[1:2, :] = bias_k[...]
        sums_out[2:3, :] = bias_v[...]
        sums_out[3:4, :] = scale_grad[...] / scale[...]
        shift_out[...] = shift_in[...]
        for p in range(3):
            part_copy(info[0], w_qkv, w_buf, sems, p).wait()

        @pl.loop(0, 3 * groups)
        def _(j):
            row = sums_out[pl.ds(j // groups, 1), pl.ds(pl.multiple_of((j % groups) * GROUP, GROUP), GROUP)]
            shift_out[...] += exact_row(row, w_buf[:, pl.ds(pl.multiple_of(j * GROUP, GROUP), GROUP)])


def turn_tables():
    lane = np.arange(LANES) % HEAD
    freqs = np.where(lane < ROT, 10000.0 ** (-(lane % (ROT // 2)) / (ROT // 2)), 0.0)
    waves = lambda places: np.stack([np.cos(places[:, None] * freqs), np.sin(places[:, None] * freqs)], axis=1)
    fine = np.concatenate(
        [
            waves(np.arange(8)).transpose(1, 0, 2).reshape(16, LANES),
            np.broadcast_to(np.where(lane < ROT // 2, -1.0, 0.0), (8, LANES)),
            np.broadcast_to(np.where((lane >= ROT // 2) & (lane < ROT), 1.0, 0.0), (8, LANES)),
        ]
    )
    return waves(np.arange(LEN // 8) * 8.0).astype(np.float32), fine.astype(np.float32)


def prepare_kernel(*refs):
    *parts, points, basis, vectors, mix_high, mix_low = refs
    at = 0
    for part in parts:
        count = part.shape[0]
        vectors[:, at : at + count] = part[...].astype(F32).reshape(1, count)
        at += count
    table = jnp.dot(basis[...], points[...], precision=lax.Precision.HIGHEST, preferred_element_type=F32)
    wide = jnp.concatenate([table] * PACK, axis=1)
    _, block_mask = patterns()
    tall = jnp.where(block_mask, jnp.concatenate([wide] * PACK, axis=0), 0.0)
    mix_high[...], mix_low[...] = split(tall)


def prepare(parts, qmc_points):
    places = np.arange(HEAD)
    cosines = np.cos(np.pi * (places[:, None] + 0.5) * places[None, :] / HEAD)
    cosines = cosines * np.where(places == 0, math.sqrt(1.0 / HEAD), math.sqrt(2.0 / HEAD))[None, :]
    total = sum(item.shape[0] for item in parts)
    vectors, high, low = pl.pallas_call(
        prepare_kernel,
        out_shape=(
            jax.ShapeDtypeStruct((1, total), F32),
            jax.ShapeDtypeStruct((GROUP, GROUP), BF),
            jax.ShapeDtypeStruct((GROUP, GROUP), BF),
        ),
        compiler_params=params(),
        name="prepare",
    )(*parts, qmc_points, jnp.asarray(cosines * HEAD ** (-0.25), F32))
    return vectors, (high, low)


def stored(tile, info, own):
    return ((tile // own) ^ info[0]) * own + tile % own


def attention_front(info, normed, target, w_qkv, w_proj, vectors, mix, turns):
    total, dim = normed.shape
    half = dim // 2
    tiles = total // TILE
    front = lambda i, info: (stored(i, info, tiles // 2), 0)
    plain = lambda i, info: (i, 0)
    block = lambda k: pl.BlockSpec((dim, half), lambda i, info: (0, 2 * k + info[0]), pipeline_mode=pl.Buffered(1))
    groups = half // GROUP
    return pl.pallas_call(
        attn_front_kernel,
        out_shape=(
            *(jax.ShapeDtypeStruct((total, half), BF) for _ in range(8)),
            *(jax.ShapeDtypeStruct((1, half), F32) for _ in range(2)),
        ),
        grid_spec=pltpu.PrefetchScalarGridSpec(
            num_scalar_prefetch=1,
            grid=(tiles,),
            in_specs=[
                pl.BlockSpec((TILE, dim), front),
                pl.BlockSpec((TILE, dim), front),
                block(0),
                block(1),
                block(2),
                vector_spec(half, 5 * dim, 0),
                vector_spec(half, 6 * dim, 0),
                vector_spec(half, 7 * dim, 0),
                pl.BlockSpec((half, dim), lambda i, info: (info[0], 0), pipeline_mode=pl.Buffered(1)),
                vector_spec(half, 2 * dim, 0),
            ]
            + [whole(item.shape) for item in (*mix, *turns)],
            out_specs=[pl.BlockSpec((TILE, half), front)] * 2
            + [pl.BlockSpec((TILE, half), plain)] * 6
            + [whole((1, half))] * 2,
            scratch_shapes=[pltpu.VMEM((groups, GROUP, GROUP), F32), pltpu.VMEM((groups, 1, GROUP), F32)],
        ),
        compiler_params=params(),
        cost_estimate=cost(8 * total * dim * half + 64 * total * half * GROUP, 12 * total * dim, 2 * total * half),
        name="attention_front",
    )(info, normed, target, w_qkv, w_qkv, w_qkv, vectors, vectors, vectors, w_proj, vectors, *mix, *turns)


def attention_rear(info, saved, bias_q, scale_sum, w_qkv, vectors, shift, mix, turns):
    total, half = saved[0].shape
    dim = w_qkv.shape[0]
    tiles = total // TILE
    rear = lambda i, info: (stored(tiles - 1 - i, info, tiles // 2), 0)
    plain = lambda i, info: (tiles - 1 - i, 0)
    groups = half // GROUP
    return pl.pallas_call(
        partial(attn_rear_kernel, tiles),
        out_shape=(
            *(jax.ShapeDtypeStruct((total, half), BF) for _ in range(2)),
            jax.ShapeDtypeStruct((4, half), F32),
            jax.ShapeDtypeStruct((1, dim), F32),
        ),
        grid_spec=pltpu.PrefetchScalarGridSpec(
            num_scalar_prefetch=1,
            grid=(tiles,),
            in_specs=[pl.BlockSpec((TILE, half), plain)] * 6
            + [whole(item.shape) for item in (*mix, *turns, bias_q, scale_sum)]
            + [vector_spec(half, 2 * dim, 0), anywhere(), whole(shift.shape)],
            out_specs=[pl.BlockSpec((TILE, half), rear)] * 2 + [whole((4, half)), whole((1, dim))],
            scratch_shapes=[pltpu.VMEM((1, half), F32) for _ in range(3)]
            + [pltpu.VMEM((dim, 3 * half), BF), pltpu.SemaphoreType.DMA((3,))]
            + [pltpu.VMEM((groups, GROUP, GROUP), F32), pltpu.VMEM((groups, 1, GROUP), F32)],
        ),
        compiler_params=params(),
        cost_estimate=cost(48 * total * half * GROUP, 16 * total * half, 0),
        name="attention_rear",
    )(info, *saved, *mix, *turns, bias_q, scale_sum, vectors, w_qkv, shift)


def out_kernel(own, info, act, attended, w_proj, w_down, *rest):
    step = pl.program_id(0)
    if own:
        res, received, first, second, out, down_buf, sems = rest
    else:
        out, down_buf, sems = rest

    @pl.when(step == 0)
    def _():
        @pl.loop(0, down_buf.shape[0] // LANES)
        def _(j):
            strip_copy(info[0], w_down, down_buf, sems, 1, j).start()

        @pl.loop(0, down_buf.shape[0] // LANES)
        def _(j):
            strip_copy(info[0], w_down, down_buf, sems, 1, j).wait()

    value = mm(act[...], down_buf[...]) + mm(attended[...], w_proj[...])
    if own:
        value = value + received[...].astype(F32) + (first[...] + second[...]) + res[...].astype(F32)
    out[...] = value.astype(BF)


def out_rows(own, info, act, attended, w_proj, w_down, res=None, received=None, vectors=None):
    total, ff = act.shape
    dim = w_proj.shape[1]
    half = attended.shape[1]
    rows = total // 2
    tiles = rows // TILE
    shift = 0 if own else tiles
    shifted = lambda i, info: (i + shift, 0)
    plain = lambda i, info: (i, 0)
    extra, extra_specs = (), []
    if own:
        extra = (res, received, vectors, vectors)
        extra_specs = [pl.BlockSpec((TILE, dim), plain), pl.BlockSpec((TILE, dim), plain)]
        extra_specs += [vector_spec(dim, 3 * dim), vector_spec(dim, 4 * dim)]
    return pl.pallas_call(
        partial(out_kernel, own),
        out_shape=jax.ShapeDtypeStruct((rows, dim), BF),
        grid_spec=pltpu.PrefetchScalarGridSpec(
            num_scalar_prefetch=1,
            grid=(tiles,),
            in_specs=[
                pl.BlockSpec((TILE, ff), shifted),
                pl.BlockSpec((TILE, half), shifted),
                pl.BlockSpec((half, dim), lambda i, info: (info[0], 0), pipeline_mode=pl.Buffered(1)),
                anywhere(),
            ]
            + extra_specs,
            out_specs=pl.BlockSpec((TILE, dim), plain),
            scratch_shapes=[
                pltpu.VMEM((ff, dim), BF),
                pltpu.SemaphoreType.DMA((2, ff // LANES)),
            ],
        ),
        compiler_params=params(),
        cost_estimate=cost(2 * rows * dim * (ff + half), 2 * rows * (ff + half + dim) + 2 * dim * (ff + half)),
        name="out_rows",
    )(info, act, attended, w_proj, w_down, *extra)


def back_kernel(own, info, dq, dk, dv, up_grad, w_qkv, w_up, *rest):
    step = pl.program_id(0)
    if own:
        res, gain, target, received, out, w_buf, up_buf, part_sems, sems = rest
    else:
        out, w_buf, up_buf, part_sems, sems = rest
    grads = (dq, dk, dv)
    half = dq.shape[1]

    @pl.when(step == 0)
    def _():
        for p in range(3):
            part_copy(info[0], w_qkv, w_buf, part_sems, p).start()

        @pl.loop(0, up_buf.shape[1] // LANES)
        def _(j):
            strip_copy(info[0], w_up, up_buf, sems, 0, j).start()

        for p in range(3):
            part_copy(info[0], w_qkv, w_buf, part_sems, p).wait()

        @pl.loop(0, up_buf.shape[1] // LANES)
        def _(j):
            strip_copy(info[0], w_up, up_buf, sems, 0, j).wait()

    value = mm(up_grad[...], up_buf[...], NT)
    for p in range(3):
        value = value + mm(grads[p][...], w_buf[:, p * half : (p + 1) * half], NT)
    if own:
        xhat, rstd = norm_stats(res[...].astype(F32))
        scaled = (value + received[...].astype(F32)) * gain[...]
        middle = jnp.mean(scaled, axis=-1, keepdims=True)
        slope = jnp.mean(scaled * xhat, axis=-1, keepdims=True)
        out[...] = target[...].astype(F32) + rstd * (scaled - middle - xhat * slope)
    else:
        out[...] = value.astype(BF)


def back_rows(own, info, dq, dk, dv, up_grad, w_qkv, w_up, res=None, vectors=None, target=None, received=None):
    total, ff = up_grad.shape
    rows, dim = total // 2, w_qkv.shape[0]
    half = dq.shape[1]
    tiles = rows // TILE
    shift = 0 if own else tiles
    shifted = lambda i, info: (i + shift, 0)
    plain = lambda i, info: (i, 0)
    extra, extra_specs = (), []
    if own:
        extra = (res, vectors, target, received)
        extra_specs = [
            pl.BlockSpec((TILE, dim), plain),
            vector_spec(dim, 0),
            pl.BlockSpec((TILE, dim), plain),
            pl.BlockSpec((TILE, dim), plain),
        ]
    return pl.pallas_call(
        partial(back_kernel, own),
        out_shape=jax.ShapeDtypeStruct((rows, dim), F32 if own else BF),
        grid_spec=pltpu.PrefetchScalarGridSpec(
            num_scalar_prefetch=1,
            grid=(tiles,),
            in_specs=[pl.BlockSpec((TILE, half), shifted)] * 3
            + [pl.BlockSpec((TILE, ff), shifted), anywhere(), anywhere()]
            + extra_specs,
            out_specs=pl.BlockSpec((TILE, dim), plain),
            scratch_shapes=[
                pltpu.VMEM((dim, 3 * half), BF),
                pltpu.VMEM((dim, ff), BF),
                pltpu.SemaphoreType.DMA((3,)),
                pltpu.SemaphoreType.DMA((2, ff // LANES)),
            ],
        ),
        compiler_params=params(),
        cost_estimate=cost(2 * rows * dim * (ff + 3 * half), 2 * rows * (ff + 3 * half + 3 * dim) + 2 * dim * (ff + 3 * half)),
        name="back_rows",
    )(info, dq, dk, dv, up_grad, w_qkv, w_up, *extra)


def bit_orders(ndp):
    bits = [1 << j for j in range(ndp.bit_length() - 1)]
    return tuple(bits), tuple(bits[1::-1] + bits[2:])


def spots(me, ndp):
    apart = jnp.asarray(np.arange(ndp, dtype=np.int32)) ^ me
    rows = []
    for order in bit_orders(ndp):
        spot = jnp.zeros((ndp,), jnp.int32)
        for j, bit in enumerate(order):
            spot = spot + (((apart // bit) % 2) << (len(order) - 1 - j))
        rows.append(spot)
    return jnp.stack(rows)


def add(left, right, kind=BF):
    return (left.astype(F32) + right.astype(F32)).astype(kind)


def cross(value, bit, ndp):
    return lax.ppermute(value, "dp", [(i, i ^ bit) for i in range(ndp)])


class Reduction:
    def __init__(self, first, second, ndp):
        self.ndp = ndp
        self.orders = bit_orders(ndp)
        self.at = 0
        self.pairs = [first, second]
        self.fly()

    def fly(self):
        self.received = [
            cross(send, order[self.at], self.ndp) for (send, keep), order in zip(self.pairs, self.orders)
        ]

    def land(self, token=None):
        if token is not None:
            token, *self.received = lax.optimization_barrier((token, *self.received))
        self.step()
        return token

    def step(self):
        keeps = [keep for send, keep in self.pairs]
        self.at += 1
        steps = len(self.orders[0])
        if self.at == steps:
            parts = [add(k, r, F32)[0] for k, r in zip(keeps, self.received)]
            self.result = jnp.concatenate(parts, axis=0) if len(parts) > 1 else parts[0]
            return
        cut = keeps[0].shape[0] // 2
        pairs = [
            (add(k[cut:], r[cut:]), add(k[:cut], r[:cut])) for k, r in zip(keeps, self.received)
        ]
        if self.at == 2 and len(pairs) == 2:
            pairs = [tuple(jnp.concatenate(items, axis=1) for items in zip(*pairs))]
        self.pairs = pairs

    def hold(self, token):
        if self.at == len(self.orders[0]):
            token, self.result = lax.optimization_barrier((token, self.result))
        return token

    def finish(self):
        if 0 < self.at < len(self.orders[0]):
            self.fly()
        while self.at < len(self.orders[0]):
            self.land()
            if self.at < len(self.orders[0]):
                self.fly()
        return self.result

    def values(self):
        return [item for pair in self.pairs for item in pair]

    def after(self, token):
        if self.at < len(self.orders[0]):
            token, *items = lax.optimization_barrier((token, *self.values()))
            self.pairs = [(items[2 * j], items[2 * j + 1]) for j in range(len(items) // 2)]
            self.fly()
        else:
            token, self.result = lax.optimization_barrier((token, self.result))
        return token


def swap(value):
    return lax.ppermute(value, "stream", [(0, 1), (1, 0)])


def per_device(
    ndp, residual, cotangent, ln_gain, ln_bias, w_qkv, b_qkv, w_proj, b_proj, feature_scale,
    w_up, b_up, w_down, b_down, qmc_points, slot_lengths,
):
    own_rows, dim = residual.shape
    half = dim // 2
    ff = w_up.shape[1]
    side = lax.axis_index("stream")
    me = lax.axis_index("dp")
    info = jnp.stack([side, me, slot_lengths[0]]).astype(jnp.int32)
    table = spots(me, ndp)
    vectors, mix = prepare((ln_gain, ln_bias, feature_scale, b_proj, b_down, b_qkv, b_up), qmc_points)

    other_res = swap(residual)
    other_cot = swap(cotangent)
    *mine, target_sum = mlp_rows(0, info, residual, cotangent, vectors, w_up, w_down)
    normed, target, act, up_grad, upb, shift = mlp_rows(
        1, info, other_res, other_cot, vectors, w_up, w_down, mine
    )

    turns = tuple(jnp.asarray(item) for item in turn_tables())
    parts = mlp_weight_grads(ndp, table, act, target, normed, up_grad)
    mlp_sums = Reduction(parts[:2], parts[2:], ndp)

    attended, dq, *saved, bias_q, scale_sum = attention_front(
        info, normed, target, w_qkv, w_proj, vectors, mix, turns
    )
    attended = mlp_sums.land(attended)
    info = mlp_sums.after(info)
    dk, dv, sums, shift = attention_rear(info, saved, bias_q, scale_sum, w_qkv, vectors, shift, mix, turns)
    dk = mlp_sums.land(dk)
    table = mlp_sums.after(table)

    mine = lax.broadcasted_iota(jnp.int32, (1, 2, 1), 1) == side
    spread = lambda item: jnp.where(mine, item[:, None, :], 0.0)
    four = spread(sums)
    small = jnp.concatenate(
        [
            shift.reshape(ndp, -1),
            four[:3].reshape(ndp, -1),
            target_sum.reshape(ndp, -1),
            four[3].reshape(ndp, -1),
            spread(upb.reshape(-1, LANES)).reshape(ndp, -1),
        ],
        axis=1,
    )
    count = small.shape[1]
    extra = jnp.pad(small.astype(BF), ((0, 0), (0, 8 * half - count))).reshape(ndp, 8, half)
    parts = attn_weight_grads(ndp, table, normed, target, attended, dq, dk, dv, extra)
    attn_sums = Reduction(parts[:2], parts[2:], ndp)
    mlp_sums.land()
    info = mlp_sums.after(info)

    back_send = back_rows(False, info, dq, dk, dv, up_grad, w_qkv, w_up)
    back_send = attn_sums.land(back_send)
    info = attn_sums.after(info)
    back_received = swap(back_send)
    out_send = out_rows(False, info, act, attended, w_proj, w_down)
    out_send = attn_sums.land(mlp_sums.land(out_send))
    info = attn_sums.after(mlp_sums.after(info))
    out_received = swap(out_send)
    residual_grad = back_rows(
        True, info, dq, dk, dv, up_grad, w_qkv, w_up, residual, vectors, target, back_received
    )
    residual_grad = mlp_sums.hold(attn_sums.land(residual_grad))
    info = attn_sums.after(info)
    block_out = out_rows(True, info, act, attended, w_proj, w_down, residual, out_received, vectors)
    block_out = attn_sums.land(block_out)
    mlp_total, attn_total = mlp_sums.finish(), attn_sums.finish()

    blk = ff // (2 * ndp)
    size = dim // ndp
    small_size = size // 2
    down_rows = mlp_total[:blk]
    per = max(LANES // blk, 1)
    owners = [
        (v * 2 + s, (2 * (v // per) + s) * per + v % per) for v in range(ndp) for s in range(2)
    ]
    if any(a != b for a, b in owners):
        down_rows = lax.ppermute(down_rows, ("dp", "stream"), owners)

    def halves(blocks):
        blocks = blocks.reshape(blocks.shape[0], 2, small_size, blocks.shape[2])
        pick = lambda at: lax.dynamic_index_in_dim(blocks, at, 1, keepdims=False)
        return pick(side), pick(1 - side)

    def order(own, other):
        return jnp.where(side == 0, own, other), jnp.where(side == 0, other, own)

    keep, give = halves(mlp_total[blk:].reshape(2, size, -1))
    first, second = order(keep, swap(give))
    apart = lambda item: jnp.transpose(item, (1, 0, 2)).reshape(small_size, -1, 1, LANES)
    upw_grad = jnp.concatenate([apart(first), apart(second)], axis=2).reshape(small_size, ff)

    keep, give = halves(attn_total[: 3 * size].reshape(3, size, half))
    rest = attn_total[4 * size :]
    received = swap(jnp.concatenate([give.reshape(3 * small_size, half), rest], axis=0))
    first, second = order(keep, received[: 3 * small_size].reshape(3, small_size, half))
    qkvw_grad = jnp.concatenate([item[p] for p in range(3) for item in (first, second)], axis=1)
    proj_rows = jnp.concatenate(
        [attn_total[3 * size + p * small_size : 3 * size + (p + 1) * small_size] for p in range(2)], axis=1
    )
    proj_owners = [(v * 2 + s, ndp * s + v) for v in range(ndp) for s in range(2)]
    projw_grad = lax.ppermute(proj_rows, ("dp", "stream"), proj_owners)

    flat = (rest + received[3 * small_size :]).reshape(-1)
    ends = np.cumsum([0, size, 3 * size, size, size, 2 * blk])
    pieces = [
        lax.dynamic_index_in_dim(flat[a:b].reshape(2, -1), side, 0, keepdims=False)
        for a, b in zip(ends[:-1], ends[1:])
    ]
    shift_grad, qkvb_grad, projb_grad, scale_grad, upb_grad = pieces
    mine_at = (2 * me + side) * small_size
    near = lambda item: lax.dynamic_slice_in_dim(item, mine_at, small_size).astype(F32)
    along = jnp.sum(near(w_qkv) * qkvw_grad, axis=1) + jnp.sum(near(w_up) * upw_grad, axis=1)
    gain_grad = (along - near(ln_bias) * shift_grad) / near(ln_gain)

    return (
        block_out, residual_grad, gain_grad, shift_grad, qkvw_grad, qkvb_grad, projw_grad,
        projb_grad, scale_grad, upw_grad, upb_grad, down_rows, projb_grad,
    )


def solution(mesh):
    rows = P(("dp", "stream"), None)
    items = P(("dp", "stream"))
    return jax.shard_map(
        partial(per_device, mesh.shape["dp"]),
        mesh=mesh,
        in_specs=(rows, rows) + (P(),) * 12 + (P("dp"),),
        out_specs=(rows, rows, items, items, rows, items, rows, items, items, rows, items, rows, items),
        check_vma=False,
    )
```

```python
from functools import partial
import math

import jax
import jax.numpy as jnp
import numpy as np
from jax import lax
from jax.experimental import pallas as pl
from jax.experimental.pallas import tpu as pltpu
from jax.sharding import PartitionSpec as P

HEAD = 64
ROT = 16
LEN = 2048
EPSILON = 1e-05

BF = jnp.bfloat16
F32 = jnp.float32
TILE = 256
CHUNK = 128
GROUP = 256
PACK = GROUP // HEAD
LANES = 128
ERFC = tuple(
    item * math.sqrt(0.5 * math.pi)
    for item in (0.254829592, -0.284496736, 1.421413741, -1.453152027, 1.061405429)
)
VMEM_CAP = 55 * 1024 * 1024

NN = (((1,), (0,)), ((), ()))
NT = (((1,), (1,)), ((), ()))
TN = (((0,), (0,)), ((), ()))


def mm(left, right, dims=NN):
    return lax.dot_general(left, right, dims, preferred_element_type=F32)


def split(value):
    high = value.astype(BF)
    return high, (value - high.astype(F32)).astype(BF)


def whole(shape):
    rank = len(shape)
    return pl.BlockSpec(shape, lambda *_: (0,) * rank, pipeline_mode=pl.Buffered(1))


def anywhere():
    return pl.BlockSpec(memory_space=pl.ANY)


def params(limit=VMEM_CAP):
    return pltpu.CompilerParams(vmem_limit_bytes=limit)


def vector_spec(width, at, side=None):
    return pl.BlockSpec(
        (1, width),
        lambda i, info: (0, at // width + (0 if side is None else info[0])),
        pipeline_mode=pl.Buffered(1),
    )


def cost(flops, moved, trans=0):
    return pl.CostEstimate(flops=int(0.4 * flops), bytes_accessed=int(0.4 * moved), transcendentals=int(0.4 * trans))


def exact_row(row, weights):
    high, low = split(jnp.broadcast_to(row, (8, row.shape[1])))
    both = mm(jnp.concatenate([high, low], axis=0), weights, NT)
    return both[0:1] + both[8:9]


def norm_stats(rows):
    mean = jnp.mean(rows, axis=-1, keepdims=True)
    centred = rows - mean
    rstd = lax.rsqrt(jnp.mean(centred * centred, axis=-1, keepdims=True) + EPSILON)
    return centred * rstd, rstd


def strip_copy(side, source, buf, sems, kind, j):
    there = pl.ds(pl.multiple_of((2 * j + side) * LANES, LANES), LANES)
    here = pl.ds(pl.multiple_of(j * LANES, LANES), LANES)
    if kind == 0:
        return pltpu.make_async_copy(source.at[:, there], buf.at[:, here], sems.at[kind, j])
    return pltpu.make_async_copy(source.at[there, :], buf.at[here, :], sems.at[kind, j])


def part_copy(side, source, buf, sems, p):
    width = buf.shape[1] // 3
    there = pl.ds(pl.multiple_of((2 * p + side) * width, LANES), width)
    return pltpu.make_async_copy(source.at[:, there], buf.at[:, p * width : (p + 1) * width], sems.at[p])


def mlp_kernel(half, tiles, info, res, cot, gain, bias, b_up, w_up, w_down, *rest):
    normed, target, act, up_grad, upb, sums, up_buf, down_buf, sems = rest[-9:]
    step = pl.program_id(0)
    side = info[0]

    @pl.when(step == 0)
    def _():
        @pl.loop(0, up_buf.shape[1] // LANES)
        def _(j):
            strip_copy(side, w_up, up_buf, sems, 0, j).start()
            strip_copy(side, w_down, down_buf, sems, 1, j).start()

        if half == 0:
            upb[...] = jnp.zeros_like(upb)
            sums[...] = jnp.zeros_like(sums)
        else:
            upb[...] = rest[4][...]

    rows = res.shape[0]
    xhat, _ = norm_stats(res[...].astype(F32))
    low = (xhat * gain[...] + bias[...]).astype(BF)
    normed[...] = low
    part = side if half == 0 else 1 - side
    place = (part * tiles + step) * rows + lax.broadcasted_iota(jnp.int32, (rows, 1), 0)
    tgt = jnp.where(place < info[2], cot[...], jnp.zeros_like(cot))
    target[...] = tgt
    ones = jnp.ones((8, rows), BF)
    if half == 0:
        sums[...] += mm(ones, tgt)[0:1]
    width = 1024
    strips = width // LANES

    @pl.loop(0, up_buf.shape[1] // width)
    def _(j):
        cols = pl.ds(pl.multiple_of(j * width, width), width)

        @pl.when(step == 0)
        def _():
            for b in range(strips):
                strip_copy(side, w_up, up_buf, sems, 0, j * strips + b).wait()
                strip_copy(side, w_down, down_buf, sems, 1, j * strips + b).wait()

        shift = jnp.concatenate(
            [
                b_up[:, pl.ds(pl.multiple_of((2 * (j * strips + b) + side) * LANES, LANES), LANES)]
                for b in range(strips)
            ],
            axis=1,
        )
        up = mm(low, up_buf[:, cols]) + shift
        back = mm(tgt, down_buf[cols, :], NT)
        bell = jnp.exp2(up * up * (-0.5 * math.log2(math.e)) - 0.5 * math.log2(2.0 * math.pi))
        t = 1.0 / (1.0 + (0.3275911 * math.sqrt(0.5)) * jnp.abs(up))
        poly = ERFC[4]
        for item in ERFC[3::-1]:
            poly = item + t * poly
        tail = (t * bell) * poly
        phi = jnp.where(up >= 0, 1.0 - tail, tail)
        act[:, cols] = (up * phi).astype(BF)
        grad = (back * (phi + up * bell)).astype(BF)
        up_grad[:, cols] = grad
        upb[:, cols] += mm(ones, grad)[0:1]

    if half == 1:

        @pl.when(step == tiles - 1)
        def _():
            sums[...] = jnp.zeros_like(sums)

            @pl.loop(0, upb.shape[1] // (2 * GROUP))
            def _(j):
                cols = pl.ds(pl.multiple_of(j * 2 * GROUP, GROUP), 2 * GROUP)
                sums[...] += exact_row(upb[:, cols], up_buf[:, cols])


def mlp_rows(half, info, res, cot, vectors, w_up, w_down, earlier=()):
    rows, dim = res.shape
    ff = w_up.shape[1] // 2
    tiles = rows // TILE
    total = 2 * rows
    shift = half * tiles
    row_map = lambda i, info: (i, 0)
    out_map = lambda i, info: (i + shift, 0)
    outs = (
        jax.ShapeDtypeStruct((total, dim), BF),
        jax.ShapeDtypeStruct((total, dim), BF),
        jax.ShapeDtypeStruct((total, ff), BF),
        jax.ShapeDtypeStruct((total, ff), BF),
        jax.ShapeDtypeStruct((1, ff), F32),
        jax.ShapeDtypeStruct((1, dim), F32),
    )
    return pl.pallas_call(
        partial(mlp_kernel, half, tiles),
        out_shape=outs,
        grid_spec=pltpu.PrefetchScalarGridSpec(
            num_scalar_prefetch=1,
            grid=(tiles,),
            in_specs=[
                pl.BlockSpec((TILE, dim), row_map),
                pl.BlockSpec((TILE, dim), row_map),
                vector_spec(dim, 0),
                vector_spec(dim, dim),
                vector_spec(2 * ff, 8 * dim),
                anywhere(),
                anywhere(),
            ]
            + [anywhere()] * (len(earlier) - 1)
            + [whole((1, ff))] * min(len(earlier), 1),
            out_specs=[
                pl.BlockSpec((TILE, dim), out_map),
                pl.BlockSpec((TILE, dim), out_map),
                pl.BlockSpec((TILE, ff), out_map),
                pl.BlockSpec((TILE, ff), out_map),
                whole((1, ff)),
                whole((1, dim)),
            ],
            scratch_shapes=[
                pltpu.VMEM((dim, ff), BF),
                pltpu.VMEM((ff, dim), BF),
                pltpu.SemaphoreType.DMA((2, ff // LANES)),
            ],
        ),
        input_output_aliases={8 + j: j for j in range(len(earlier) - 1)},
        compiler_params=params(63 * 1024 * 1024),
        cost_estimate=cost(4 * rows * dim * ff, 12 * rows * dim + 16 * rows * ff, 2 * rows * ff),
        name="mlp_rows",
    )(info, res, cot, vectors, vectors, vectors, w_up, w_down, *earlier)


def ship(table, which, buf, send, keep, sems, first, count):
    half = send.shape[0]
    for b in range(count):
        spot = table[which, first + b]

        @pl.when(spot >= half)
        def _():
            pltpu.make_async_copy(buf.at[first + b], send.at[spot - half], sems.at[first + b]).start()

        @pl.when(spot < half)
        def _():
            pltpu.make_async_copy(buf.at[first + b], keep.at[spot], sems.at[first + b]).start()


def shipped(buf, keep, sems):
    for b in range(buf.shape[0]):
        pltpu.make_async_copy(buf.at[b], keep.at[0], sems.at[b]).wait()


def mlp_grad_kernel(
    tiles, table, act, target, normed, up_grad, send_a, keep_a, send_b, keep_b,
    grads, buf_a, buf_b, sems_a, sems_b, sem,
):
    step = pl.program_id(0)

    @pl.when(step == 0)
    def _():
        pltpu.make_async_copy(up_grad, grads, sem).start()

    @pl.when(step < tiles)
    def _():
        value = mm(act[...], target[...], TN).astype(BF)
        size = buf_a.shape[1]
        count = value.shape[0] // size
        first = step * count
        for b in range(count):
            buf_a[first + b] = value[b * size : (b + 1) * size, :]
        ship(table, 0, buf_a, send_a, keep_a, sems_a, first, count)

    @pl.when(step == tiles)
    def _():
        pltpu.make_async_copy(up_grad, grads, sem).wait()

    @pl.when(step >= tiles)
    def _():
        value = mm(normed[...], grads[...], TN).astype(BF)
        size = buf_b.shape[1] // 2
        width = buf_b.shape[2]
        count = value.shape[0] // size
        first = (step - tiles) * count
        for b in range(count):
            for p in range(2):
                buf_b[first + b, p * size : (p + 1) * size, :] = value[
                    b * size : (b + 1) * size, p * width : (p + 1) * width
                ]
        ship(table, 1, buf_b, send_b, keep_b, sems_b, first, count)

    @pl.when(step == pl.num_programs(0) - 1)
    def _():
        shipped(buf_a, keep_a, sems_a)
        shipped(buf_b, keep_b, sems_b)


def mlp_weight_grads(ndp, table, act, target, normed, up_grad):
    total, dim = normed.shape
    ff = act.shape[1]
    rows = ff // ndp
    shape = jax.ShapeDtypeStruct((ndp // 2, rows, dim), BF)
    wide, narrow = 512, 256
    tiles = ff // wide
    return pl.pallas_call(
        partial(mlp_grad_kernel, tiles),
        out_shape=(shape,) * 4,
        grid_spec=pltpu.PrefetchScalarGridSpec(
            num_scalar_prefetch=1,
            grid=(tiles + dim // narrow,),
            in_specs=[
                pl.BlockSpec((total, wide), lambda i, t: (0, jnp.minimum(i, tiles - 1))),
                whole((total, dim)),
                pl.BlockSpec((total, narrow), lambda i, t: (0, jnp.maximum(i - tiles, 0))),
                anywhere(),
            ],
            out_specs=[anywhere()] * 4,
            scratch_shapes=[pltpu.VMEM((total, ff), BF)]
            + [pltpu.VMEM((ndp, rows, dim), BF)] * 2
            + [pltpu.SemaphoreType.DMA((ndp,))] * 2
            + [pltpu.SemaphoreType.DMA],
        ),
        compiler_params=params(),
        cost_estimate=cost(4 * total * dim * ff, 4 * total * (dim + ff) + 4 * dim * ff),
        name="mlp_weight_grads",
    )(table, act, target, normed, up_grad)


def attn_grad_kernel(
    table, normed, attended, target, dq, dk, dv, extra, send_a, keep_a, send_b, keep_b, buf_a, buf_b, sems_a, sems_b
):
    step = pl.program_id(0)
    ndp = buf_a.shape[0]
    size = buf_a.shape[1] // 2
    small = size // 2
    half = dq.shape[1]

    @pl.when(step == 0)
    def _():
        value = mm(attended[...], target[...], TN).astype(BF)
        for b in range(ndp):
            for p in range(2):
                at = size + p * small
                buf_b[b, at : at + small, :] = value[b * small : (b + 1) * small, p * half : (p + 1) * half]
            buf_b[b, 2 * size :, :] = extra[b]

    count = normed.shape[1] // size
    first = step * count
    for item, buf, at in ((dq, buf_a, 0), (dk, buf_a, size), (dv, buf_b, 0)):
        value = mm(normed[...], item[...], TN).astype(BF)
        for b in range(count):
            buf[first + b, at : at + size, :] = value[b * size : (b + 1) * size, :]
    ship(table, 0, buf_a, send_a, keep_a, sems_a, first, count)
    ship(table, 1, buf_b, send_b, keep_b, sems_b, first, count)

    @pl.when(step == pl.num_programs(0) - 1)
    def _():
        shipped(buf_a, keep_a, sems_a)
        shipped(buf_b, keep_b, sems_b)


def attn_weight_grads(ndp, table, normed, target, attended, dq, dk, dv, extra):
    total, dim = normed.shape
    half = dq.shape[1]
    rows = 2 * dim // ndp
    more = extra.shape[1]
    shapes = [jax.ShapeDtypeStruct((ndp // 2, rows + j * more, half), BF) for j in range(2)]
    step = 256
    return pl.pallas_call(
        attn_grad_kernel,
        out_shape=(shapes[0], shapes[0], shapes[1], shapes[1]),
        grid_spec=pltpu.PrefetchScalarGridSpec(
            num_scalar_prefetch=1,
            grid=(dim // step,),
            in_specs=[
                pl.BlockSpec((total, step), lambda i, t: (0, i)),
                whole((total, half)),
                whole((total, dim)),
            ]
            + [whole((total, half))] * 3
            + [whole(extra.shape)],
            out_specs=[anywhere()] * 4,
            scratch_shapes=[pltpu.VMEM((ndp, rows + j * more, half), BF) for j in range(2)]
            + [pltpu.SemaphoreType.DMA((ndp,))] * 2,
        ),
        compiler_params=params(),
        cost_estimate=cost(8 * total * dim * half, 2 * total * (2 * dim + 4 * half) + 8 * dim * half),
        name="attn_weight_grads",
    )(table, normed, attended, target, dq, dk, dv, extra)


def turn(value, cosine, sine_low, sine_high):
    pieces = []
    for j in range(value.shape[1] // LANES):
        item = value[:, j * LANES : (j + 1) * LANES]
        pieces.append(
            item * cosine
            + pltpu.roll(item, LANES - ROT // 2, 1) * sine_low
            + pltpu.roll(item, ROT // 2, 1) * sine_high
        )
    return jnp.concatenate(pieces, axis=1)


def patterns():
    row_head = lax.broadcasted_iota(jnp.int32, (PACK * CHUNK, GROUP), 0) // CHUNK
    lane_head = lax.broadcasted_iota(jnp.int32, (PACK * CHUNK, GROUP), 1) // HEAD
    block_row = lax.broadcasted_iota(jnp.int32, (GROUP, GROUP), 0) // HEAD
    block_col = lax.broadcasted_iota(jnp.int32, (GROUP, GROUP), 1) // HEAD
    return row_head == lane_head, block_row == block_col


def interleave(items, lag):
    waiting = [(j * lag, item) for j, item in enumerate(items)]
    at = 0
    while waiting:
        alive = []
        for begin, item in waiting:
            if at < begin or next(item, waiting) is not waiting:
                alive.append((begin, item))
        waiting = alive
        at += 1


def stack(mask, item):
    return jnp.where(mask, jnp.concatenate([item] * PACK, axis=0), jnp.zeros((), BF))


def sum_heads(item, ones):
    high, low = split(item)
    return mm(high, ones) + mm(low, ones)


def tables(coarse, fine, tile):
    rows = TILE // 8
    co, so = [], []
    outer = coarse[pl.ds(tile * rows, rows)]
    ci, si = fine[0:8, :][None], fine[8:16, :][None]
    co, so = outer[:, 0:1, :], outer[:, 1:2, :]
    flat = lambda item: item.reshape(TILE, LANES)
    cosine = flat(co * ci - so * si)
    sine = so * ci + co * si
    return cosine, flat(sine * fine[16:24, :][None]), flat(sine * fine[24:32, :][None])


def attn_front_kernel(
    info, normed, target, w_q, w_k, w_v, b_q, b_k, b_v, w_proj, scale, mix_high, mix_low, base, inner,
    attended, dq, fq_s, fk_s, v_s, tk_s, gn_s, gx_s, bias_q, scale_grad, state, total,
):
    step = pl.program_id(0)
    groups = w_q.shape[1] // GROUP
    span = TILE // CHUNK
    stack_mask, block_mask = patterns()
    ones = jnp.where(block_mask, 1.0, 0.0).astype(BF)
    causal = lax.broadcasted_iota(jnp.int32, (CHUNK, PACK * CHUNK), 0) >= (
        lax.broadcasted_iota(jnp.int32, (CHUNK, PACK * CHUNK), 1) % CHUNK
    )
    lower = jnp.where(
        lax.broadcasted_iota(jnp.int32, (CHUNK, CHUNK), 0) >= lax.broadcasted_iota(jnp.int32, (CHUNK, CHUNK), 1),
        1.0,
        0.0,
    ).astype(BF)

    @pl.when(step == 0)
    def _():
        for item in (state, total, bias_q, scale_grad):
            item[...] = jnp.zeros_like(item)

    x = normed[...]
    cosine, low, high = tables(base, inner, step)
    grad_all = mm(target[...], w_proj[...], NT)
    feats, turned, values, held, before = {}, {}, {}, {}, {}

    def feature(g, which):
        cols = slice(g * GROUP, (g + 1) * GROUP)
        w, b, out = ((w_q, b_q, fq_s), (w_k, b_k, fk_s))[which]
        t = mm(x, w[:, cols]) + b[:, cols]
        yield
        t = turn(t, cosine, low, high)
        turned[which, g] = t
        t_high, t_low = split(t)
        spread = mm(t_high, mix_high[...]) + mm(t_low, mix_high[...]) + mm(t_high, mix_low[...])
        yield
        square = sum_heads(t * t, ones)
        yield
        feats[which, g] = (scale[:, cols] * jnp.exp(spread - square * (0.5 * HEAD ** (-0.5)))).astype(BF)
        out[:, cols] = feats[which, g]
        if which == 1:
            tk_s[:, cols] = t.astype(BF)
            values[g] = (mm(x, w_v[:, cols]) + b_v[:, cols]).astype(BF)
            v_s[:, cols] = values[g]
        yield

    def unit(g, c):
        cols = slice(g * GROUP, (g + 1) * GROUP)
        rows = slice(c * CHUNK, (c + 1) * CHUNK)
        fq, fk, vc = feats[0, g][rows], feats[1, g][rows], values[g][rows]
        stack_k, stack_v = stack(stack_mask, fk), stack(stack_mask, vc)
        kept = state[g]
        held = kept.astype(BF)
        state[g] = kept + jnp.where(block_mask, mm(fk, vc, TN), 0.0)
        keys = mm(lower, fk) + total[g]
        total[g] = keys[CHUNK - 1 : CHUNK, :]
        yield
        weight = jnp.where(causal, mm(fq, stack_k, NT), 0.0).astype(BF)
        wide = fq.astype(F32)
        den = sum_heads(wide * keys, ones)
        yield
        num = mm(weight, stack_v) + mm(fq, held)
        inverse = 1.0 / den
        yield
        mixed = num * inverse
        attended[rows, cols] = mixed.astype(BF)
        gn = (grad_all[rows, cols] * inverse).astype(BF)
        gn_s[rows, cols] = gn
        edge = jnp.where(causal, mm(gn, stack_v, NT), 0.0).astype(BF)
        yield
        grad_den = -sum_heads(gn.astype(F32) * mixed, ones)
        gx_s[rows, cols] = (grad_den * wide).astype(BF)
        yield
        dfq = mm(edge, stack_k) + mm(gn, held, NT) + grad_den * keys
        back = dfq * wide
        back_low = back.astype(BF)
        scale_grad[:, cols] += jnp.sum(back, axis=0, keepdims=True)
        yield
        dt = mm(back_low, mix_high[...], NT) + mm(back_low, mix_low[...], NT)
        dt = dt - mm(back_low, ones) * turned[0, g][rows] * (HEAD ** (-0.5))
        yield
        out = turn(dt, cosine[rows], -low[rows], -high[rows]).astype(BF)
        dq[rows, cols] = out
        bias_q[:, cols] += jnp.sum(out.astype(F32), axis=0, keepdims=True)
        yield

    interleave([feature(g, which) for g in range(groups) for which in range(2)], 0)
    interleave([unit(g, c) for c in range(span) for g in range(groups)], 0)


def attn_rear_kernel(
    tiles, info, fq_s, fk_s, v_s, tk_s, gn_s, gx_s, mix_high, mix_low, base, inner, bias_in, scale_in, scale,
    w_qkv, shift_in, dk, dv, sums_out, shift_out, bias_k, bias_v, scale_grad, w_buf, sems, state, total,
):
    step = pl.program_id(0)
    tile = tiles - 1 - step
    groups = dk.shape[1] // GROUP
    span = TILE // CHUNK
    stack_mask, block_mask = patterns()
    ones = jnp.where(block_mask, 1.0, 0.0).astype(BF)
    causal = lax.broadcasted_iota(jnp.int32, (CHUNK, PACK * CHUNK), 1) % CHUNK >= (
        lax.broadcasted_iota(jnp.int32, (CHUNK, PACK * CHUNK), 0)
    )
    upper = jnp.where(
        lax.broadcasted_iota(jnp.int32, (CHUNK, CHUNK), 1) >= lax.broadcasted_iota(jnp.int32, (CHUNK, CHUNK), 0),
        1.0,
        0.0,
    ).astype(BF)

    @pl.when(step == 0)
    def _():
        for item in (state, total, bias_k, bias_v):
            item[...] = jnp.zeros_like(item)
        for p in range(3):
            part_copy(info[0], w_qkv, w_buf, sems, p).start()
        scale_grad[...] = scale_in[...]

    cosine, low, high = tables(base, inner, tile)

    def unit(g, c):
        cols = slice(g * GROUP, (g + 1) * GROUP)
        rows = slice(c * CHUNK, (c + 1) * CHUNK)
        fq, fk, vc, gn = fq_s[rows, cols], fk_s[rows, cols], v_s[rows, cols], gn_s[rows, cols]
        stack_q, stack_g = stack(stack_mask, fq), stack(stack_mask, gn)
        kept = state[g]
        held = kept.astype(BF)
        state[g] = kept + jnp.where(block_mask, mm(fq, gn, TN), 0.0)
        sums = mm(upper, gx_s[rows, cols]) + total[g]
        total[g] = sums[0:1, :]
        yield
        edge = jnp.where(causal, mm(vc, stack_g, NT), 0.0).astype(BF)
        yield
        weight = jnp.where(causal, mm(fk, stack_q, NT), 0.0).astype(BF)
        yield
        dfk = mm(edge, stack_q) + mm(vc, held, NT) + sums
        back = dfk * fk.astype(F32)
        back_low = back.astype(BF)
        scale_grad[:, cols] += jnp.sum(back, axis=0, keepdims=True)
        yield
        dvc = (mm(weight, stack_g) + mm(fk, held)).astype(BF)
        dv[rows, cols] = dvc
        bias_v[:, cols] += jnp.sum(dvc.astype(F32), axis=0, keepdims=True)
        yield
        dt = mm(back_low, mix_high[...], NT) + mm(back_low, mix_low[...], NT)
        dt = dt - mm(back_low, ones) * tk_s[rows, cols].astype(F32) * (HEAD ** (-0.5))
        yield
        out = turn(dt, cosine[rows], -low[rows], -high[rows]).astype(BF)
        dk[rows, cols] = out
        bias_k[:, cols] += jnp.sum(out.astype(F32), axis=0, keepdims=True)
        yield

    interleave([unit(g, c) for c in reversed(range(span)) for g in range(groups)], 1)

    @pl.when(step == tiles - 1)
    def _():
        sums_out[0:1, :] = bias_in[...]
        sums_out[1:2, :] = bias_k[...]
        sums_out[2:3, :] = bias_v[...]
        sums_out[3:4, :] = scale_grad[...] / scale[...]
        shift_out[...] = shift_in[...]
        for p in range(3):
            part_copy(info[0], w_qkv, w_buf, sems, p).wait()

        @pl.loop(0, 3 * groups)
        def _(j):
            row = sums_out[pl.ds(j // groups, 1), pl.ds(pl.multiple_of((j % groups) * GROUP, GROUP), GROUP)]
            shift_out[...] += exact_row(row, w_buf[:, pl.ds(pl.multiple_of(j * GROUP, GROUP), GROUP)])


def turn_tables():
    lane = np.arange(LANES) % HEAD
    freqs = np.where(lane < ROT, 10000.0 ** (-(lane % (ROT // 2)) / (ROT // 2)), 0.0)
    waves = lambda places: np.stack([np.cos(places[:, None] * freqs), np.sin(places[:, None] * freqs)], axis=1)
    fine = np.concatenate(
        [
            waves(np.arange(8)).transpose(1, 0, 2).reshape(16, LANES),
            np.broadcast_to(np.where(lane < ROT // 2, -1.0, 0.0), (8, LANES)),
            np.broadcast_to(np.where((lane >= ROT // 2) & (lane < ROT), 1.0, 0.0), (8, LANES)),
        ]
    )
    return waves(np.arange(LEN // 8) * 8.0).astype(np.float32), fine.astype(np.float32)


def prepare_kernel(*refs):
    *parts, points, basis, vectors, mix_high, mix_low = refs
    at = 0
    for part in parts:
        count = part.shape[0]
        vectors[:, at : at + count] = part[...].astype(F32).reshape(1, count)
        at += count
    table = jnp.dot(basis[...], points[...], precision=lax.Precision.HIGHEST, preferred_element_type=F32)
    wide = jnp.concatenate([table] * PACK, axis=1)
    _, block_mask = patterns()
    tall = jnp.where(block_mask, jnp.concatenate([wide] * PACK, axis=0), 0.0)
    mix_high[...], mix_low[...] = split(tall)


def prepare(parts, qmc_points):
    places = np.arange(HEAD)
    cosines = np.cos(np.pi * (places[:, None] + 0.5) * places[None, :] / HEAD)
    cosines = cosines * np.where(places == 0, math.sqrt(1.0 / HEAD), math.sqrt(2.0 / HEAD))[None, :]
    total = sum(item.shape[0] for item in parts)
    vectors, high, low = pl.pallas_call(
        prepare_kernel,
        out_shape=(
            jax.ShapeDtypeStruct((1, total), F32),
            jax.ShapeDtypeStruct((GROUP, GROUP), BF),
            jax.ShapeDtypeStruct((GROUP, GROUP), BF),
        ),
        compiler_params=params(),
        name="prepare",
    )(*parts, qmc_points, jnp.asarray(cosines * HEAD ** (-0.25), F32))
    return vectors, (high, low)


def stored(tile, info, own):
    return ((tile // own) ^ info[0]) * own + tile % own


def attention_front(info, normed, target, w_qkv, w_proj, vectors, mix, turns):
    total, dim = normed.shape
    half = dim // 2
    tiles = total // TILE
    front = lambda i, info: (stored(i, info, tiles // 2), 0)
    plain = lambda i, info: (i, 0)
    block = lambda k: pl.BlockSpec((dim, half), lambda i, info: (0, 2 * k + info[0]), pipeline_mode=pl.Buffered(1))
    groups = half // GROUP
    return pl.pallas_call(
        attn_front_kernel,
        out_shape=(
            *(jax.ShapeDtypeStruct((total, half), BF) for _ in range(8)),
            *(jax.ShapeDtypeStruct((1, half), F32) for _ in range(2)),
        ),
        grid_spec=pltpu.PrefetchScalarGridSpec(
            num_scalar_prefetch=1,
            grid=(tiles,),
            in_specs=[
                pl.BlockSpec((TILE, dim), front),
                pl.BlockSpec((TILE, dim), front),
                block(0),
                block(1),
                block(2),
                vector_spec(half, 5 * dim, 0),
                vector_spec(half, 6 * dim, 0),
                vector_spec(half, 7 * dim, 0),
                pl.BlockSpec((half, dim), lambda i, info: (info[0], 0), pipeline_mode=pl.Buffered(1)),
                vector_spec(half, 2 * dim, 0),
            ]
            + [whole(item.shape) for item in (*mix, *turns)],
            out_specs=[pl.BlockSpec((TILE, half), front)] * 2
            + [pl.BlockSpec((TILE, half), plain)] * 6
            + [whole((1, half))] * 2,
            scratch_shapes=[pltpu.VMEM((groups, GROUP, GROUP), F32), pltpu.VMEM((groups, 1, GROUP), F32)],
        ),
        compiler_params=params(),
        cost_estimate=cost(8 * total * dim * half + 64 * total * half * GROUP, 12 * total * dim, 2 * total * half),
        name="attention_front",
    )(info, normed, target, w_qkv, w_qkv, w_qkv, vectors, vectors, vectors, w_proj, vectors, *mix, *turns)


def attention_rear(info, saved, bias_q, scale_sum, w_qkv, vectors, shift, mix, turns):
    total, half = saved[0].shape
    dim = w_qkv.shape[0]
    tiles = total // TILE
    rear = lambda i, info: (stored(tiles - 1 - i, info, tiles // 2), 0)
    plain = lambda i, info: (tiles - 1 - i, 0)
    groups = half // GROUP
    return pl.pallas_call(
        partial(attn_rear_kernel, tiles),
        out_shape=(
            *(jax.ShapeDtypeStruct((total, half), BF) for _ in range(2)),
            jax.ShapeDtypeStruct((4, half), F32),
            jax.ShapeDtypeStruct((1, dim), F32),
        ),
        grid_spec=pltpu.PrefetchScalarGridSpec(
            num_scalar_prefetch=1,
            grid=(tiles,),
            in_specs=[pl.BlockSpec((TILE, half), plain)] * 6
            + [whole(item.shape) for item in (*mix, *turns, bias_q, scale_sum)]
            + [vector_spec(half, 2 * dim, 0), anywhere(), whole(shift.shape)],
            out_specs=[pl.BlockSpec((TILE, half), rear)] * 2 + [whole((4, half)), whole((1, dim))],
            scratch_shapes=[pltpu.VMEM((1, half), F32) for _ in range(3)]
            + [pltpu.VMEM((dim, 3 * half), BF), pltpu.SemaphoreType.DMA((3,))]
            + [pltpu.VMEM((groups, GROUP, GROUP), F32), pltpu.VMEM((groups, 1, GROUP), F32)],
        ),
        compiler_params=params(),
        cost_estimate=cost(48 * total * half * GROUP, 16 * total * half, 0),
        name="attention_rear",
    )(info, *saved, *mix, *turns, bias_q, scale_sum, vectors, w_qkv, shift)


def out_kernel(own, info, act, attended, w_proj, w_down, *rest):
    step = pl.program_id(0)
    if own:
        res, received, first, second, out, down_buf, sems = rest
    else:
        out, down_buf, sems = rest

    @pl.when(step == 0)
    def _():
        @pl.loop(0, down_buf.shape[0] // LANES)
        def _(j):
            strip_copy(info[0], w_down, down_buf, sems, 1, j).start()

        @pl.loop(0, down_buf.shape[0] // LANES)
        def _(j):
            strip_copy(info[0], w_down, down_buf, sems, 1, j).wait()

    value = mm(act[...], down_buf[...]) + mm(attended[...], w_proj[...])
    if own:
        value = value + received[...].astype(F32) + (first[...] + second[...]) + res[...].astype(F32)
    out[...] = value.astype(BF)


def out_rows(own, info, act, attended, w_proj, w_down, res=None, received=None, vectors=None):
    total, ff = act.shape
    dim = w_proj.shape[1]
    half = attended.shape[1]
    rows = total // 2
    tiles = rows // TILE
    shift = 0 if own else tiles
    shifted = lambda i, info: (i + shift, 0)
    plain = lambda i, info: (i, 0)
    extra, extra_specs = (), []
    if own:
        extra = (res, received, vectors, vectors)
        extra_specs = [pl.BlockSpec((TILE, dim), plain), pl.BlockSpec((TILE, dim), plain)]
        extra_specs += [vector_spec(dim, 3 * dim), vector_spec(dim, 4 * dim)]
    return pl.pallas_call(
        partial(out_kernel, own),
        out_shape=jax.ShapeDtypeStruct((rows, dim), BF),
        grid_spec=pltpu.PrefetchScalarGridSpec(
            num_scalar_prefetch=1,
            grid=(tiles,),
            in_specs=[
                pl.BlockSpec((TILE, ff), shifted),
                pl.BlockSpec((TILE, half), shifted),
                pl.BlockSpec((half, dim), lambda i, info: (info[0], 0), pipeline_mode=pl.Buffered(1)),
                anywhere(),
            ]
            + extra_specs,
            out_specs=pl.BlockSpec((TILE, dim), plain),
            scratch_shapes=[
                pltpu.VMEM((ff, dim), BF),
                pltpu.SemaphoreType.DMA((2, ff // LANES)),
            ],
        ),
        compiler_params=params(),
        cost_estimate=cost(2 * rows * dim * (ff + half), 2 * rows * (ff + half + dim) + 2 * dim * (ff + half)),
        name="out_rows",
    )(info, act, attended, w_proj, w_down, *extra)


def back_kernel(own, info, dq, dk, dv, up_grad, w_qkv, w_up, *rest):
    step = pl.program_id(0)
    if own:
        res, gain, target, received, out, w_buf, up_buf, part_sems, sems = rest
    else:
        out, w_buf, up_buf, part_sems, sems = rest
    grads = (dq, dk, dv)
    half = dq.shape[1]

    @pl.when(step == 0)
    def _():
        for p in range(3):
            part_copy(info[0], w_qkv, w_buf, part_sems, p).start()

        @pl.loop(0, up_buf.shape[1] // LANES)
        def _(j):
            strip_copy(info[0], w_up, up_buf, sems, 0, j).start()

        for p in range(3):
            part_copy(info[0], w_qkv, w_buf, part_sems, p).wait()

        @pl.loop(0, up_buf.shape[1] // LANES)
        def _(j):
            strip_copy(info[0], w_up, up_buf, sems, 0, j).wait()

    value = mm(up_grad[...], up_buf[...], NT)
    for p in range(3):
        value = value + mm(grads[p][...], w_buf[:, p * half : (p + 1) * half], NT)
    if own:
        xhat, rstd = norm_stats(res[...].astype(F32))
        scaled = (value + received[...].astype(F32)) * gain[...]
        middle = jnp.mean(scaled, axis=-1, keepdims=True)
        slope = jnp.mean(scaled * xhat, axis=-1, keepdims=True)
        out[...] = target[...].astype(F32) + rstd * (scaled - middle - xhat * slope)
    else:
        out[...] = value.astype(BF)


def back_rows(own, info, dq, dk, dv, up_grad, w_qkv, w_up, res=None, vectors=None, target=None, received=None):
    total, ff = up_grad.shape
    rows, dim = total // 2, w_qkv.shape[0]
    half = dq.shape[1]
    tiles = rows // TILE
    shift = 0 if own else tiles
    shifted = lambda i, info: (i + shift, 0)
    plain = lambda i, info: (i, 0)
    extra, extra_specs = (), []
    if own:
        extra = (res, vectors, target, received)
        extra_specs = [
            pl.BlockSpec((TILE, dim), plain),
            vector_spec(dim, 0),
            pl.BlockSpec((TILE, dim), plain),
            pl.BlockSpec((TILE, dim), plain),
        ]
    return pl.pallas_call(
        partial(back_kernel, own),
        out_shape=jax.ShapeDtypeStruct((rows, dim), F32 if own else BF),
        grid_spec=pltpu.PrefetchScalarGridSpec(
            num_scalar_prefetch=1,
            grid=(tiles,),
            in_specs=[pl.BlockSpec((TILE, half), shifted)] * 3
            + [pl.BlockSpec((TILE, ff), shifted), anywhere(), anywhere()]
            + extra_specs,
            out_specs=pl.BlockSpec((TILE, dim), plain),
            scratch_shapes=[
                pltpu.VMEM((dim, 3 * half), BF),
                pltpu.VMEM((dim, ff), BF),
                pltpu.SemaphoreType.DMA((3,)),
                pltpu.SemaphoreType.DMA((2, ff // LANES)),
            ],
        ),
        compiler_params=params(),
        cost_estimate=cost(2 * rows * dim * (ff + 3 * half), 2 * rows * (ff + 3 * half + 3 * dim) + 2 * dim * (ff + 3 * half)),
        name="back_rows",
    )(info, dq, dk, dv, up_grad, w_qkv, w_up, *extra)


def bit_orders(ndp):
    bits = [1 << j for j in range(ndp.bit_length() - 1)]
    return tuple(bits), tuple(bits[1::-1] + bits[2:])


def spots(me, ndp):
    apart = jnp.asarray(np.arange(ndp, dtype=np.int32)) ^ me
    rows = []
    for order in bit_orders(ndp):
        spot = jnp.zeros((ndp,), jnp.int32)
        for j, bit in enumerate(order):
            spot = spot + (((apart // bit) % 2) << (len(order) - 1 - j))
        rows.append(spot)
    return jnp.stack(rows)


def add(left, right, kind=BF):
    return (left.astype(F32) + right.astype(F32)).astype(kind)


def cross(value, bit, ndp):
    return lax.ppermute(value, "dp", [(i, i ^ bit) for i in range(ndp)])


class Reduction:
    def __init__(self, first, second, ndp):
        self.ndp = ndp
        self.orders = bit_orders(ndp)
        self.at = 0
        self.pairs = [first, second]
        self.fly()

    def fly(self):
        self.received = [
            cross(send, order[self.at], self.ndp) for (send, keep), order in zip(self.pairs, self.orders)
        ]

    def land(self, token=None):
        if token is not None:
            token, *self.received = lax.optimization_barrier((token, *self.received))
        self.step()
        return token

    def step(self):
        keeps = [keep for send, keep in self.pairs]
        self.at += 1
        steps = len(self.orders[0])
        if self.at == steps:
            parts = [add(k, r, F32)[0] for k, r in zip(keeps, self.received)]
            self.result = jnp.concatenate(parts, axis=0) if len(parts) > 1 else parts[0]
            return
        cut = keeps[0].shape[0] // 2
        pairs = [
            (add(k[cut:], r[cut:]), add(k[:cut], r[:cut])) for k, r in zip(keeps, self.received)
        ]
        if self.at == 2 and len(pairs) == 2:
            pairs = [tuple(jnp.concatenate(items, axis=1) for items in zip(*pairs))]
        self.pairs = pairs

    def hold(self, token):
        if self.at == len(self.orders[0]):
            token, self.result = lax.optimization_barrier((token, self.result))
        return token

    def finish(self):
        if 0 < self.at < len(self.orders[0]):
            self.fly()
        while self.at < len(self.orders[0]):
            self.land()
            if self.at < len(self.orders[0]):
                self.fly()
        return self.result

    def values(self):
        return [item for pair in self.pairs for item in pair]

    def after(self, token):
        if self.at < len(self.orders[0]):
            token, *items = lax.optimization_barrier((token, *self.values()))
            self.pairs = [(items[2 * j], items[2 * j + 1]) for j in range(len(items) // 2)]
            self.fly()
        else:
            token, self.result = lax.optimization_barrier((token, self.result))
        return token


def swap(value):
    return lax.ppermute(value, "stream", [(0, 1), (1, 0)])


def per_device(
    ndp, residual, cotangent, ln_gain, ln_bias, w_qkv, b_qkv, w_proj, b_proj, feature_scale,
    w_up, b_up, w_down, b_down, qmc_points, slot_lengths,
):
    own_rows, dim = residual.shape
    half = dim // 2
    ff = w_up.shape[1]
    side = lax.axis_index("stream")
    me = lax.axis_index("dp")
    info = jnp.stack([side, me, slot_lengths[0]]).astype(jnp.int32)
    table = spots(me, ndp)
    vectors, mix = prepare((ln_gain, ln_bias, feature_scale, b_proj, b_down, b_qkv, b_up), qmc_points)

    other_res = swap(residual)
    other_cot = swap(cotangent)
    *mine, target_sum = mlp_rows(0, info, residual, cotangent, vectors, w_up, w_down)
    normed, target, act, up_grad, upb, shift = mlp_rows(
        1, info, other_res, other_cot, vectors, w_up, w_down, mine
    )

    turns = tuple(jnp.asarray(item) for item in turn_tables())
    parts = mlp_weight_grads(ndp, table, act, target, normed, up_grad)
    mlp_sums = Reduction(parts[:2], parts[2:], ndp)

    attended, dq, *saved, bias_q, scale_sum = attention_front(
        info, normed, target, w_qkv, w_proj, vectors, mix, turns
    )
    attended = mlp_sums.land(attended)
    info = mlp_sums.after(info)
    dk, dv, sums, shift = attention_rear(info, saved, bias_q, scale_sum, w_qkv, vectors, shift, mix, turns)
    dk = mlp_sums.land(dk)
    table = mlp_sums.after(table)

    mine = lax.broadcasted_iota(jnp.int32, (1, 2, 1), 1) == side
    spread = lambda item: jnp.where(mine, item[:, None, :], 0.0)
    four = spread(sums)
    small = jnp.concatenate(
        [
            shift.reshape(ndp, -1),
            four[:3].reshape(ndp, -1),
            target_sum.reshape(ndp, -1),
            four[3].reshape(ndp, -1),
            spread(upb.reshape(-1, LANES)).reshape(ndp, -1),
        ],
        axis=1,
    )
    count = small.shape[1]
    extra = jnp.pad(small.astype(BF), ((0, 0), (0, 8 * half - count))).reshape(ndp, 8, half)
    parts = attn_weight_grads(ndp, table, normed, target, attended, dq, dk, dv, extra)
    attn_sums = Reduction(parts[:2], parts[2:], ndp)
    mlp_sums.land()
    info = mlp_sums.after(info)

    back_send = back_rows(False, info, dq, dk, dv, up_grad, w_qkv, w_up)
    back_send = attn_sums.land(back_send)
    info = attn_sums.after(info)
    back_received = swap(back_send)
    out_send = out_rows(False, info, act, attended, w_proj, w_down)
    out_send = attn_sums.land(mlp_sums.land(out_send))
    info = attn_sums.after(mlp_sums.after(info))
    out_received = swap(out_send)
    residual_grad = back_rows(
        True, info, dq, dk, dv, up_grad, w_qkv, w_up, residual, vectors, target, back_received
    )
    residual_grad = mlp_sums.hold(attn_sums.land(residual_grad))
    info = attn_sums.after(info)
    block_out = out_rows(True, info, act, attended, w_proj, w_down, residual, out_received, vectors)
    block_out = attn_sums.land(block_out)
    mlp_total, attn_total = mlp_sums.finish(), attn_sums.finish()

    blk = ff // (2 * ndp)
    size = dim // ndp
    small_size = size // 2
    down_rows = mlp_total[:blk]
    per = max(LANES // blk, 1)
    owners = [
        (v * 2 + s, (2 * (v // per) + s) * per + v % per) for v in range(ndp) for s in range(2)
    ]
    if any(a != b for a, b in owners):
        down_rows = lax.ppermute(down_rows, ("dp", "stream"), owners)

    def halves(blocks):
        blocks = blocks.reshape(blocks.shape[0], 2, small_size, blocks.shape[2])
        pick = lambda at: lax.dynamic_index_in_dim(blocks, at, 1, keepdims=False)
        return pick(side), pick(1 - side)

    def order(own, other):
        return jnp.where(side == 0, own, other), jnp.where(side == 0, other, own)

    keep, give = halves(mlp_total[blk:].reshape(2, size, -1))
    first, second = order(keep, swap(give))
    apart = lambda item: jnp.transpose(item, (1, 0, 2)).reshape(small_size, -1, 1, LANES)
    upw_grad = jnp.concatenate([apart(first), apart(second)], axis=2).reshape(small_size, ff)

    keep, give = halves(attn_total[: 3 * size].reshape(3, size, half))
    rest = attn_total[4 * size :]
    received = swap(jnp.concatenate([give.reshape(3 * small_size, half), rest], axis=0))
    first, second = order(keep, received[: 3 * small_size].reshape(3, small_size, half))
    qkvw_grad = jnp.concatenate([item[p] for p in range(3) for item in (first, second)], axis=1)
    proj_rows = jnp.concatenate(
        [attn_total[3 * size + p * small_size : 3 * size + (p + 1) * small_size] for p in range(2)], axis=1
    )
    proj_owners = [(v * 2 + s, ndp * s + v) for v in range(ndp) for s in range(2)]
    projw_grad = lax.ppermute(proj_rows, ("dp", "stream"), proj_owners)

    flat = (rest + received[3 * small_size :]).reshape(-1)
    ends = np.cumsum([0, size, 3 * size, size, size, 2 * blk])
    pieces = [
        lax.dynamic_index_in_dim(flat[a:b].reshape(2, -1), side, 0, keepdims=False)
        for a, b in zip(ends[:-1], ends[1:])
    ]
    shift_grad, qkvb_grad, projb_grad, scale_grad, upb_grad = pieces
    mine_at = (2 * me + side) * small_size
    near = lambda item: lax.dynamic_slice_in_dim(item, mine_at, small_size).astype(F32)
    along = jnp.sum(near(w_qkv) * qkvw_grad, axis=1) + jnp.sum(near(w_up) * upw_grad, axis=1)
    gain_grad = (along - near(ln_bias) * shift_grad) / near(ln_gain)

    return (
        block_out, residual_grad, gain_grad, shift_grad, qkvw_grad, qkvb_grad, projw_grad,
        projb_grad, scale_grad, upw_grad, upb_grad, down_rows, projb_grad,
    )


def solution(mesh):
    rows = P(("dp", "stream"), None)
    items = P(("dp", "stream"))
    return jax.shard_map(
        partial(per_device, mesh.shape["dp"]),
        mesh=mesh,
        in_specs=(rows, rows) + (P(),) * 12 + (P("dp"),),
        out_specs=(rows, rows, items, items, rows, items, rows, items, items, rows, items, rows, items),
        check_vma=False,
    )
```

```python
from functools import partial
import math

import jax
import jax.numpy as jnp
import numpy as np
from jax import lax
from jax.experimental import pallas as pl
from jax.experimental.pallas import tpu as pltpu
from jax.sharding import PartitionSpec as P

HEAD = 64
ROT = 16
LEN = 2048
EPSILON = 1e-05

BF = jnp.bfloat16
F32 = jnp.float32
TILE = 256
CHUNK = 128
GROUP = 256
PACK = GROUP // HEAD
LANES = 128
ERFC = tuple(
    item * math.sqrt(0.5 * math.pi)
    for item in (0.254829592, -0.284496736, 1.421413741, -1.453152027, 1.061405429)
)
VMEM_CAP = 55 * 1024 * 1024

NN = (((1,), (0,)), ((), ()))
NT = (((1,), (1,)), ((), ()))
TN = (((0,), (0,)), ((), ()))


def mm(left, right, dims=NN):
    return lax.dot_general(left, right, dims, preferred_element_type=F32)


def split(value):
    high = value.astype(BF)
    return high, (value - high.astype(F32)).astype(BF)


def whole(shape):
    rank = len(shape)
    return pl.BlockSpec(shape, lambda *_: (0,) * rank, pipeline_mode=pl.Buffered(1))


def anywhere():
    return pl.BlockSpec(memory_space=pl.ANY)


def params(limit=VMEM_CAP):
    return pltpu.CompilerParams(vmem_limit_bytes=limit)


def vector_spec(width, at, side=None):
    return pl.BlockSpec(
        (1, width),
        lambda i, info: (0, at // width + (0 if side is None else info[0])),
        pipeline_mode=pl.Buffered(1),
    )


def cost(flops, moved, trans=0):
    return pl.CostEstimate(flops=int(0.4 * flops), bytes_accessed=int(0.4 * moved), transcendentals=int(0.4 * trans))


def exact_row(row, weights):
    high, low = split(jnp.broadcast_to(row, (8, row.shape[1])))
    both = mm(jnp.concatenate([high, low], axis=0), weights, NT)
    return both[0:1] + both[8:9]


def norm_stats(rows):
    mean = jnp.mean(rows, axis=-1, keepdims=True)
    centred = rows - mean
    rstd = lax.rsqrt(jnp.mean(centred * centred, axis=-1, keepdims=True) + EPSILON)
    return centred * rstd, rstd


def strip_copy(side, source, buf, sems, kind, j):
    there = pl.ds(pl.multiple_of((2 * j + side) * LANES, LANES), LANES)
    here = pl.ds(pl.multiple_of(j * LANES, LANES), LANES)
    if kind == 0:
        return pltpu.make_async_copy(source.at[:, there], buf.at[:, here], sems.at[kind, j])
    return pltpu.make_async_copy(source.at[there, :], buf.at[here, :], sems.at[kind, j])


def part_copy(side, source, buf, sems, p):
    width = buf.shape[1] // 3
    there = pl.ds(pl.multiple_of((2 * p + side) * width, LANES), width)
    return pltpu.make_async_copy(source.at[:, there], buf.at[:, p * width : (p + 1) * width], sems.at[p])


def mlp_kernel(half, tiles, info, res, cot, gain, bias, b_up, w_up, w_down, *rest):
    normed, target, act, up_grad, upb, sums, up_buf, down_buf, sems = rest[-9:]
    step = pl.program_id(0)
    side = info[0]

    @pl.when(step == 0)
    def _():
        @pl.loop(0, up_buf.shape[1] // LANES)
        def _(j):
            strip_copy(side, w_up, up_buf, sems, 0, j).start()
            strip_copy(side, w_down, down_buf, sems, 1, j).start()

        if half == 0:
            upb[...] = jnp.zeros_like(upb)
            sums[...] = jnp.zeros_like(sums)
        else:
            upb[...] = rest[4][...]
            sums[...] = jnp.zeros_like(sums)

    rows = res.shape[0]
    xhat, _ = norm_stats(res[...].astype(F32))
    low = (xhat * gain[...] + bias[...]).astype(BF)
    normed[...] = low
    part = side if half == 0 else 1 - side
    place = (part * tiles + step) * rows + lax.broadcasted_iota(jnp.int32, (rows, 1), 0)
    tgt = jnp.where(place < info[2], cot[...], jnp.zeros_like(cot))
    target[...] = tgt
    ones = jnp.ones((8, rows), BF)
    if half == 0:
        sums[...] += mm(ones, tgt)[0:1]
    width = 1024
    strips = width // LANES

    @pl.loop(0, up_buf.shape[1] // width)
    def _(j):
        cols = pl.ds(pl.multiple_of(j * width, width), width)

        @pl.when(step == 0)
        def _():
            for b in range(strips):
                strip_copy(side, w_up, up_buf, sems, 0, j * strips + b).wait()
                strip_copy(side, w_down, down_buf, sems, 1, j * strips + b).wait()

        shift = jnp.concatenate(
            [
                b_up[:, pl.ds(pl.multiple_of((2 * (j * strips + b) + side) * LANES, LANES), LANES)]
                for b in range(strips)
            ],
            axis=1,
        )
        up = mm(low, up_buf[:, cols]) + shift
        back = mm(tgt, down_buf[cols, :], NT)
        bell = jnp.exp2(up * up * (-0.5 * math.log2(math.e)) - 0.5 * math.log2(2.0 * math.pi))
        t = 1.0 / (1.0 + (0.3275911 * math.sqrt(0.5)) * jnp.abs(up))
        poly = ERFC[4]
        for item in ERFC[3::-1]:
            poly = item + t * poly
        tail = (t * bell) * poly
        phi = jnp.where(up >= 0, 1.0 - tail, tail)
        act[:, cols] = (up * phi).astype(BF)
        grad = (back * (phi + up * bell)).astype(BF)
        up_grad[:, cols] = grad
        upb[:, cols] += mm(ones, grad)[0:1]


def mlp_rows(half, info, res, cot, vectors, w_up, w_down, earlier=()):
    rows, dim = res.shape
    ff = w_up.shape[1] // 2
    tiles = rows // TILE
    total = 2 * rows
    shift = half * tiles
    row_map = lambda i, info: (i, 0)
    out_map = lambda i, info: (i + shift, 0)
    outs = (
        jax.ShapeDtypeStruct((total, dim), BF),
        jax.ShapeDtypeStruct((total, dim), BF),
        jax.ShapeDtypeStruct((total, ff), BF),
        jax.ShapeDtypeStruct((total, ff), BF),
        jax.ShapeDtypeStruct((1, ff), F32),
        jax.ShapeDtypeStruct((1, dim), F32),
    )
    return pl.pallas_call(
        partial(mlp_kernel, half, tiles),
        out_shape=outs,
        grid_spec=pltpu.PrefetchScalarGridSpec(
            num_scalar_prefetch=1,
            grid=(tiles,),
            in_specs=[
                pl.BlockSpec((TILE, dim), row_map),
                pl.BlockSpec((TILE, dim), row_map),
                vector_spec(dim, 0),
                vector_spec(dim, dim),
                vector_spec(2 * ff, 8 * dim),
                anywhere(),
                anywhere(),
            ]
            + [anywhere()] * (len(earlier) - 1)
            + [whole((1, ff))] * min(len(earlier), 1),
            out_specs=[
                pl.BlockSpec((TILE, dim), out_map),
                pl.BlockSpec((TILE, dim), out_map),
                pl.BlockSpec((TILE, ff), out_map),
                pl.BlockSpec((TILE, ff), out_map),
                whole((1, ff)),
                whole((1, dim)),
            ],
            scratch_shapes=[
                pltpu.VMEM((dim, ff), BF),
                pltpu.VMEM((ff, dim), BF),
                pltpu.SemaphoreType.DMA((2, ff // LANES)),
            ],
        ),
        input_output_aliases={8 + j: j for j in range(len(earlier) - 1)},
        compiler_params=params(63 * 1024 * 1024),
        cost_estimate=cost(4 * rows * dim * ff, 12 * rows * dim + 16 * rows * ff, 2 * rows * ff),
        name="mlp_rows",
    )(info, res, cot, vectors, vectors, vectors, w_up, w_down, *earlier)


def ship(table, which, buf, send, keep, sems, first, count):
    half = send.shape[0]
    for b in range(count):
        spot = table[which, first + b]

        @pl.when(spot >= half)
        def _():
            pltpu.make_async_copy(buf.at[first + b], send.at[spot - half], sems.at[first + b]).start()

        @pl.when(spot < half)
        def _():
            pltpu.make_async_copy(buf.at[first + b], keep.at[spot], sems.at[first + b]).start()


def shipped(buf, keep, sems):
    for b in range(buf.shape[0]):
        pltpu.make_async_copy(buf.at[b], keep.at[0], sems.at[b]).wait()


def mlp_grad_kernel(
    tiles, table, act, target, normed, up_grad, send_a, keep_a, send_b, keep_b,
    grads, buf_a, buf_b, sems_a, sems_b, sem,
):
    step = pl.program_id(0)

    @pl.when(step == 0)
    def _():
        pltpu.make_async_copy(up_grad, grads, sem).start()

    @pl.when(step < tiles)
    def _():
        value = mm(act[...], target[...], TN).astype(BF)
        size = buf_a.shape[1]
        count = value.shape[0] // size
        first = step * count
        for b in range(count):
            buf_a[first + b] = value[b * size : (b + 1) * size, :]
        ship(table, 0, buf_a, send_a, keep_a, sems_a, first, count)

    @pl.when(step == tiles)
    def _():
        pltpu.make_async_copy(up_grad, grads, sem).wait()

    @pl.when(step >= tiles)
    def _():
        value = mm(normed[...], grads[...], TN).astype(BF)
        size = buf_b.shape[1] // 2
        width = buf_b.shape[2]
        count = value.shape[0] // size
        first = (step - tiles) * count
        for b in range(count):
            for p in range(2):
                buf_b[first + b, p * size : (p + 1) * size, :] = value[
                    b * size : (b + 1) * size, p * width : (p + 1) * width
                ]
        ship(table, 1, buf_b, send_b, keep_b, sems_b, first, count)

    @pl.when(step == pl.num_programs(0) - 1)
    def _():
        shipped(buf_a, keep_a, sems_a)
        shipped(buf_b, keep_b, sems_b)


def mlp_weight_grads(ndp, table, act, target, normed, up_grad):
    total, dim = normed.shape
    ff = act.shape[1]
    rows = ff // ndp
    shape = jax.ShapeDtypeStruct((ndp // 2, rows, dim), BF)
    wide, narrow = 512, 256
    tiles = ff // wide
    return pl.pallas_call(
        partial(mlp_grad_kernel, tiles),
        out_shape=(shape,) * 4,
        grid_spec=pltpu.PrefetchScalarGridSpec(
            num_scalar_prefetch=1,
            grid=(tiles + dim // narrow,),
            in_specs=[
                pl.BlockSpec((total, wide), lambda i, t: (0, jnp.minimum(i, tiles - 1))),
                whole((total, dim)),
                pl.BlockSpec((total, narrow), lambda i, t: (0, jnp.maximum(i - tiles, 0))),
                anywhere(),
            ],
            out_specs=[anywhere()] * 4,
            scratch_shapes=[pltpu.VMEM((total, ff), BF)]
            + [pltpu.VMEM((ndp, rows, dim), BF)] * 2
            + [pltpu.SemaphoreType.DMA((ndp,))] * 2
            + [pltpu.SemaphoreType.DMA],
        ),
        compiler_params=params(),
        cost_estimate=cost(4 * total * dim * ff, 4 * total * (dim + ff) + 4 * dim * ff),
        name="mlp_weight_grads",
    )(table, act, target, normed, up_grad)


def attn_grad_kernel(
    table, normed, attended, target, dq, dk, dv, extra, send_a, keep_a, send_b, keep_b, buf_a, buf_b, sems_a, sems_b
):
    step = pl.program_id(0)
    ndp = buf_a.shape[0]
    size = buf_a.shape[1] // 2
    small = size // 2
    half = dq.shape[1]

    @pl.when(step == 0)
    def _():
        value = mm(attended[...], target[...], TN).astype(BF)
        for b in range(ndp):
            for p in range(2):
                at = size + p * small
                buf_b[b, at : at + small, :] = value[b * small : (b + 1) * small, p * half : (p + 1) * half]
            buf_b[b, 2 * size :, :] = extra[b]

    count = normed.shape[1] // size
    first = step * count
    for item, buf, at in ((dq, buf_a, 0), (dk, buf_a, size), (dv, buf_b, 0)):
        value = mm(normed[...], item[...], TN).astype(BF)
        for b in range(count):
            buf[first + b, at : at + size, :] = value[b * size : (b + 1) * size, :]
    ship(table, 0, buf_a, send_a, keep_a, sems_a, first, count)
    ship(table, 1, buf_b, send_b, keep_b, sems_b, first, count)

    @pl.when(step == pl.num_programs(0) - 1)
    def _():
        shipped(buf_a, keep_a, sems_a)
        shipped(buf_b, keep_b, sems_b)


def attn_weight_grads(ndp, table, normed, target, attended, dq, dk, dv, extra):
    total, dim = normed.shape
    half = dq.shape[1]
    rows = 2 * dim // ndp
    more = extra.shape[1]
    shapes = [jax.ShapeDtypeStruct((ndp // 2, rows + j * more, half), BF) for j in range(2)]
    step = 256
    return pl.pallas_call(
        attn_grad_kernel,
        out_shape=(shapes[0], shapes[0], shapes[1], shapes[1]),
        grid_spec=pltpu.PrefetchScalarGridSpec(
            num_scalar_prefetch=1,
            grid=(dim // step,),
            in_specs=[
                pl.BlockSpec((total, step), lambda i, t: (0, i)),
                whole((total, half)),
                whole((total, dim)),
            ]
            + [whole((total, half))] * 3
            + [whole(extra.shape)],
            out_specs=[anywhere()] * 4,
            scratch_shapes=[pltpu.VMEM((ndp, rows + j * more, half), BF) for j in range(2)]
            + [pltpu.SemaphoreType.DMA((ndp,))] * 2,
        ),
        compiler_params=params(),
        cost_estimate=cost(8 * total * dim * half, 2 * total * (2 * dim + 4 * half) + 8 * dim * half),
        name="attn_weight_grads",
    )(table, normed, attended, target, dq, dk, dv, extra)


def turn(value, cosine, sine_low, sine_high):
    pieces = []
    for j in range(value.shape[1] // LANES):
        item = value[:, j * LANES : (j + 1) * LANES]
        pieces.append(
            item * cosine
            + pltpu.roll(item, LANES - ROT // 2, 1) * sine_low
            + pltpu.roll(item, ROT // 2, 1) * sine_high
        )
    return jnp.concatenate(pieces, axis=1)


def patterns():
    row_head = lax.broadcasted_iota(jnp.int32, (PACK * CHUNK, GROUP), 0) // CHUNK
    lane_head = lax.broadcasted_iota(jnp.int32, (PACK * CHUNK, GROUP), 1) // HEAD
    block_row = lax.broadcasted_iota(jnp.int32, (GROUP, GROUP), 0) // HEAD
    block_col = lax.broadcasted_iota(jnp.int32, (GROUP, GROUP), 1) // HEAD
    return row_head == lane_head, block_row == block_col


def interleave(items, lag):
    waiting = [(j * lag, item) for j, item in enumerate(items)]
    at = 0
    while waiting:
        alive = []
        for begin, item in waiting:
            if at < begin or next(item, waiting) is not waiting:
                alive.append((begin, item))
        waiting = alive
        at += 1


def stack(mask, item):
    return jnp.where(mask, jnp.concatenate([item] * PACK, axis=0), jnp.zeros((), BF))


def sum_heads(item, ones):
    high, low = split(item)
    return mm(high, ones) + mm(low, ones)


def tables(coarse, fine, tile):
    rows = TILE // 8
    co, so = [], []
    outer = coarse[pl.ds(tile * rows, rows)]
    ci, si = fine[0:8, :][None], fine[8:16, :][None]
    co, so = outer[:, 0:1, :], outer[:, 1:2, :]
    flat = lambda item: item.reshape(TILE, LANES)
    cosine = flat(co * ci - so * si)
    sine = so * ci + co * si
    return cosine, flat(sine * fine[16:24, :][None]), flat(sine * fine[24:32, :][None])


def attn_front_kernel(
    info, normed, target, w_q, w_k, w_v, b_q, b_k, b_v, w_proj, scale, mix_high, mix_low, base, inner, upb, w_up,
    attended, dq, fq_s, fk_s, v_s, tk_s, gn_s, gx_s, bias_q, scale_grad, shift, state, total, up_buf, sems,
):
    step = pl.program_id(0)
    strips = up_buf.shape[1] // LANES
    groups = w_q.shape[1] // GROUP
    span = TILE // CHUNK
    stack_mask, block_mask = patterns()
    ones = jnp.where(block_mask, 1.0, 0.0).astype(BF)
    causal = lax.broadcasted_iota(jnp.int32, (CHUNK, PACK * CHUNK), 0) >= (
        lax.broadcasted_iota(jnp.int32, (CHUNK, PACK * CHUNK), 1) % CHUNK
    )
    lower = jnp.where(
        lax.broadcasted_iota(jnp.int32, (CHUNK, CHUNK), 0) >= lax.broadcasted_iota(jnp.int32, (CHUNK, CHUNK), 1),
        1.0,
        0.0,
    ).astype(BF)

    @pl.when(step == 0)
    def _():
        for item in (state, total, bias_q, scale_grad, shift):
            item[...] = jnp.zeros_like(item)

        @pl.loop(0, strips)
        def _(j):
            strip_copy(info[0], w_up, up_buf, sems, 0, j).start()

    x = normed[...]
    cosine, low, high = tables(base, inner, step)
    grad_all = mm(target[...], w_proj[...], NT)
    feats, turned, values, held, before = {}, {}, {}, {}, {}

    def feature(g, which):
        cols = slice(g * GROUP, (g + 1) * GROUP)
        w, b, out = ((w_q, b_q, fq_s), (w_k, b_k, fk_s))[which]
        t = mm(x, w[:, cols]) + b[:, cols]
        yield
        t = turn(t, cosine, low, high)
        turned[which, g] = t
        t_high, t_low = split(t)
        spread = mm(t_high, mix_high[...]) + mm(t_low, mix_high[...]) + mm(t_high, mix_low[...])
        yield
        square = sum_heads(t * t, ones)
        yield
        feats[which, g] = (scale[:, cols] * jnp.exp(spread - square * (0.5 * HEAD ** (-0.5)))).astype(BF)
        out[:, cols] = feats[which, g]
        if which == 1:
            tk_s[:, cols] = t.astype(BF)
            values[g] = (mm(x, w_v[:, cols]) + b_v[:, cols]).astype(BF)
            v_s[:, cols] = values[g]
        yield

    def unit(g, c):
        cols = slice(g * GROUP, (g + 1) * GROUP)
        rows = slice(c * CHUNK, (c + 1) * CHUNK)
        fq, fk, vc = feats[0, g][rows], feats[1, g][rows], values[g][rows]
        stack_k, stack_v = stack(stack_mask, fk), stack(stack_mask, vc)
        kept = state[g]
        held = kept.astype(BF)
        state[g] = kept + jnp.where(block_mask, mm(fk, vc, TN), 0.0)
        keys = mm(lower, fk) + total[g]
        total[g] = keys[CHUNK - 1 : CHUNK, :]
        yield
        weight = jnp.where(causal, mm(fq, stack_k, NT), 0.0).astype(BF)
        wide = fq.astype(F32)
        den = sum_heads(wide * keys, ones)
        yield
        num = mm(weight, stack_v) + mm(fq, held)
        inverse = 1.0 / den
        yield
        mixed = num * inverse
        attended[rows, cols] = mixed.astype(BF)
        gn = (grad_all[rows, cols] * inverse).astype(BF)
        gn_s[rows, cols] = gn
        edge = jnp.where(causal, mm(gn, stack_v, NT), 0.0).astype(BF)
        yield
        grad_den = -sum_heads(gn.astype(F32) * mixed, ones)
        gx_s[rows, cols] = (grad_den * wide).astype(BF)
        yield
        dfq = mm(edge, stack_k) + mm(gn, held, NT) + grad_den * keys
        back = dfq * wide
        back_low = back.astype(BF)
        scale_grad[:, cols] += jnp.sum(back, axis=0, keepdims=True)
        yield
        dt = mm(back_low, mix_high[...], NT) + mm(back_low, mix_low[...], NT)
        dt = dt - mm(back_low, ones) * turned[0, g][rows] * (HEAD ** (-0.5))
        yield
        out = turn(dt, cosine[rows], -low[rows], -high[rows]).astype(BF)
        dq[rows, cols] = out
        bias_q[:, cols] += jnp.sum(out.astype(F32), axis=0, keepdims=True)
        yield

    interleave([feature(g, which) for g in range(groups) for which in range(2)], 0)
    interleave([unit(g, c) for c in range(span) for g in range(groups)], 0)

    @pl.when(step == pl.num_programs(0) - 1)
    def _():
        @pl.loop(0, strips)
        def _(j):
            strip_copy(info[0], w_up, up_buf, sems, 0, j).wait()

        @pl.loop(0, upb.shape[1] // GROUP)
        def _(j):
            cols = pl.ds(pl.multiple_of(j * GROUP, GROUP), GROUP)
            shift[...] += exact_row(upb[:, cols], up_buf[:, cols])


def attn_rear_kernel(
    tiles, info, fq_s, fk_s, v_s, tk_s, gn_s, gx_s, mix_high, mix_low, base, inner, bias_in, scale_in, scale,
    w_qkv, shift_in, dk, dv, sums_out, shift_out, bias_k, bias_v, scale_grad, w_buf, sems, state, total,
):
    step = pl.program_id(0)
    tile = tiles - 1 - step
    groups = dk.shape[1] // GROUP
    span = TILE // CHUNK
    stack_mask, block_mask = patterns()
    ones = jnp.where(block_mask, 1.0, 0.0).astype(BF)
    causal = lax.broadcasted_iota(jnp.int32, (CHUNK, PACK * CHUNK), 1) % CHUNK >= (
        lax.broadcasted_iota(jnp.int32, (CHUNK, PACK * CHUNK), 0)
    )
    upper = jnp.where(
        lax.broadcasted_iota(jnp.int32, (CHUNK, CHUNK), 1) >= lax.broadcasted_iota(jnp.int32, (CHUNK, CHUNK), 0),
        1.0,
        0.0,
    ).astype(BF)

    @pl.when(step == 0)
    def _():
        for item in (state, total, bias_k, bias_v):
            item[...] = jnp.zeros_like(item)
        for p in range(3):
            part_copy(info[0], w_qkv, w_buf, sems, p).start()
        scale_grad[...] = scale_in[...]

    cosine, low, high = tables(base, inner, tile)

    def unit(g, c):
        cols = slice(g * GROUP, (g + 1) * GROUP)
        rows = slice(c * CHUNK, (c + 1) * CHUNK)
        fq, fk, vc, gn = fq_s[rows, cols], fk_s[rows, cols], v_s[rows, cols], gn_s[rows, cols]
        stack_q, stack_g = stack(stack_mask, fq), stack(stack_mask, gn)
        kept = state[g]
        held = kept.astype(BF)
        state[g] = kept + jnp.where(block_mask, mm(fq, gn, TN), 0.0)
        sums = mm(upper, gx_s[rows, cols]) + total[g]
        total[g] = sums[0:1, :]
        yield
        edge = jnp.where(causal, mm(vc, stack_g, NT), 0.0).astype(BF)
        yield
        weight = jnp.where(causal, mm(fk, stack_q, NT), 0.0).astype(BF)
        yield
        dfk = mm(edge, stack_q) + mm(vc, held, NT) + sums
        back = dfk * fk.astype(F32)
        back_low = back.astype(BF)
        scale_grad[:, cols] += jnp.sum(back, axis=0, keepdims=True)
        yield
        dvc = (mm(weight, stack_g) + mm(fk, held)).astype(BF)
        dv[rows, cols] = dvc
        bias_v[:, cols] += jnp.sum(dvc.astype(F32), axis=0, keepdims=True)
        yield
        dt = mm(back_low, mix_high[...], NT) + mm(back_low, mix_low[...], NT)
        dt = dt - mm(back_low, ones) * tk_s[rows, cols].astype(F32) * (HEAD ** (-0.5))
        yield
        out = turn(dt, cosine[rows], -low[rows], -high[rows]).astype(BF)
        dk[rows, cols] = out
        bias_k[:, cols] += jnp.sum(out.astype(F32), axis=0, keepdims=True)
        yield

    interleave([unit(g, c) for c in reversed(range(span)) for g in range(groups)], 1)

    @pl.when(step == tiles - 1)
    def _():
        sums_out[0:1, :] = bias_in[...]
        sums_out[1:2, :] = bias_k[...]
        sums_out[2:3, :] = bias_v[...]
        sums_out[3:4, :] = scale_grad[...] / scale[...]
        shift_out[...] = shift_in[...]
        for p in range(3):
            part_copy(info[0], w_qkv, w_buf, sems, p).wait()

        @pl.loop(0, 3 * groups)
        def _(j):
            row = sums_out[pl.ds(j // groups, 1), pl.ds(pl.multiple_of((j % groups) * GROUP, GROUP), GROUP)]
            shift_out[...] += exact_row(row, w_buf[:, pl.ds(pl.multiple_of(j * GROUP, GROUP), GROUP)])


def turn_tables():
    lane = np.arange(LANES) % HEAD
    freqs = np.where(lane < ROT, 10000.0 ** (-(lane % (ROT // 2)) / (ROT // 2)), 0.0)
    waves = lambda places: np.stack([np.cos(places[:, None] * freqs), np.sin(places[:, None] * freqs)], axis=1)
    fine = np.concatenate(
        [
            waves(np.arange(8)).transpose(1, 0, 2).reshape(16, LANES),
            np.broadcast_to(np.where(lane < ROT // 2, -1.0, 0.0), (8, LANES)),
            np.broadcast_to(np.where((lane >= ROT // 2) & (lane < ROT), 1.0, 0.0), (8, LANES)),
        ]
    )
    return waves(np.arange(LEN // 8) * 8.0).astype(np.float32), fine.astype(np.float32)


def prepare_kernel(*refs):
    *parts, points, basis, vectors, mix_high, mix_low = refs
    at = 0
    for part in parts:
        count = part.shape[0]
        vectors[:, at : at + count] = part[...].astype(F32).reshape(1, count)
        at += count
    table = jnp.dot(basis[...], points[...], precision=lax.Precision.HIGHEST, preferred_element_type=F32)
    wide = jnp.concatenate([table] * PACK, axis=1)
    _, block_mask = patterns()
    tall = jnp.where(block_mask, jnp.concatenate([wide] * PACK, axis=0), 0.0)
    mix_high[...], mix_low[...] = split(tall)


def prepare(parts, qmc_points):
    places = np.arange(HEAD)
    cosines = np.cos(np.pi * (places[:, None] + 0.5) * places[None, :] / HEAD)
    cosines = cosines * np.where(places == 0, math.sqrt(1.0 / HEAD), math.sqrt(2.0 / HEAD))[None, :]
    total = sum(item.shape[0] for item in parts)
    vectors, high, low = pl.pallas_call(
        prepare_kernel,
        out_shape=(
            jax.ShapeDtypeStruct((1, total), F32),
            jax.ShapeDtypeStruct((GROUP, GROUP), BF),
            jax.ShapeDtypeStruct((GROUP, GROUP), BF),
        ),
        compiler_params=params(),
        name="prepare",
    )(*parts, qmc_points, jnp.asarray(cosines * HEAD ** (-0.25), F32))
    return vectors, (high, low)


def stored(tile, info, own):
    return ((tile // own) ^ info[0]) * own + tile % own


def attention_front(info, normed, target, w_qkv, w_proj, vectors, mix, turns, upb, w_up):
    total, dim = normed.shape
    ff = upb.shape[1]
    half = dim // 2
    tiles = total // TILE
    front = lambda i, info: (stored(i, info, tiles // 2), 0)
    plain = lambda i, info: (i, 0)
    block = lambda k: pl.BlockSpec((dim, half), lambda i, info: (0, 2 * k + info[0]), pipeline_mode=pl.Buffered(1))
    groups = half // GROUP
    return pl.pallas_call(
        attn_front_kernel,
        out_shape=(
            *(jax.ShapeDtypeStruct((total, half), BF) for _ in range(8)),
            *(jax.ShapeDtypeStruct((1, half), F32) for _ in range(2)),
            jax.ShapeDtypeStruct((1, dim), F32),
        ),
        grid_spec=pltpu.PrefetchScalarGridSpec(
            num_scalar_prefetch=1,
            grid=(tiles,),
            in_specs=[
                pl.BlockSpec((TILE, dim), front),
                pl.BlockSpec((TILE, dim), front),
                block(0),
                block(1),
                block(2),
                vector_spec(half, 5 * dim, 0),
                vector_spec(half, 6 * dim, 0),
                vector_spec(half, 7 * dim, 0),
                pl.BlockSpec((half, dim), lambda i, info: (info[0], 0), pipeline_mode=pl.Buffered(1)),
                vector_spec(half, 2 * dim, 0),
            ]
            + [whole(item.shape) for item in (*mix, *turns, upb)]
            + [anywhere()],
            out_specs=[pl.BlockSpec((TILE, half), front)] * 2
            + [pl.BlockSpec((TILE, half), plain)] * 6
            + [whole((1, half))] * 2
            + [whole((1, dim))],
            scratch_shapes=[
                pltpu.VMEM((groups, GROUP, GROUP), F32),
                pltpu.VMEM((groups, 1, GROUP), F32),
                pltpu.VMEM((dim, ff), BF),
                pltpu.SemaphoreType.DMA((1, ff // LANES)),
            ],
        ),
        compiler_params=params(),
        cost_estimate=cost(8 * total * dim * half + 64 * total * half * GROUP, 12 * total * dim, 2 * total * half),
        name="attention_front",
    )(info, normed, target, w_qkv, w_qkv, w_qkv, vectors, vectors, vectors, w_proj, vectors, *mix, *turns, upb, w_up)


def attention_rear(info, saved, bias_q, scale_sum, w_qkv, vectors, shift, mix, turns):
    total, half = saved[0].shape
    dim = w_qkv.shape[0]
    tiles = total // TILE
    rear = lambda i, info: (stored(tiles - 1 - i, info, tiles // 2), 0)
    plain = lambda i, info: (tiles - 1 - i, 0)
    groups = half // GROUP
    return pl.pallas_call(
        partial(attn_rear_kernel, tiles),
        out_shape=(
            *(jax.ShapeDtypeStruct((total, half), BF) for _ in range(2)),
            jax.ShapeDtypeStruct((4, half), F32),
            jax.ShapeDtypeStruct((1, dim), F32),
        ),
        grid_spec=pltpu.PrefetchScalarGridSpec(
            num_scalar_prefetch=1,
            grid=(tiles,),
            in_specs=[pl.BlockSpec((TILE, half), plain)] * 6
            + [whole(item.shape) for item in (*mix, *turns, bias_q, scale_sum)]
            + [vector_spec(half, 2 * dim, 0), anywhere(), whole(shift.shape)],
            out_specs=[pl.BlockSpec((TILE, half), rear)] * 2 + [whole((4, half)), whole((1, dim))],
            scratch_shapes=[pltpu.VMEM((1, half), F32) for _ in range(3)]
            + [pltpu.VMEM((dim, 3 * half), BF), pltpu.SemaphoreType.DMA((3,))]
            + [pltpu.VMEM((groups, GROUP, GROUP), F32), pltpu.VMEM((groups, 1, GROUP), F32)],
        ),
        compiler_params=params(),
        cost_estimate=cost(48 * total * half * GROUP, 16 * total * half, 0),
        name="attention_rear",
    )(info, *saved, *mix, *turns, bias_q, scale_sum, vectors, w_qkv, shift)


def out_kernel(own, info, act, attended, w_proj, w_down, *rest):
    step = pl.program_id(0)
    if own:
        res, received, first, second, out, down_buf, sems = rest
    else:
        out, down_buf, sems = rest

    @pl.when(step == 0)
    def _():
        @pl.loop(0, down_buf.shape[0] // LANES)
        def _(j):
            strip_copy(info[0], w_down, down_buf, sems, 1, j).start()

        @pl.loop(0, down_buf.shape[0] // LANES)
        def _(j):
            strip_copy(info[0], w_down, down_buf, sems, 1, j).wait()

    value = mm(act[...], down_buf[...]) + mm(attended[...], w_proj[...])
    if own:
        value = value + received[...].astype(F32) + (first[...] + second[...]) + res[...].astype(F32)
    out[...] = value.astype(BF)


def out_rows(own, info, act, attended, w_proj, w_down, res=None, received=None, vectors=None):
    total, ff = act.shape
    dim = w_proj.shape[1]
    half = attended.shape[1]
    rows = total // 2
    tiles = rows // TILE
    shift = 0 if own else tiles
    shifted = lambda i, info: (i + shift, 0)
    plain = lambda i, info: (i, 0)
    extra, extra_specs = (), []
    if own:
        extra = (res, received, vectors, vectors)
        extra_specs = [pl.BlockSpec((TILE, dim), plain), pl.BlockSpec((TILE, dim), plain)]
        extra_specs += [vector_spec(dim, 3 * dim), vector_spec(dim, 4 * dim)]
    return pl.pallas_call(
        partial(out_kernel, own),
        out_shape=jax.ShapeDtypeStruct((rows, dim), BF),
        grid_spec=pltpu.PrefetchScalarGridSpec(
            num_scalar_prefetch=1,
            grid=(tiles,),
            in_specs=[
                pl.BlockSpec((TILE, ff), shifted),
                pl.BlockSpec((TILE, half), shifted),
                pl.BlockSpec((half, dim), lambda i, info: (info[0], 0), pipeline_mode=pl.Buffered(1)),
                anywhere(),
            ]
            + extra_specs,
            out_specs=pl.BlockSpec((TILE, dim), plain),
            scratch_shapes=[
                pltpu.VMEM((ff, dim), BF),
                pltpu.SemaphoreType.DMA((2, ff // LANES)),
            ],
        ),
        compiler_params=params(),
        cost_estimate=cost(2 * rows * dim * (ff + half), 2 * rows * (ff + half + dim) + 2 * dim * (ff + half)),
        name="out_rows",
    )(info, act, attended, w_proj, w_down, *extra)


def back_kernel(own, info, dq, dk, dv, up_grad, w_qkv, w_up, *rest):
    step = pl.program_id(0)
    if own:
        res, gain, target, received, out, w_buf, up_buf, part_sems, sems = rest
    else:
        out, w_buf, up_buf, part_sems, sems = rest
    grads = (dq, dk, dv)
    half = dq.shape[1]

    @pl.when(step == 0)
    def _():
        for p in range(3):
            part_copy(info[0], w_qkv, w_buf, part_sems, p).start()

        @pl.loop(0, up_buf.shape[1] // LANES)
        def _(j):
            strip_copy(info[0], w_up, up_buf, sems, 0, j).start()

        for p in range(3):
            part_copy(info[0], w_qkv, w_buf, part_sems, p).wait()

        @pl.loop(0, up_buf.shape[1] // LANES)
        def _(j):
            strip_copy(info[0], w_up, up_buf, sems, 0, j).wait()

    value = mm(up_grad[...], up_buf[...], NT)
    for p in range(3):
        value = value + mm(grads[p][...], w_buf[:, p * half : (p + 1) * half], NT)
    if own:
        xhat, rstd = norm_stats(res[...].astype(F32))
        scaled = (value + received[...].astype(F32)) * gain[...]
        middle = jnp.mean(scaled, axis=-1, keepdims=True)
        slope = jnp.mean(scaled * xhat, axis=-1, keepdims=True)
        out[...] = target[...].astype(F32) + rstd * (scaled - middle - xhat * slope)
    else:
        out[...] = value.astype(BF)


def back_rows(own, info, dq, dk, dv, up_grad, w_qkv, w_up, res=None, vectors=None, target=None, received=None):
    total, ff = up_grad.shape
    rows, dim = total // 2, w_qkv.shape[0]
    half = dq.shape[1]
    tiles = rows // TILE
    shift = 0 if own else tiles
    shifted = lambda i, info: (i + shift, 0)
    plain = lambda i, info: (i, 0)
    extra, extra_specs = (), []
    if own:
        extra = (res, vectors, target, received)
        extra_specs = [
            pl.BlockSpec((TILE, dim), plain),
            vector_spec(dim, 0),
            pl.BlockSpec((TILE, dim), plain),
            pl.BlockSpec((TILE, dim), plain),
        ]
    return pl.pallas_call(
        partial(back_kernel, own),
        out_shape=jax.ShapeDtypeStruct((rows, dim), F32 if own else BF),
        grid_spec=pltpu.PrefetchScalarGridSpec(
            num_scalar_prefetch=1,
            grid=(tiles,),
            in_specs=[pl.BlockSpec((TILE, half), shifted)] * 3
            + [pl.BlockSpec((TILE, ff), shifted), anywhere(), anywhere()]
            + extra_specs,
            out_specs=pl.BlockSpec((TILE, dim), plain),
            scratch_shapes=[
                pltpu.VMEM((dim, 3 * half), BF),
                pltpu.VMEM((dim, ff), BF),
                pltpu.SemaphoreType.DMA((3,)),
                pltpu.SemaphoreType.DMA((2, ff // LANES)),
            ],
        ),
        compiler_params=params(),
        cost_estimate=cost(2 * rows * dim * (ff + 3 * half), 2 * rows * (ff + 3 * half + 3 * dim) + 2 * dim * (ff + 3 * half)),
        name="back_rows",
    )(info, dq, dk, dv, up_grad, w_qkv, w_up, *extra)


def bit_orders(ndp):
    bits = [1 << j for j in range(ndp.bit_length() - 1)]
    return tuple(bits), tuple(bits[1::-1] + bits[2:])


def spots(me, ndp):
    apart = jnp.asarray(np.arange(ndp, dtype=np.int32)) ^ me
    rows = []
    for order in bit_orders(ndp):
        spot = jnp.zeros((ndp,), jnp.int32)
        for j, bit in enumerate(order):
            spot = spot + (((apart // bit) % 2) << (len(order) - 1 - j))
        rows.append(spot)
    return jnp.stack(rows)


def add(left, right, kind=BF):
    return (left.astype(F32) + right.astype(F32)).astype(kind)


def cross(value, bit, ndp):
    return lax.ppermute(value, "dp", [(i, i ^ bit) for i in range(ndp)])


class Reduction:
    def __init__(self, first, second, ndp):
        self.ndp = ndp
        self.orders = bit_orders(ndp)
        self.at = 0
        self.pairs = [first, second]
        self.fly()

    def fly(self):
        self.received = [
            cross(send, order[self.at], self.ndp) for (send, keep), order in zip(self.pairs, self.orders)
        ]

    def land(self, token=None):
        if token is not None:
            token, *self.received = lax.optimization_barrier((token, *self.received))
        self.step()
        return token

    def step(self):
        keeps = [keep for send, keep in self.pairs]
        self.at += 1
        steps = len(self.orders[0])
        if self.at == steps:
            parts = [add(k, r, F32)[0] for k, r in zip(keeps, self.received)]
            self.result = jnp.concatenate(parts, axis=0) if len(parts) > 1 else parts[0]
            return
        cut = keeps[0].shape[0] // 2
        pairs = [
            (add(k[cut:], r[cut:]), add(k[:cut], r[:cut])) for k, r in zip(keeps, self.received)
        ]
        if self.at == 2 and len(pairs) == 2:
            pairs = [tuple(jnp.concatenate(items, axis=1) for items in zip(*pairs))]
        self.pairs = pairs

    def hold(self, token):
        if self.at == len(self.orders[0]):
            token, self.result = lax.optimization_barrier((token, self.result))
        return token

    def finish(self):
        if 0 < self.at < len(self.orders[0]):
            self.fly()
        while self.at < len(self.orders[0]):
            self.land()
            if self.at < len(self.orders[0]):
                self.fly()
        return self.result

    def values(self):
        return [item for pair in self.pairs for item in pair]

    def after(self, token):
        if self.at < len(self.orders[0]):
            token, *items = lax.optimization_barrier((token, *self.values()))
            self.pairs = [(items[2 * j], items[2 * j + 1]) for j in range(len(items) // 2)]
            self.fly()
        else:
            token, self.result = lax.optimization_barrier((token, self.result))
        return token


def swap(value):
    return lax.ppermute(value, "stream", [(0, 1), (1, 0)])


def per_device(
    ndp, residual, cotangent, ln_gain, ln_bias, w_qkv, b_qkv, w_proj, b_proj, feature_scale,
    w_up, b_up, w_down, b_down, qmc_points, slot_lengths,
):
    own_rows, dim = residual.shape
    half = dim // 2
    ff = w_up.shape[1]
    side = lax.axis_index("stream")
    me = lax.axis_index("dp")
    info = jnp.stack([side, me, slot_lengths[0]]).astype(jnp.int32)
    table = spots(me, ndp)
    vectors, mix = prepare((ln_gain, ln_bias, feature_scale, b_proj, b_down, b_qkv, b_up), qmc_points)

    other_res = swap(residual)
    other_cot = swap(cotangent)
    *mine, target_sum = mlp_rows(0, info, residual, cotangent, vectors, w_up, w_down)
    normed, target, act, up_grad, upb, _ = mlp_rows(
        1, info, other_res, other_cot, vectors, w_up, w_down, mine
    )

    turns = tuple(jnp.asarray(item) for item in turn_tables())
    parts = mlp_weight_grads(ndp, table, act, target, normed, up_grad)
    mlp_sums = Reduction(parts[:2], parts[2:], ndp)

    attended, dq, *saved, bias_q, scale_sum, shift = attention_front(
        info, normed, target, w_qkv, w_proj, vectors, mix, turns, upb, w_up
    )
    attended = mlp_sums.land(attended)
    info = mlp_sums.after(info)
    dk, dv, sums, shift = attention_rear(info, saved, bias_q, scale_sum, w_qkv, vectors, shift, mix, turns)
    dk = mlp_sums.land(dk)
    table = mlp_sums.after(table)

    mine = lax.broadcasted_iota(jnp.int32, (1, 2, 1), 1) == side
    spread = lambda item: jnp.where(mine, item[:, None, :], 0.0)
    four = spread(sums)
    small = jnp.concatenate(
        [
            shift.reshape(ndp, -1),
            four[:3].reshape(ndp, -1),
            target_sum.reshape(ndp, -1),
            four[3].reshape(ndp, -1),
            spread(upb.reshape(-1, LANES)).reshape(ndp, -1),
        ],
        axis=1,
    )
    count = small.shape[1]
    extra = jnp.pad(small.astype(BF), ((0, 0), (0, 8 * half - count))).reshape(ndp, 8, half)
    parts = attn_weight_grads(ndp, table, normed, target, attended, dq, dk, dv, extra)
    attn_sums = Reduction(parts[:2], parts[2:], ndp)
    mlp_sums.land()
    info = mlp_sums.after(info)

    back_send = back_rows(False, info, dq, dk, dv, up_grad, w_qkv, w_up)
    back_send = attn_sums.land(back_send)
    info = attn_sums.after(info)
    back_received = swap(back_send)
    out_send = out_rows(False, info, act, attended, w_proj, w_down)
    out_send = attn_sums.land(mlp_sums.land(out_send))
    info = attn_sums.after(mlp_sums.after(info))
    out_received = swap(out_send)
    residual_grad = back_rows(
        True, info, dq, dk, dv, up_grad, w_qkv, w_up, residual, vectors, target, back_received
    )
    residual_grad = mlp_sums.hold(attn_sums.land(residual_grad))
    info = attn_sums.after(info)
    block_out = out_rows(True, info, act, attended, w_proj, w_down, residual, out_received, vectors)
    block_out = attn_sums.land(block_out)
    mlp_total, attn_total = mlp_sums.finish(), attn_sums.finish()

    blk = ff // (2 * ndp)
    size = dim // ndp
    small_size = size // 2
    down_rows = mlp_total[:blk]
    per = max(LANES // blk, 1)
    owners = [
        (v * 2 + s, (2 * (v // per) + s) * per + v % per) for v in range(ndp) for s in range(2)
    ]
    if any(a != b for a, b in owners):
        down_rows = lax.ppermute(down_rows, ("dp", "stream"), owners)

    def halves(blocks):
        blocks = blocks.reshape(blocks.shape[0], 2, small_size, blocks.shape[2])
        pick = lambda at: lax.dynamic_index_in_dim(blocks, at, 1, keepdims=False)
        return pick(side), pick(1 - side)

    def order(own, other):
        return jnp.where(side == 0, own, other), jnp.where(side == 0, other, own)

    keep, give = halves(mlp_total[blk:].reshape(2, size, -1))
    first, second = order(keep, swap(give))
    apart = lambda item: jnp.transpose(item, (1, 0, 2)).reshape(small_size, -1, 1, LANES)
    upw_grad = jnp.concatenate([apart(first), apart(second)], axis=2).reshape(small_size, ff)

    keep, give = halves(attn_total[: 3 * size].reshape(3, size, half))
    rest = attn_total[4 * size :]
    received = swap(jnp.concatenate([give.reshape(3 * small_size, half), rest], axis=0))
    first, second = order(keep, received[: 3 * small_size].reshape(3, small_size, half))
    qkvw_grad = jnp.concatenate([item[p] for p in range(3) for item in (first, second)], axis=1)
    proj_rows = jnp.concatenate(
        [attn_total[3 * size + p * small_size : 3 * size + (p + 1) * small_size] for p in range(2)], axis=1
    )
    proj_owners = [(v * 2 + s, ndp * s + v) for v in range(ndp) for s in range(2)]
    projw_grad = lax.ppermute(proj_rows, ("dp", "stream"), proj_owners)

    flat = (rest + received[3 * small_size :]).reshape(-1)
    ends = np.cumsum([0, size, 3 * size, size, size, 2 * blk])
    pieces = [
        lax.dynamic_index_in_dim(flat[a:b].reshape(2, -1), side, 0, keepdims=False)
        for a, b in zip(ends[:-1], ends[1:])
    ]
    shift_grad, qkvb_grad, projb_grad, scale_grad, upb_grad = pieces
    mine_at = (2 * me + side) * small_size
    near = lambda item: lax.dynamic_slice_in_dim(item, mine_at, small_size).astype(F32)
    along = jnp.sum(near(w_qkv) * qkvw_grad, axis=1) + jnp.sum(near(w_up) * upw_grad, axis=1)
    gain_grad = (along - near(ln_bias) * shift_grad) / near(ln_gain)

    return (
        block_out, residual_grad, gain_grad, shift_grad, qkvw_grad, qkvb_grad, projw_grad,
        projb_grad, scale_grad, upw_grad, upb_grad, down_rows, projb_grad,
    )


def solution(mesh):
    rows = P(("dp", "stream"), None)
    items = P(("dp", "stream"))
    return jax.shard_map(
        partial(per_device, mesh.shape["dp"]),
        mesh=mesh,
        in_specs=(rows, rows) + (P(),) * 12 + (P("dp"),),
        out_specs=(rows, rows, items, items, rows, items, rows, items, items, rows, items, rows, items),
        check_vma=False,
    )
```

```python
from functools import partial
import math

import jax
import jax.numpy as jnp
import numpy as np
from jax import lax
from jax.experimental import pallas as pl
from jax.experimental.pallas import tpu as pltpu
from jax.sharding import PartitionSpec as P

HEAD = 64
ROT = 16
LEN = 2048
EPSILON = 1e-05

BF = jnp.bfloat16
F32 = jnp.float32
TILE = 256
CHUNK = 128
GROUP = 256
PACK = GROUP // HEAD
LANES = 128
ERFC = tuple(
    item * math.sqrt(0.5 * math.pi)
    for item in (0.254829592, -0.284496736, 1.421413741, -1.453152027, 1.061405429)
)
VMEM_CAP = 55 * 1024 * 1024

NN = (((1,), (0,)), ((), ()))
NT = (((1,), (1,)), ((), ()))
TN = (((0,), (0,)), ((), ()))


def mm(left, right, dims=NN):
    return lax.dot_general(left, right, dims, preferred_element_type=F32)


def split(value):
    high = value.astype(BF)
    return high, (value - high.astype(F32)).astype(BF)


def whole(shape):
    rank = len(shape)
    return pl.BlockSpec(shape, lambda *_: (0,) * rank, pipeline_mode=pl.Buffered(1))


def anywhere():
    return pl.BlockSpec(memory_space=pl.ANY)


def params(limit=VMEM_CAP):
    return pltpu.CompilerParams(vmem_limit_bytes=limit)


def vector_spec(width, at, side=None):
    return pl.BlockSpec(
        (1, width),
        lambda i, info: (0, at // width + (0 if side is None else info[0])),
        pipeline_mode=pl.Buffered(1),
    )


def cost(flops, moved, trans=0):
    return pl.CostEstimate(flops=int(0.4 * flops), bytes_accessed=int(0.4 * moved), transcendentals=int(0.4 * trans))


def exact_row(row, weights):
    high, low = split(jnp.broadcast_to(row, (8, row.shape[1])))
    both = mm(jnp.concatenate([high, low], axis=0), weights, NT)
    return both[0:1] + both[8:9]


def norm_stats(rows):
    mean = jnp.mean(rows, axis=-1, keepdims=True)
    centred = rows - mean
    rstd = lax.rsqrt(jnp.mean(centred * centred, axis=-1, keepdims=True) + EPSILON)
    return centred * rstd, rstd


def strip_copy(side, source, buf, sems, kind, j):
    there = pl.ds(pl.multiple_of((2 * j + side) * LANES, LANES), LANES)
    here = pl.ds(pl.multiple_of(j * LANES, LANES), LANES)
    if kind == 0:
        return pltpu.make_async_copy(source.at[:, there], buf.at[:, here], sems.at[kind, j])
    return pltpu.make_async_copy(source.at[there, :], buf.at[here, :], sems.at[kind, j])


def part_copy(side, source, buf, sems, p):
    width = buf.shape[1] // 3
    there = pl.ds(pl.multiple_of((2 * p + side) * width, LANES), width)
    return pltpu.make_async_copy(source.at[:, there], buf.at[:, p * width : (p + 1) * width], sems.at[p])


def mlp_kernel(half, tiles, info, res, cot, gain, bias, b_up, w_up, w_down, *rest):
    normed, target, act, up_grad, upb, sums, up_buf, down_buf, sems = rest[-9:]
    step = pl.program_id(0)
    side = info[0]

    @pl.when(step == 0)
    def _():
        @pl.loop(0, up_buf.shape[1] // LANES)
        def _(j):
            strip_copy(side, w_up, up_buf, sems, 0, j).start()
            strip_copy(side, w_down, down_buf, sems, 1, j).start()

        if half == 0:
            upb[...] = jnp.zeros_like(upb)
            sums[...] = jnp.zeros_like(sums)
        else:
            upb[...] = rest[4][...]
            sums[...] = jnp.zeros_like(sums)

    rows = res.shape[0]
    xhat, _ = norm_stats(res[...].astype(F32))
    low = (xhat * gain[...] + bias[...]).astype(BF)
    normed[...] = low
    part = side if half == 0 else 1 - side
    place = (part * tiles + step) * rows + lax.broadcasted_iota(jnp.int32, (rows, 1), 0)
    tgt = jnp.where(place < info[2], cot[...], jnp.zeros_like(cot))
    target[...] = tgt
    ones = jnp.ones((8, rows), BF)
    if half == 0:
        sums[...] += mm(ones, tgt)[0:1]
    width = 1024
    strips = width // LANES

    @pl.loop(0, up_buf.shape[1] // width)
    def _(j):
        cols = pl.ds(pl.multiple_of(j * width, width), width)

        @pl.when(step == 0)
        def _():
            for b in range(strips):
                strip_copy(side, w_up, up_buf, sems, 0, j * strips + b).wait()
                strip_copy(side, w_down, down_buf, sems, 1, j * strips + b).wait()

        shift = jnp.concatenate(
            [
                b_up[:, pl.ds(pl.multiple_of((2 * (j * strips + b) + side) * LANES, LANES), LANES)]
                for b in range(strips)
            ],
            axis=1,
        )
        up = mm(low, up_buf[:, cols]) + shift
        back = mm(tgt, down_buf[cols, :], NT)
        bell = jnp.exp2(up * up * (-0.5 * math.log2(math.e)) - 0.5 * math.log2(2.0 * math.pi))
        t = 1.0 / (1.0 + (0.3275911 * math.sqrt(0.5)) * jnp.abs(up))
        poly = ERFC[4]
        for item in ERFC[3::-1]:
            poly = item + t * poly
        tail = (t * bell) * poly
        phi = jnp.where(up >= 0, 1.0 - tail, tail)
        act[:, cols] = (up * phi).astype(BF)
        grad = (back * (phi + up * bell)).astype(BF)
        up_grad[:, cols] = grad
        upb[:, cols] += mm(ones, grad)[0:1]


def mlp_rows(half, info, res, cot, vectors, w_up, w_down, earlier=()):
    rows, dim = res.shape
    ff = w_up.shape[1] // 2
    tiles = rows // TILE
    total = 2 * rows
    shift = half * tiles
    row_map = lambda i, info: (i, 0)
    out_map = lambda i, info: (i + shift, 0)
    outs = (
        jax.ShapeDtypeStruct((total, dim), BF),
        jax.ShapeDtypeStruct((total, dim), BF),
        jax.ShapeDtypeStruct((total, ff), BF),
        jax.ShapeDtypeStruct((total, ff), BF),
        jax.ShapeDtypeStruct((1, ff), F32),
        jax.ShapeDtypeStruct((1, dim), F32),
    )
    return pl.pallas_call(
        partial(mlp_kernel, half, tiles),
        out_shape=outs,
        grid_spec=pltpu.PrefetchScalarGridSpec(
            num_scalar_prefetch=1,
            grid=(tiles,),
            in_specs=[
                pl.BlockSpec((TILE, dim), row_map),
                pl.BlockSpec((TILE, dim), row_map),
                vector_spec(dim, 0),
                vector_spec(dim, dim),
                vector_spec(2 * ff, 8 * dim),
                anywhere(),
                anywhere(),
            ]
            + [anywhere()] * (len(earlier) - 1)
            + [whole((1, ff))] * min(len(earlier), 1),
            out_specs=[
                pl.BlockSpec((TILE, dim), out_map),
                pl.BlockSpec((TILE, dim), out_map),
                pl.BlockSpec((TILE, ff), out_map),
                pl.BlockSpec((TILE, ff), out_map),
                whole((1, ff)),
                whole((1, dim)),
            ],
            scratch_shapes=[
                pltpu.VMEM((dim, ff), BF),
                pltpu.VMEM((ff, dim), BF),
                pltpu.SemaphoreType.DMA((2, ff // LANES)),
            ],
        ),
        input_output_aliases={8 + j: j for j in range(len(earlier) - 1)},
        compiler_params=params(63 * 1024 * 1024),
        cost_estimate=cost(4 * rows * dim * ff, 12 * rows * dim + 16 * rows * ff, 2 * rows * ff),
        name="mlp_rows",
    )(info, res, cot, vectors, vectors, vectors, w_up, w_down, *earlier)


def ship(table, which, buf, send, keep, sems, first, count):
    half = send.shape[0]
    for b in range(count):
        spot = table[which, first + b]

        @pl.when(spot >= half)
        def _():
            pltpu.make_async_copy(buf.at[first + b], send.at[spot - half], sems.at[first + b]).start()

        @pl.when(spot < half)
        def _():
            pltpu.make_async_copy(buf.at[first + b], keep.at[spot], sems.at[first + b]).start()


def shipped(buf, keep, sems):
    for b in range(buf.shape[0]):
        pltpu.make_async_copy(buf.at[b], keep.at[0], sems.at[b]).wait()


def mlp_grad_kernel(
    tiles, table, act, target, normed, up_grad, send_a, keep_a, send_b, keep_b,
    grads, buf_a, buf_b, sems_a, sems_b, sem,
):
    step = pl.program_id(0)

    @pl.when(step == 0)
    def _():
        pltpu.make_async_copy(up_grad, grads, sem).start()

    @pl.when(step < tiles)
    def _():
        value = mm(act[...], target[...], TN).astype(BF)
        size = buf_a.shape[1]
        count = value.shape[0] // size
        first = step * count
        for b in range(count):
            buf_a[first + b] = value[b * size : (b + 1) * size, :]
        ship(table, 0, buf_a, send_a, keep_a, sems_a, first, count)

    @pl.when(step == tiles)
    def _():
        pltpu.make_async_copy(up_grad, grads, sem).wait()

    @pl.when(step >= tiles)
    def _():
        value = mm(normed[...], grads[...], TN).astype(BF)
        size = buf_b.shape[1] // 2
        width = buf_b.shape[2]
        count = value.shape[0] // size
        first = (step - tiles) * count
        for b in range(count):
            for p in range(2):
                buf_b[first + b, p * size : (p + 1) * size, :] = value[
                    b * size : (b + 1) * size, p * width : (p + 1) * width
                ]
        ship(table, 1, buf_b, send_b, keep_b, sems_b, first, count)

    @pl.when(step == pl.num_programs(0) - 1)
    def _():
        shipped(buf_a, keep_a, sems_a)
        shipped(buf_b, keep_b, sems_b)


def mlp_weight_grads(ndp, table, act, target, normed, up_grad):
    total, dim = normed.shape
    ff = act.shape[1]
    rows = ff // ndp
    shape = jax.ShapeDtypeStruct((ndp // 2, rows, dim), BF)
    wide, narrow = 512, 256
    tiles = ff // wide
    return pl.pallas_call(
        partial(mlp_grad_kernel, tiles),
        out_shape=(shape,) * 4,
        grid_spec=pltpu.PrefetchScalarGridSpec(
            num_scalar_prefetch=1,
            grid=(tiles + dim // narrow,),
            in_specs=[
                pl.BlockSpec((total, wide), lambda i, t: (0, jnp.minimum(i, tiles - 1))),
                whole((total, dim)),
                pl.BlockSpec((total, narrow), lambda i, t: (0, jnp.maximum(i - tiles, 0))),
                anywhere(),
            ],
            out_specs=[anywhere()] * 4,
            scratch_shapes=[pltpu.VMEM((total, ff), BF)]
            + [pltpu.VMEM((ndp, rows, dim), BF)] * 2
            + [pltpu.SemaphoreType.DMA((ndp,))] * 2
            + [pltpu.SemaphoreType.DMA],
        ),
        compiler_params=params(),
        cost_estimate=cost(4 * total * dim * ff, 4 * total * (dim + ff) + 4 * dim * ff),
        name="mlp_weight_grads",
    )(table, act, target, normed, up_grad)


def attn_grad_kernel(
    table, normed, attended, target, dq, dk, dv, extra, send_a, keep_a, send_b, keep_b, buf_a, buf_b, sems_a, sems_b
):
    step = pl.program_id(0)
    ndp = buf_a.shape[0]
    size = buf_a.shape[1] // 2
    small = size // 2
    half = dq.shape[1]

    @pl.when(step == 0)
    def _():
        value = mm(attended[...], target[...], TN).astype(BF)
        for b in range(ndp):
            for p in range(2):
                at = size + p * small
                buf_b[b, at : at + small, :] = value[b * small : (b + 1) * small, p * half : (p + 1) * half]
            buf_b[b, 2 * size :, :] = extra[b]

    count = normed.shape[1] // size
    first = step * count
    for item, buf, at in ((dq, buf_a, 0), (dk, buf_a, size), (dv, buf_b, 0)):
        value = mm(normed[...], item[...], TN).astype(BF)
        for b in range(count):
            buf[first + b, at : at + size, :] = value[b * size : (b + 1) * size, :]
    ship(table, 0, buf_a, send_a, keep_a, sems_a, first, count)
    ship(table, 1, buf_b, send_b, keep_b, sems_b, first, count)

    @pl.when(step == pl.num_programs(0) - 1)
    def _():
        shipped(buf_a, keep_a, sems_a)
        shipped(buf_b, keep_b, sems_b)


def attn_weight_grads(ndp, table, normed, target, attended, dq, dk, dv, extra):
    total, dim = normed.shape
    half = dq.shape[1]
    rows = 2 * dim // ndp
    more = extra.shape[1]
    shapes = [jax.ShapeDtypeStruct((ndp // 2, rows + j * more, half), BF) for j in range(2)]
    step = 256
    return pl.pallas_call(
        attn_grad_kernel,
        out_shape=(shapes[0], shapes[0], shapes[1], shapes[1]),
        grid_spec=pltpu.PrefetchScalarGridSpec(
            num_scalar_prefetch=1,
            grid=(dim // step,),
            in_specs=[
                pl.BlockSpec((total, step), lambda i, t: (0, i)),
                whole((total, half)),
                whole((total, dim)),
            ]
            + [whole((total, half))] * 3
            + [whole(extra.shape)],
            out_specs=[anywhere()] * 4,
            scratch_shapes=[pltpu.VMEM((ndp, rows + j * more, half), BF) for j in range(2)]
            + [pltpu.SemaphoreType.DMA((ndp,))] * 2,
        ),
        compiler_params=params(),
        cost_estimate=cost(8 * total * dim * half, 2 * total * (2 * dim + 4 * half) + 8 * dim * half),
        name="attn_weight_grads",
    )(table, normed, attended, target, dq, dk, dv, extra)


def turn(value, cosine, sine_low, sine_high):
    pieces = []
    for j in range(value.shape[1] // LANES):
        item = value[:, j * LANES : (j + 1) * LANES]
        pieces.append(
            item * cosine
            + pltpu.roll(item, LANES - ROT // 2, 1) * sine_low
            + pltpu.roll(item, ROT // 2, 1) * sine_high
        )
    return jnp.concatenate(pieces, axis=1)


def patterns():
    row_head = lax.broadcasted_iota(jnp.int32, (PACK * CHUNK, GROUP), 0) // CHUNK
    lane_head = lax.broadcasted_iota(jnp.int32, (PACK * CHUNK, GROUP), 1) // HEAD
    block_row = lax.broadcasted_iota(jnp.int32, (GROUP, GROUP), 0) // HEAD
    block_col = lax.broadcasted_iota(jnp.int32, (GROUP, GROUP), 1) // HEAD
    return row_head == lane_head, block_row == block_col


def interleave(items, lag):
    waiting = [(j * lag, item) for j, item in enumerate(items)]
    at = 0
    while waiting:
        alive = []
        for begin, item in waiting:
            if at < begin or next(item, waiting) is not waiting:
                alive.append((begin, item))
        waiting = alive
        at += 1


def stack(mask, item):
    return jnp.where(mask, jnp.concatenate([item] * PACK, axis=0), jnp.zeros((), BF))


def sum_heads(item, ones):
    high, low = split(item)
    return mm(high, ones) + mm(low, ones)


def tables(coarse, fine, tile):
    rows = TILE // 8
    co, so = [], []
    outer = coarse[pl.ds(tile * rows, rows)]
    ci, si = fine[0:8, :][None], fine[8:16, :][None]
    co, so = outer[:, 0:1, :], outer[:, 1:2, :]
    flat = lambda item: item.reshape(TILE, LANES)
    cosine = flat(co * ci - so * si)
    sine = so * ci + co * si
    return cosine, flat(sine * fine[16:24, :][None]), flat(sine * fine[24:32, :][None])


def attn_front_kernel(
    info, normed, target, w_q, w_k, w_v, b_q, b_k, b_v, w_proj, scale, mix_high, mix_low, base, inner, upb, w_up,
    attended, dq, fq_s, fk_s, v_s, tk_s, gn_s, gx_s, bias_q, scale_grad, shift, state, total, up_buf, sems,
):
    step = pl.program_id(0)
    strips = up_buf.shape[1] // LANES
    groups = w_q.shape[1] // GROUP
    span = TILE // CHUNK
    stack_mask, block_mask = patterns()
    ones = jnp.where(block_mask, 1.0, 0.0).astype(BF)
    causal = lax.broadcasted_iota(jnp.int32, (CHUNK, PACK * CHUNK), 0) >= (
        lax.broadcasted_iota(jnp.int32, (CHUNK, PACK * CHUNK), 1) % CHUNK
    )
    lower = jnp.where(
        lax.broadcasted_iota(jnp.int32, (CHUNK, CHUNK), 0) >= lax.broadcasted_iota(jnp.int32, (CHUNK, CHUNK), 1),
        1.0,
        0.0,
    ).astype(BF)

    @pl.when(step == 0)
    def _():
        for item in (state, total, bias_q, scale_grad, shift):
            item[...] = jnp.zeros_like(item)

        @pl.loop(0, strips)
        def _(j):
            strip_copy(info[0], w_up, up_buf, sems, 0, j).start()

    x = normed[...]
    cosine, low, high = tables(base, inner, step)
    grad_all = mm(target[...], w_proj[...], NT)
    feats, turned, values, held, before = {}, {}, {}, {}, {}

    def feature(g, which):
        cols = slice(g * GROUP, (g + 1) * GROUP)
        w, b, out = ((w_q, b_q, fq_s), (w_k, b_k, fk_s))[which]
        t = mm(x, w[:, cols]) + b[:, cols]
        yield
        t = turn(t, cosine, low, high)
        turned[which, g] = t
        t_high, t_low = split(t)
        spread = mm(t_high, mix_high[...]) + mm(t_low, mix_high[...]) + mm(t_high, mix_low[...])
        yield
        square = sum_heads(t * t, ones)
        yield
        feats[which, g] = (scale[:, cols] * jnp.exp(spread - square * (0.5 * HEAD ** (-0.5)))).astype(BF)
        out[:, cols] = feats[which, g]
        if which == 1:
            tk_s[:, cols] = t.astype(BF)
            values[g] = (mm(x, w_v[:, cols]) + b_v[:, cols]).astype(BF)
            v_s[:, cols] = values[g]
        yield

    def unit(g, c):
        cols = slice(g * GROUP, (g + 1) * GROUP)
        rows = slice(c * CHUNK, (c + 1) * CHUNK)
        fq, fk, vc = feats[0, g][rows], feats[1, g][rows], values[g][rows]
        stack_k, stack_v = stack(stack_mask, fk), stack(stack_mask, vc)
        kept = state[g]
        held = kept.astype(BF)
        state[g] = kept + jnp.where(block_mask, mm(fk, vc, TN), 0.0)
        keys = mm(lower, fk) + total[g]
        total[g] = keys[CHUNK - 1 : CHUNK, :]
        yield
        weight = jnp.where(causal, mm(fq, stack_k, NT), 0.0).astype(BF)
        wide = fq.astype(F32)
        den = sum_heads(wide * keys, ones)
        yield
        num = mm(weight, stack_v) + mm(fq, held)
        inverse = 1.0 / den
        yield
        mixed = num * inverse
        attended[rows, cols] = mixed.astype(BF)
        gn = (grad_all[rows, cols] * inverse).astype(BF)
        gn_s[rows, cols] = gn
        edge = jnp.where(causal, mm(gn, stack_v, NT), 0.0).astype(BF)
        yield
        grad_den = -sum_heads(gn.astype(F32) * mixed, ones)
        gx_s[rows, cols] = (grad_den * wide).astype(BF)
        yield
        dfq = mm(edge, stack_k) + mm(gn, held, NT) + grad_den * keys
        back = dfq * wide
        back_low = back.astype(BF)
        scale_grad[:, cols] += jnp.sum(back, axis=0, keepdims=True)
        yield
        dt = mm(back_low, mix_high[...], NT)
        dt = dt - mm(back_low, ones) * turned[0, g][rows] * (HEAD ** (-0.5))
        yield
        out = turn(dt, cosine[rows], -low[rows], -high[rows]).astype(BF)
        dq[rows, cols] = out
        bias_q[:, cols] += jnp.sum(out.astype(F32), axis=0, keepdims=True)
        yield

    interleave([feature(g, which) for g in range(groups) for which in range(2)], 0)
    interleave([unit(g, c) for c in range(span) for g in range(groups)], 0)

    @pl.when(step == pl.num_programs(0) - 1)
    def _():
        @pl.loop(0, strips)
        def _(j):
            strip_copy(info[0], w_up, up_buf, sems, 0, j).wait()

        @pl.loop(0, upb.shape[1] // (2 * GROUP))
        def _(j):
            cols = pl.ds(pl.multiple_of(j * 2 * GROUP, GROUP), 2 * GROUP)
            shift[...] += exact_row(upb[:, cols], up_buf[:, cols])


def attn_rear_kernel(
    tiles, info, fq_s, fk_s, v_s, tk_s, gn_s, gx_s, mix_high, mix_low, base, inner, bias_in, scale_in, scale,
    w_qkv, shift_in, dk, dv, sums_out, shift_out, bias_k, bias_v, scale_grad, w_buf, sems, state, total,
):
    step = pl.program_id(0)
    tile = tiles - 1 - step
    groups = dk.shape[1] // GROUP
    span = TILE // CHUNK
    stack_mask, block_mask = patterns()
    ones = jnp.where(block_mask, 1.0, 0.0).astype(BF)
    causal = lax.broadcasted_iota(jnp.int32, (CHUNK, PACK * CHUNK), 1) % CHUNK >= (
        lax.broadcasted_iota(jnp.int32, (CHUNK, PACK * CHUNK), 0)
    )
    upper = jnp.where(
        lax.broadcasted_iota(jnp.int32, (CHUNK, CHUNK), 1) >= lax.broadcasted_iota(jnp.int32, (CHUNK, CHUNK), 0),
        1.0,
        0.0,
    ).astype(BF)

    @pl.when(step == 0)
    def _():
        for item in (state, total, bias_k, bias_v):
            item[...] = jnp.zeros_like(item)
        for p in range(3):
            part_copy(info[0], w_qkv, w_buf, sems, p).start()
        scale_grad[...] = scale_in[...]

    cosine, low, high = tables(base, inner, tile)

    def unit(g, c):
        cols = slice(g * GROUP, (g + 1) * GROUP)
        rows = slice(c * CHUNK, (c + 1) * CHUNK)
        fq, fk, vc, gn = fq_s[rows, cols], fk_s[rows, cols], v_s[rows, cols], gn_s[rows, cols]
        stack_q, stack_g = stack(stack_mask, fq), stack(stack_mask, gn)
        kept = state[g]
        held = kept.astype(BF)
        state[g] = kept + jnp.where(block_mask, mm(fq, gn, TN), 0.0)
        sums = mm(upper, gx_s[rows, cols]) + total[g]
        total[g] = sums[0:1, :]
        yield
        edge = jnp.where(causal, mm(vc, stack_g, NT), 0.0).astype(BF)
        yield
        weight = jnp.where(causal, mm(fk, stack_q, NT), 0.0).astype(BF)
        yield
        dfk = mm(edge, stack_q) + mm(vc, held, NT) + sums
        back = dfk * fk.astype(F32)
        back_low = back.astype(BF)
        scale_grad[:, cols] += jnp.sum(back, axis=0, keepdims=True)
        yield
        dvc = (mm(weight, stack_g) + mm(fk, held)).astype(BF)
        dv[rows, cols] = dvc
        bias_v[:, cols] += jnp.sum(dvc.astype(F32), axis=0, keepdims=True)
        yield
        dt = mm(back_low, mix_high[...], NT)
        dt = dt - mm(back_low, ones) * tk_s[rows, cols].astype(F32) * (HEAD ** (-0.5))
        yield
        out = turn(dt, cosine[rows], -low[rows], -high[rows]).astype(BF)
        dk[rows, cols] = out
        bias_k[:, cols] += jnp.sum(out.astype(F32), axis=0, keepdims=True)
        yield

    interleave([unit(g, c) for c in reversed(range(span)) for g in range(groups)], 1)

    @pl.when(step == tiles - 1)
    def _():
        sums_out[0:1, :] = bias_in[...]
        sums_out[1:2, :] = bias_k[...]
        sums_out[2:3, :] = bias_v[...]
        sums_out[3:4, :] = scale_grad[...] / scale[...]
        shift_out[...] = shift_in[...]
        for p in range(3):
            part_copy(info[0], w_qkv, w_buf, sems, p).wait()

        @pl.loop(0, 3 * groups)
        def _(j):
            row = sums_out[pl.ds(j // groups, 1), pl.ds(pl.multiple_of((j % groups) * GROUP, GROUP), GROUP)]
            shift_out[...] += exact_row(row, w_buf[:, pl.ds(pl.multiple_of(j * GROUP, GROUP), GROUP)])


def turn_tables():
    lane = np.arange(LANES) % HEAD
    freqs = np.where(lane < ROT, 10000.0 ** (-(lane % (ROT // 2)) / (ROT // 2)), 0.0)
    waves = lambda places: np.stack([np.cos(places[:, None] * freqs), np.sin(places[:, None] * freqs)], axis=1)
    fine = np.concatenate(
        [
            waves(np.arange(8)).transpose(1, 0, 2).reshape(16, LANES),
            np.broadcast_to(np.where(lane < ROT // 2, -1.0, 0.0), (8, LANES)),
            np.broadcast_to(np.where((lane >= ROT // 2) & (lane < ROT), 1.0, 0.0), (8, LANES)),
        ]
    )
    return waves(np.arange(LEN // 8) * 8.0).astype(np.float32), fine.astype(np.float32)


def prepare_kernel(*refs):
    *parts, points, basis, vectors, mix_high, mix_low = refs
    at = 0
    for part in parts:
        count = part.shape[0]
        vectors[:, at : at + count] = part[...].astype(F32).reshape(1, count)
        at += count
    table = jnp.dot(basis[...], points[...], precision=lax.Precision.HIGHEST, preferred_element_type=F32)
    wide = jnp.concatenate([table] * PACK, axis=1)
    _, block_mask = patterns()
    tall = jnp.where(block_mask, jnp.concatenate([wide] * PACK, axis=0), 0.0)
    mix_high[...], mix_low[...] = split(tall)


def prepare(parts, qmc_points):
    places = np.arange(HEAD)
    cosines = np.cos(np.pi * (places[:, None] + 0.5) * places[None, :] / HEAD)
    cosines = cosines * np.where(places == 0, math.sqrt(1.0 / HEAD), math.sqrt(2.0 / HEAD))[None, :]
    total = sum(item.shape[0] for item in parts)
    vectors, high, low = pl.pallas_call(
        prepare_kernel,
        out_shape=(
            jax.ShapeDtypeStruct((1, total), F32),
            jax.ShapeDtypeStruct((GROUP, GROUP), BF),
            jax.ShapeDtypeStruct((GROUP, GROUP), BF),
        ),
        compiler_params=params(),
        name="prepare",
    )(*parts, qmc_points, jnp.asarray(cosines * HEAD ** (-0.25), F32))
    return vectors, (high, low)


def stored(tile, info, own):
    return ((tile // own) ^ info[0]) * own + tile % own


def attention_front(info, normed, target, w_qkv, w_proj, vectors, mix, turns, upb, w_up):
    total, dim = normed.shape
    ff = upb.shape[1]
    half = dim // 2
    tiles = total // TILE
    front = lambda i, info: (stored(i, info, tiles // 2), 0)
    plain = lambda i, info: (i, 0)
    block = lambda k: pl.BlockSpec((dim, half), lambda i, info: (0, 2 * k + info[0]), pipeline_mode=pl.Buffered(1))
    groups = half // GROUP
    return pl.pallas_call(
        attn_front_kernel,
        out_shape=(
            *(jax.ShapeDtypeStruct((total, half), BF) for _ in range(8)),
            *(jax.ShapeDtypeStruct((1, half), F32) for _ in range(2)),
            jax.ShapeDtypeStruct((1, dim), F32),
        ),
        grid_spec=pltpu.PrefetchScalarGridSpec(
            num_scalar_prefetch=1,
            grid=(tiles,),
            in_specs=[
                pl.BlockSpec((TILE, dim), front),
                pl.BlockSpec((TILE, dim), front),
                block(0),
                block(1),
                block(2),
                vector_spec(half, 5 * dim, 0),
                vector_spec(half, 6 * dim, 0),
                vector_spec(half, 7 * dim, 0),
                pl.BlockSpec((half, dim), lambda i, info: (info[0], 0), pipeline_mode=pl.Buffered(1)),
                vector_spec(half, 2 * dim, 0),
            ]
            + [whole(item.shape) for item in (*mix, *turns, upb)]
            + [anywhere()],
            out_specs=[pl.BlockSpec((TILE, half), front)] * 2
            + [pl.BlockSpec((TILE, half), plain)] * 6
            + [whole((1, half))] * 2
            + [whole((1, dim))],
            scratch_shapes=[
                pltpu.VMEM((groups, GROUP, GROUP), F32),
                pltpu.VMEM((groups, 1, GROUP), F32),
                pltpu.VMEM((dim, ff), BF),
                pltpu.SemaphoreType.DMA((1, ff // LANES)),
            ],
        ),
        compiler_params=params(),
        cost_estimate=cost(8 * total * dim * half + 64 * total * half * GROUP, 12 * total * dim, 2 * total * half),
        name="attention_front",
    )(info, normed, target, w_qkv, w_qkv, w_qkv, vectors, vectors, vectors, w_proj, vectors, *mix, *turns, upb, w_up)


def attention_rear(info, saved, bias_q, scale_sum, w_qkv, vectors, shift, mix, turns):
    total, half = saved[0].shape
    dim = w_qkv.shape[0]
    tiles = total // TILE
    rear = lambda i, info: (stored(tiles - 1 - i, info, tiles // 2), 0)
    plain = lambda i, info: (tiles - 1 - i, 0)
    groups = half // GROUP
    return pl.pallas_call(
        partial(attn_rear_kernel, tiles),
        out_shape=(
            *(jax.ShapeDtypeStruct((total, half), BF) for _ in range(2)),
            jax.ShapeDtypeStruct((4, half), F32),
            jax.ShapeDtypeStruct((1, dim), F32),
        ),
        grid_spec=pltpu.PrefetchScalarGridSpec(
            num_scalar_prefetch=1,
            grid=(tiles,),
            in_specs=[pl.BlockSpec((TILE, half), plain)] * 6
            + [whole(item.shape) for item in (*mix, *turns, bias_q, scale_sum)]
            + [vector_spec(half, 2 * dim, 0), anywhere(), whole(shift.shape)],
            out_specs=[pl.BlockSpec((TILE, half), rear)] * 2 + [whole((4, half)), whole((1, dim))],
            scratch_shapes=[pltpu.VMEM((1, half), F32) for _ in range(3)]
            + [pltpu.VMEM((dim, 3 * half), BF), pltpu.SemaphoreType.DMA((3,))]
            + [pltpu.VMEM((groups, GROUP, GROUP), F32), pltpu.VMEM((groups, 1, GROUP), F32)],
        ),
        compiler_params=params(),
        cost_estimate=cost(48 * total * half * GROUP, 16 * total * half, 0),
        name="attention_rear",
    )(info, *saved, *mix, *turns, bias_q, scale_sum, vectors, w_qkv, shift)


def out_kernel(own, info, act, attended, w_proj, w_down, *rest):
    step = pl.program_id(0)
    if own:
        res, received, first, second, out, down_buf, sems = rest
    else:
        out, down_buf, sems = rest

    @pl.when(step == 0)
    def _():
        @pl.loop(0, down_buf.shape[0] // LANES)
        def _(j):
            strip_copy(info[0], w_down, down_buf, sems, 1, j).start()

        @pl.loop(0, down_buf.shape[0] // LANES)
        def _(j):
            strip_copy(info[0], w_down, down_buf, sems, 1, j).wait()

    value = mm(act[...], down_buf[...]) + mm(attended[...], w_proj[...])
    if own:
        value = value + received[...].astype(F32) + (first[...] + second[...]) + res[...].astype(F32)
    out[...] = value.astype(BF)


def out_rows(own, info, act, attended, w_proj, w_down, res=None, received=None, vectors=None):
    total, ff = act.shape
    dim = w_proj.shape[1]
    half = attended.shape[1]
    rows = total // 2
    tiles = rows // TILE
    shift = 0 if own else tiles
    shifted = lambda i, info: (i + shift, 0)
    plain = lambda i, info: (i, 0)
    extra, extra_specs = (), []
    if own:
        extra = (res, received, vectors, vectors)
        extra_specs = [pl.BlockSpec((TILE, dim), plain), pl.BlockSpec((TILE, dim), plain)]
        extra_specs += [vector_spec(dim, 3 * dim), vector_spec(dim, 4 * dim)]
    return pl.pallas_call(
        partial(out_kernel, own),
        out_shape=jax.ShapeDtypeStruct((rows, dim), BF),
        grid_spec=pltpu.PrefetchScalarGridSpec(
            num_scalar_prefetch=1,
            grid=(tiles,),
            in_specs=[
                pl.BlockSpec((TILE, ff), shifted),
                pl.BlockSpec((TILE, half), shifted),
                pl.BlockSpec((half, dim), lambda i, info: (info[0], 0), pipeline_mode=pl.Buffered(1)),
                anywhere(),
            ]
            + extra_specs,
            out_specs=pl.BlockSpec((TILE, dim), plain),
            scratch_shapes=[
                pltpu.VMEM((ff, dim), BF),
                pltpu.SemaphoreType.DMA((2, ff // LANES)),
            ],
        ),
        compiler_params=params(),
        cost_estimate=cost(2 * rows * dim * (ff + half), 2 * rows * (ff + half + dim) + 2 * dim * (ff + half)),
        name="out_rows",
    )(info, act, attended, w_proj, w_down, *extra)


def back_kernel(own, info, dq, dk, dv, up_grad, w_qkv, w_up, *rest):
    step = pl.program_id(0)
    if own:
        res, gain, target, received, out, w_buf, up_buf, part_sems, sems = rest
    else:
        out, w_buf, up_buf, part_sems, sems = rest
    grads = (dq, dk, dv)
    half = dq.shape[1]

    @pl.when(step == 0)
    def _():
        for p in range(3):
            part_copy(info[0], w_qkv, w_buf, part_sems, p).start()

        @pl.loop(0, up_buf.shape[1] // LANES)
        def _(j):
            strip_copy(info[0], w_up, up_buf, sems, 0, j).start()

        for p in range(3):
            part_copy(info[0], w_qkv, w_buf, part_sems, p).wait()

        @pl.loop(0, up_buf.shape[1] // LANES)
        def _(j):
            strip_copy(info[0], w_up, up_buf, sems, 0, j).wait()

    value = mm(up_grad[...], up_buf[...], NT)
    for p in range(3):
        value = value + mm(grads[p][...], w_buf[:, p * half : (p + 1) * half], NT)
    if own:
        xhat, rstd = norm_stats(res[...].astype(F32))
        scaled = (value + received[...].astype(F32)) * gain[...]
        middle = jnp.mean(scaled, axis=-1, keepdims=True)
        slope = jnp.mean(scaled * xhat, axis=-1, keepdims=True)
        out[...] = target[...].astype(F32) + rstd * (scaled - middle - xhat * slope)
    else:
        out[...] = value.astype(BF)


def back_rows(own, info, dq, dk, dv, up_grad, w_qkv, w_up, res=None, vectors=None, target=None, received=None):
    total, ff = up_grad.shape
    rows, dim = total // 2, w_qkv.shape[0]
    half = dq.shape[1]
    tiles = rows // TILE
    shift = 0 if own else tiles
    shifted = lambda i, info: (i + shift, 0)
    plain = lambda i, info: (i, 0)
    extra, extra_specs = (), []
    if own:
        extra = (res, vectors, target, received)
        extra_specs = [
            pl.BlockSpec((TILE, dim), plain),
            vector_spec(dim, 0),
            pl.BlockSpec((TILE, dim), plain),
            pl.BlockSpec((TILE, dim), plain),
        ]
    return pl.pallas_call(
        partial(back_kernel, own),
        out_shape=jax.ShapeDtypeStruct((rows, dim), F32 if own else BF),
        grid_spec=pltpu.PrefetchScalarGridSpec(
            num_scalar_prefetch=1,
            grid=(tiles,),
            in_specs=[pl.BlockSpec((TILE, half), shifted)] * 3
            + [pl.BlockSpec((TILE, ff), shifted), anywhere(), anywhere()]
            + extra_specs,
            out_specs=pl.BlockSpec((TILE, dim), plain),
            scratch_shapes=[
                pltpu.VMEM((dim, 3 * half), BF),
                pltpu.VMEM((dim, ff), BF),
                pltpu.SemaphoreType.DMA((3,)),
                pltpu.SemaphoreType.DMA((2, ff // LANES)),
            ],
        ),
        compiler_params=params(),
        cost_estimate=cost(2 * rows * dim * (ff + 3 * half), 2 * rows * (ff + 3 * half + 3 * dim) + 2 * dim * (ff + 3 * half)),
        name="back_rows",
    )(info, dq, dk, dv, up_grad, w_qkv, w_up, *extra)


def bit_orders(ndp):
    bits = [1 << j for j in range(ndp.bit_length() - 1)]
    return tuple(bits), tuple(bits[1::-1] + bits[2:])


def spots(me, ndp):
    apart = jnp.asarray(np.arange(ndp, dtype=np.int32)) ^ me
    rows = []
    for order in bit_orders(ndp):
        spot = jnp.zeros((ndp,), jnp.int32)
        for j, bit in enumerate(order):
            spot = spot + (((apart // bit) % 2) << (len(order) - 1 - j))
        rows.append(spot)
    return jnp.stack(rows)


def add(left, right, kind=BF):
    return (left.astype(F32) + right.astype(F32)).astype(kind)


def cross(value, bit, ndp):
    return lax.ppermute(value, "dp", [(i, i ^ bit) for i in range(ndp)])


class Reduction:
    def __init__(self, first, second, ndp):
        self.ndp = ndp
        self.orders = bit_orders(ndp)
        self.at = 0
        self.pairs = [first, second]
        self.fly()

    def fly(self):
        self.received = [
            cross(send, order[self.at], self.ndp) for (send, keep), order in zip(self.pairs, self.orders)
        ]

    def land(self, token=None):
        if token is not None:
            token, *self.received = lax.optimization_barrier((token, *self.received))
        self.step()
        return token

    def step(self):
        keeps = [keep for send, keep in self.pairs]
        self.at += 1
        steps = len(self.orders[0])
        if self.at == steps:
            parts = [add(k, r, F32)[0] for k, r in zip(keeps, self.received)]
            self.result = jnp.concatenate(parts, axis=0) if len(parts) > 1 else parts[0]
            return
        cut = keeps[0].shape[0] // 2
        pairs = [
            (add(k[cut:], r[cut:]), add(k[:cut], r[:cut])) for k, r in zip(keeps, self.received)
        ]
        if self.at == 2 and len(pairs) == 2:
            pairs = [tuple(jnp.concatenate(items, axis=1) for items in zip(*pairs))]
        self.pairs = pairs

    def hold(self, token):
        if self.at == len(self.orders[0]):
            token, self.result = lax.optimization_barrier((token, self.result))
        return token

    def finish(self):
        if 0 < self.at < len(self.orders[0]):
            self.fly()
        while self.at < len(self.orders[0]):
            self.land()
            if self.at < len(self.orders[0]):
                self.fly()
        return self.result

    def values(self):
        return [item for pair in self.pairs for item in pair]

    def after(self, token):
        if self.at < len(self.orders[0]):
            token, *items = lax.optimization_barrier((token, *self.values()))
            self.pairs = [(items[2 * j], items[2 * j + 1]) for j in range(len(items) // 2)]
            self.fly()
        else:
            token, self.result = lax.optimization_barrier((token, self.result))
        return token


def swap(value):
    return lax.ppermute(value, "stream", [(0, 1), (1, 0)])


def per_device(
    ndp, residual, cotangent, ln_gain, ln_bias, w_qkv, b_qkv, w_proj, b_proj, feature_scale,
    w_up, b_up, w_down, b_down, qmc_points, slot_lengths,
):
    own_rows, dim = residual.shape
    half = dim // 2
    ff = w_up.shape[1]
    side = lax.axis_index("stream")
    me = lax.axis_index("dp")
    info = jnp.stack([side, me, slot_lengths[0]]).astype(jnp.int32)
    table = spots(me, ndp)
    vectors, mix = prepare((ln_gain, ln_bias, feature_scale, b_proj, b_down, b_qkv, b_up), qmc_points)

    other_res = swap(residual)
    other_cot = swap(cotangent)
    *mine, target_sum = mlp_rows(0, info, residual, cotangent, vectors, w_up, w_down)
    normed, target, act, up_grad, upb, _ = mlp_rows(
        1, info, other_res, other_cot, vectors, w_up, w_down, mine
    )

    turns = tuple(jnp.asarray(item) for item in turn_tables())
    parts = mlp_weight_grads(ndp, table, act, target, normed, up_grad)
    mlp_sums = Reduction(parts[:2], parts[2:], ndp)

    attended, dq, *saved, bias_q, scale_sum, shift = attention_front(
        info, normed, target, w_qkv, w_proj, vectors, mix, turns, upb, w_up
    )
    attended = mlp_sums.land(attended)
    info = mlp_sums.after(info)
    dk, dv, sums, shift = attention_rear(info, saved, bias_q, scale_sum, w_qkv, vectors, shift, mix, turns)
    dk = mlp_sums.land(dk)
    table = mlp_sums.after(table)

    mine = lax.broadcasted_iota(jnp.int32, (1, 2, 1), 1) == side
    spread = lambda item: jnp.where(mine, item[:, None, :], 0.0)
    four = spread(sums)
    small = jnp.concatenate(
        [
            shift.reshape(ndp, -1),
            four[:3].reshape(ndp, -1),
            target_sum.reshape(ndp, -1),
            four[3].reshape(ndp, -1),
            spread(upb.reshape(-1, LANES)).reshape(ndp, -1),
        ],
        axis=1,
    )
    count = small.shape[1]
    extra = jnp.pad(small.astype(BF), ((0, 0), (0, 8 * half - count))).reshape(ndp, 8, half)
    parts = attn_weight_grads(ndp, table, normed, target, attended, dq, dk, dv, extra)
    attn_sums = Reduction(parts[:2], parts[2:], ndp)
    mlp_sums.land()
    info = mlp_sums.after(info)

    back_send = back_rows(False, info, dq, dk, dv, up_grad, w_qkv, w_up)
    back_send = attn_sums.land(back_send)
    info = attn_sums.after(info)
    back_received = swap(back_send)
    out_send = out_rows(False, info, act, attended, w_proj, w_down)
    out_send = attn_sums.land(mlp_sums.land(out_send))
    info = attn_sums.after(mlp_sums.after(info))
    out_received = swap(out_send)
    residual_grad = back_rows(
        True, info, dq, dk, dv, up_grad, w_qkv, w_up, residual, vectors, target, back_received
    )
    residual_grad = mlp_sums.hold(attn_sums.land(residual_grad))
    info = attn_sums.after(info)
    block_out = out_rows(True, info, act, attended, w_proj, w_down, residual, out_received, vectors)
    block_out = attn_sums.land(block_out)
    mlp_total, attn_total = mlp_sums.finish(), attn_sums.finish()

    blk = ff // (2 * ndp)
    size = dim // ndp
    small_size = size // 2
    down_rows = mlp_total[:blk]
    per = max(LANES // blk, 1)
    owners = [
        (v * 2 + s, (2 * (v // per) + s) * per + v % per) for v in range(ndp) for s in range(2)
    ]
    if any(a != b for a, b in owners):
        down_rows = lax.ppermute(down_rows, ("dp", "stream"), owners)

    def halves(blocks):
        blocks = blocks.reshape(blocks.shape[0], 2, small_size, blocks.shape[2])
        pick = lambda at: lax.dynamic_index_in_dim(blocks, at, 1, keepdims=False)
        return pick(side), pick(1 - side)

    def order(own, other):
        return jnp.where(side == 0, own, other), jnp.where(side == 0, other, own)

    keep, give = halves(mlp_total[blk:].reshape(2, size, -1))
    first, second = order(keep, swap(give))
    apart = lambda item: jnp.transpose(item, (1, 0, 2)).reshape(small_size, -1, 1, LANES)
    upw_grad = jnp.concatenate([apart(first), apart(second)], axis=2).reshape(small_size, ff)

    keep, give = halves(attn_total[: 3 * size].reshape(3, size, half))
    rest = attn_total[4 * size :]
    received = swap(jnp.concatenate([give.reshape(3 * small_size, half), rest], axis=0))
    first, second = order(keep, received[: 3 * small_size].reshape(3, small_size, half))
    qkvw_grad = jnp.concatenate([item[p] for p in range(3) for item in (first, second)], axis=1)
    proj_rows = jnp.concatenate(
        [attn_total[3 * size + p * small_size : 3 * size + (p + 1) * small_size] for p in range(2)], axis=1
    )
    proj_owners = [(v * 2 + s, ndp * s + v) for v in range(ndp) for s in range(2)]
    projw_grad = lax.ppermute(proj_rows, ("dp", "stream"), proj_owners)

    flat = (rest + received[3 * small_size :]).reshape(-1)
    ends = np.cumsum([0, size, 3 * size, size, size, 2 * blk])
    pieces = [
        lax.dynamic_index_in_dim(flat[a:b].reshape(2, -1), side, 0, keepdims=False)
        for a, b in zip(ends[:-1], ends[1:])
    ]
    shift_grad, qkvb_grad, projb_grad, scale_grad, upb_grad = pieces
    mine_at = (2 * me + side) * small_size
    near = lambda item: lax.dynamic_slice_in_dim(item, mine_at, small_size).astype(F32)
    along = jnp.sum(near(w_qkv) * qkvw_grad, axis=1) + jnp.sum(near(w_up) * upw_grad, axis=1)
    gain_grad = (along - near(ln_bias) * shift_grad) / near(ln_gain)

    return (
        block_out, residual_grad, gain_grad, shift_grad, qkvw_grad, qkvb_grad, projw_grad,
        projb_grad, scale_grad, upw_grad, upb_grad, down_rows, projb_grad,
    )


def solution(mesh):
    rows = P(("dp", "stream"), None)
    items = P(("dp", "stream"))
    return jax.shard_map(
        partial(per_device, mesh.shape["dp"]),
        mesh=mesh,
        in_specs=(rows, rows) + (P(),) * 12 + (P("dp"),),
        out_specs=(rows, rows, items, items, rows, items, rows, items, items, rows, items, rows, items),
        check_vma=False,
    )
```
